256 devices in a mesh: grp: 2 (over x_hi), rows: 64 (over y, z, core), cols: 2 (over x_lo).
Axes of the slice: x: 4 (x_hi: 2, x_lo: 2; x = x_hi * 2 + x_lo), y: 4, z: 8, core: 2. Of those that a mesh axis runs over, the one named last changes fastest.
Arguments:
- band_vectors: float32 [49152, 1024], P('rows'), may hold values from -6 to 6
- coulomb: float32 [49152], P('rows'), may hold values from 0.1 to 10
- pair_weight: float32 [1536], replicated, may hold values from 0.25 to 4
- occ_index: int32 [1536], replicated, may hold values from 0 to 255
- vir_index: int32 [1536], replicated, may hold values from 256 to 1023
- freq_index: int32 [1024], replicated, may hold values from 0 to 15
- freq_table: float32 [16], replicated, may hold values from 0.3 to 3
Outputs:
- self_energy: float32 [1024, 1024], P(('rows', 'cols'), 'grp')
The draws below stay inside these ranges and needn't reach their ends.
Inputs may be any that keep to these rules, and one draw needn't show every extreme that they name: `occ_index`: every pair's occupied band lies below 256. `vir_index`: every pair's empty band lies at 256 or above.
All inputs are finite; a program needn't handle non-finite values.
Results may differ from the reference program's by a relative error of at most 0.0001.
Values sent between devices are 32-bit elements; how exact they have to be, the bound alone decides.
A program may use at most 64 MiB of HBM per device.

```python
import math
import jax
import jax.numpy as jnp
from jax import lax

NB = 49152
NBAND = 1024
NPAIR = 1536
NFREQ = 16
NOCC = 256
WIN = 1024
N_ROWS = 64


def plant(array, stream_key, least, high):
    spot = [jax.random.randint(jax.random.fold_in(stream_key, axis), (), 0, length) for axis, length in enumerate(array.shape)]
    longest = array.shape.index(max(array.shape))
    neighbour = spot[:longest] + [(spot[longest] + 1) % array.shape[longest]] + spot[longest + 1:]
    return array.at[tuple(spot)].set(least).at[tuple(neighbour)].set(high)


def level_of(rng, dims, cuts, least, top_value):
    factor_of = 1.0
    for dim, parts in cuts:
        steps = jax.random.uniform(jax.random.fold_in(jax.random.fold_in(rng, 6), dim), (parts,), jnp.float32, least / len(cuts), top_value / len(cuts))
        factor_of = factor_of * jnp.repeat(jnp.exp(steps), dims[dim] // parts).reshape((-1,) + (1,) * (len(dims) - 1 - dim))
    return factor_of


def normal_values(own_key, dims, spread, limit, shards=(), kind=jnp.bfloat16):
    array = jax.random.normal(own_key, dims, jnp.float32) * spread
    if len(shards) > 0:
        array = level_of(own_key, dims, shards, -0.22, 0.18) * array
    return jnp.clip(array, min=-limit, max=limit).astype(kind)


def setup_inputs(seed: int = 0) -> dict:
    seeds = jax.random.split(jax.random.key(seed), 8)
    return {
        "band_vectors": normal_values(seeds[0], (NB, NBAND), 1.0, 6.0, ((0, 64),), jnp.float32),
        "coulomb": jnp.clip(jnp.exp(math.log(10.0) - 4.6051702 * jax.random.uniform(seeds[1], (NB,), jnp.float32) ** level_of(seeds[1], (NB,), ((0, 64),), -0.2, 0.2)), 0.1, 10.0),
        "pair_weight": jnp.clip(jnp.exp(jax.random.uniform(seeds[2], (NPAIR,), jnp.float32, math.log(0.25), math.log(4.0))), 0.25, 4.0),
        "occ_index": plant(jax.random.randint(seeds[3], (NPAIR,), 0, NOCC), jax.random.fold_in(seeds[3], 1), 0, NOCC - 1).astype(jnp.int32),
        "vir_index": plant(jax.random.randint(seeds[4], (NPAIR,), NOCC, NBAND), jax.random.fold_in(seeds[4], 1), NOCC, NBAND - 1).astype(jnp.int32),
        "freq_index": plant(jax.random.randint(seeds[5], (NBAND,), 0, NFREQ), jax.random.fold_in(seeds[5], 1), 0, NFREQ - 1).astype(jnp.int32),
        "freq_table": jnp.clip(jnp.exp(jax.random.uniform(seeds[6], (NFREQ,), jnp.float32, math.log(0.3), math.log(3.0))), 0.3, 3.0),
    }


def reference(band_vectors, coulomb, pair_weight, occ_index, vir_index, freq_index, freq_table):
    highest = lax.Precision.HIGHEST
    row_block = NB // N_ROWS
    band_weight = freq_table[freq_index]

    def accumulate(totals, offset):
        response, coupling = totals
        block_rows = lax.dynamic_slice_in_dim(band_vectors, offset, row_block, 0)
        coul_rows = lax.dynamic_slice_in_dim(coulomb, offset, row_block, 0)
        pair_cols = block_rows[:, occ_index] * block_rows[:, vir_index] * pair_weight[None, :]
        weighted = pair_cols[:, :WIN] * coul_rows[:, None]
        response = response + lax.dot_general(pair_cols, weighted, (((0,), (0,)), ((), ())), precision=highest, preferred_element_type=jnp.float32)
        band_cols = block_rows * coul_rows[:, None] * band_weight[None, :]
        coupling = coupling + lax.dot_general(band_cols, pair_cols, (((0,), (0,)), ((), ())), precision=highest, preferred_element_type=jnp.float32)
        return ((response, coupling), None)
    offsets = (jnp.arange(N_ROWS) * row_block).astype(jnp.int32)
    initial = (jnp.zeros((NPAIR, WIN), jnp.float32), jnp.zeros((NBAND, NPAIR), jnp.float32))
    (response, coupling), unused = lax.scan(accumulate, initial, offsets)
    response = response * (1.0 / NB)
    coupling = coupling * (1.0 / math.sqrt(NB))
    mixed_rows = jnp.dot(coupling, response, precision=highest, preferred_element_type=jnp.float32)
    self_energy = lax.dot_general(mixed_rows, coupling[:, :WIN], (((1,), (1,)), ((), ())), precision=highest, preferred_element_type=jnp.float32)
    return self_energy * (1.0 / math.sqrt(WIN))
```

```python
import functools
import math

import jax
import jax.numpy as jnp
from jax import lax
from jax.experimental import pallas as pl
from jax.experimental.pallas import tpu as pltpu
from jax.sharding import Mesh
from jax.sharding import PartitionSpec as P

NB = 49152
ROWS = ("rows_0", "rows_1", "rows_2")
ROWS_COLS = ("rows_0", "rows_1", "rows_2", "cols")
MESH = pl.DeviceIdType.MESH
F32 = jnp.float32
BF16 = jnp.bfloat16
KB = 768
NK = KB // 128
HALF = 768


def split(x):
    hi = x.astype(BF16)
    return hi, (x - hi.astype(F32)).astype(BF16)


def pair_kernel(occ, vir, weight, v_ref, c_ref, pt_hi, pt_lo, w_hi, w_lo, vt, pt, wn):
    plane = lax.axis_index("grp") * 2 + lax.axis_index("cols")
    for k in range(NK):
        for nb in range(8):
            block = v_ref[k * 128 : (k + 1) * 128, nb * 128 : (nb + 1) * 128]
            vt[pl.ds(nb * 1024 + k, 128, stride=8), :] = block.T

    for half in range(2):
        for b in range(6):

            def one(i, carry, half=half, b=b):
                for u in range(8):
                    at = i * 8 + u
                    p = 256 * b + 128 * half + at
                    o = pl.multiple_of(occ[p] * 8, 8)
                    v = pl.multiple_of(vir[p] * 8, 8)
                    to = pl.multiple_of((768 * half + 128 * b + at) * 8, 8)
                    pt[pl.ds(to, 8), :] = vt[pl.ds(o, 8), :] * vt[pl.ds(v, 8), :] * weight[p]
                return carry

            lax.fori_loop(0, 16, one, 0)

    def rows(b, carry):
        base = pl.multiple_of(b * 128, 128)
        for k in range(NK):
            x = pt[pl.ds(base * 8 + k, 128, stride=8), :]
            hi, lo = split(x)
            pt_hi[pl.ds(base, 128), k * 128 : (k + 1) * 128] = hi
            pt_lo[pl.ds(base, 128), k * 128 : (k + 1) * 128] = lo
        return carry

    lax.fori_loop(0, 12, rows, 0)
    for k in range(NK):
        cols = slice(k * 128, (k + 1) * 128)
        c = c_ref[0:1, cols]
        for half in range(2):
            x = pt[pl.ds((768 * half + 128 * plane) * 8 + k, 128, stride=8), :] * c
            hi, lo = split(x)
            w_hi[half * 128 : (half + 1) * 128, cols] = hi
            w_lo[half * 128 : (half + 1) * 128, cols] = lo
        for g in range(32):
            wn[g * 8 : (g + 1) * 8, :] = vt[pl.ds((32 * g + 8 * plane) * 8 + k, 8, stride=8), :] * c
        hi, lo = split(wn[...])
        w_hi[256:512, cols] = hi
        w_lo[256:512, cols] = lo


def nt(a, b):
    return lax.dot_general(a, b, (((1,), (1,)), ((), ())), preferred_element_type=F32)


def nn(a, b):
    return lax.dot_general(a, b, (((1,), (0,)), ((), ())), preferred_element_type=F32)


def main_kernel(
    pt_hi, pt_lo, w_hi, w_lo, fidx, ftab, out_ref,
    r_oth, x_oth, r_in, x_in, r_acc, x_acc,
    zin_m, zin_p, yin_m, yin_p, ry_in, xz_in,
    x32, rfull, yfull, mbuf, m_in, sbuf, s_in,
    send, recv,
):
    y = lax.axis_index("rows_0")
    z = lax.axis_index("rows_1")
    c = lax.axis_index("rows_2")
    g = lax.axis_index("grp")
    cl = lax.axis_index("cols")
    plane = 2 * g + cl
    started = []
    count = [0]

    def copy(src, dst, to):
        i = count[0]
        count[0] += 1
        d = pltpu.make_async_remote_copy(
            src_ref=src, dst_ref=dst, send_sem=send.at[i], recv_sem=recv.at[i],
            device_id=to, device_id_type=MESH,
        )
        d.start()
        started.append(d)
        return d

    def zto(k):
        return {"rows_1": lax.rem(z + k + 8, 8)}

    def yto(k):
        return {"rows_0": lax.rem(y + k + 4, 4)}

    def xto(rel):
        rg, rc, rl = rel
        return {
            "grp": lax.rem(g + rg, 2),
            "rows_2": lax.rem(c + rc, 2),
            "cols": lax.rem(cl + rl, 2),
        }

    rels = [(a, b, d) for a in range(2) for b in range(2) for d in range(2)][1:]

    barrier = pltpu.get_barrier_semaphore()
    for k in range(1, 8):
        pl.semaphore_signal(barrier, inc=1, device_id=zto(k), device_id_type=MESH)
    for k in range(1, 4):
        pl.semaphore_signal(barrier, inc=1, device_id=yto(k), device_id_type=MESH)
    for rel in rels:
        pl.semaphore_signal(barrier, inc=1, device_id=xto(rel), device_id_type=MESH)

    def products(half, r_out, x_out):
        base = pl.multiple_of(half * HALF, HALF)
        ph = pt_hi[pl.ds(base, HALF), :]
        pw = pt_lo[pl.ds(base, HALF), :]
        qh, ql = w_hi[0:256, :], w_lo[0:256, :]
        r_out[...] = nt(ph, qh) + nt(ph, ql) + nt(pw, qh)
        for b in range(3):
            at = pl.multiple_of(half * HALF + b * 256, 256)
            bh = pt_hi[pl.ds(at, 256), :]
            bl = pt_lo[pl.ds(at, 256), :]
            nh, nl = w_hi[256:512, :], w_lo[256:512, :]
            x_out[:, b * 256 : (b + 1) * 256] = nt(nh, bh) + nt(nl, bh) + nt(nh, bl)

    products(1 - c, r_oth, x_oth)
    pl.semaphore_wait(barrier, 17)
    core = {"rows_2": 1 - c}
    dr = copy(r_oth, r_in, core)
    dx = copy(x_oth, x_in, core)
    products(c, r_acc, x_acc)
    dr.wait_recv()
    r_acc[...] += r_in[...]

    def zrows(k, start=0, size=96):
        return pl.ds(pl.multiple_of(lax.rem(z + k + 8, 8) * 96 + start, 8), size)

    def yrows(k, start=0, size=64):
        return pl.ds(pl.multiple_of(lax.rem(y + k + 4, 4) * 64 + start, 8), size)

    zm = copy(r_acc.at[zrows(4, 0, 48)], zin_m.at[0, 0:48], zto(-1))
    zp = copy(r_acc.at[zrows(4, 48, 48)], zin_p.at[0, 48:96], zto(1))
    dx.wait_recv()
    x_acc[...] += x_in[...]
    ym = copy(x_acc.at[yrows(2, 0, 32)], yin_m.at[0, 0:32], yto(-1))
    yp = copy(x_acc.at[yrows(2, 32, 32)], yin_p.at[0, 32:64], yto(1))

    def zstep(s, zm, zp):
        zm.wait_recv()
        if s == 1:
            zin_m[0, 0:48] += r_acc[zrows(-3, 0, 48)]
            zin_m[0, 48:96] = r_acc[zrows(-3, 48, 48)]
        else:
            zin_m[s - 1] += r_acc[zrows(s - 4)]
        zm = copy(zin_m.at[s - 1], zin_m.at[s], zto(-1))
        zp.wait_recv()
        if s == 1:
            zin_p[0, 48:96] += r_acc[zrows(3, 48, 48)]
            zin_p[0, 0:48] = r_acc[zrows(3, 0, 48)]
        else:
            zin_p[s - 1] += r_acc[zrows(4 - s)]
        zp = copy(zin_p.at[s - 1], zin_p.at[s], zto(1))
        return zm, zp

    zm, zp = zstep(1, zm, zp)
    ym.wait_recv()
    yin_m[0, 0:32] += x_acc[yrows(-1, 0, 32)]
    yin_m[0, 32:64] = x_acc[yrows(-1, 32, 32)]
    ym = copy(yin_m.at[0], yin_m.at[1], yto(-1))
    yp.wait_recv()
    yin_p[0, 32:64] += x_acc[yrows(1, 32, 32)]
    yin_p[0, 0:32] = x_acc[yrows(1, 0, 32)]
    yp = copy(yin_p.at[0], yin_p.at[1], yto(1))
    zm, zp = zstep(2, zm, zp)

    ym.wait_recv()
    yp.wait_recv()
    yin_m[1] += x_acc[yrows(0)] + yin_p[1]
    xz = []
    for k in (4, 3, 5, 2, 6, 1, 7):
        rows = pl.ds(pl.multiple_of(lax.rem(z + k, 8) * 8, 8), 8)
        xz.append(copy(yin_m.at[1, rows], xz_in.at[k], zto(k)))
    zm, zp = zstep(3, zm, zp)
    zm.wait_recv()
    zp.wait_recv()
    zin_m[3] += r_acc[zrows(0)] + zin_p[3]
    ry = []
    for k in (2, 1, 3):
        rows = pl.ds(pl.multiple_of(lax.rem(y + k, 4) * 24, 8), 24)
        ry.append(copy(zin_m.at[3, rows], ry_in.at[k], yto(k)))

    for d in xz:
        d.wait_recv()
    tile = yin_m[1, pl.ds(pl.multiple_of(z * 8, 8), 8)]
    for k in range(1, 8):
        tile = tile + xz_in[k]
    chip = y * 8 + z
    row = lax.broadcasted_iota(jnp.int32, (8, HALF), 0)
    factor = jnp.zeros((8, HALF), F32)
    for i in range(8):
        factor = jnp.where(row == i, ftab[fidx[32 * chip + 8 * plane + i]], factor)
    x32[plane] = tile * factor * (1.0 / math.sqrt(NB))
    xs = [copy(x32.at[plane], x32.at[plane], xto(rel)) for rel in ((1, 0, 0), (0, 0, 1), (1, 0, 1))]

    for d in ry:
        d.wait_recv()
    tile = zin_m[3, pl.ds(pl.multiple_of(y * 24, 8), 24)]
    for k in range(1, 4):
        tile = tile + ry_in[k]
    mine = pl.ds(pl.multiple_of((z * 4 + y) * 24, 8), 24)
    rfull[mine] = tile * (1.0 / NB)
    ry = [copy(rfull.at[mine], rfull.at[mine], yto(k)) for k in (2, 1, 3)]

    for d in xs:
        d.wait_recv()
    myrows = pl.multiple_of(chip * 32, 32)
    lanes = pl.ds(pl.multiple_of(plane * 128, 128), 128)
    for j in range(4):
        yfull[pl.ds(myrows + 8 * j, 8)] = x32[j, :, lanes]
    ymine = pl.ds(myrows, 32)
    yz = [copy(yfull.at[ymine], yfull.at[ymine], zto(k)) for k in (4, 3, 5, 2, 6, 1, 7)]

    for d in ry:
        d.wait_recv()

    def zfull(k, start=0, size=96):
        return rfull.at[zrows(k, start, size)]

    zm = copy(zfull(0), zfull(0), zto(-1))
    zp = copy(zfull(0), zfull(0), zto(1))
    for d in yz:
        d.wait_recv()

    def ychunk(k, start=0, size=256):
        return yfull.at[pl.ds(pl.multiple_of(lax.rem(y + k + 4, 4) * 256 + start, 8), size)]

    ym = copy(ychunk(0), ychunk(0), yto(-1))
    yp = copy(ychunk(0), ychunk(0), yto(1))
    for s in range(1, 3):
        zm.wait_recv()
        zm = copy(zfull(s), zfull(s), zto(-1))
        zp.wait_recv()
        zp = copy(zfull(-s), zfull(-s), zto(1))
        if s == 1:
            ym.wait_recv()
            ym = copy(ychunk(1, 0, 128), ychunk(1, 0, 128), yto(-1))
            yp.wait_recv()
            yp = copy(ychunk(-1, 128, 128), ychunk(-1, 128, 128), yto(1))
    zm.wait_recv()
    zm = copy(zfull(3, 0, 48), zfull(3, 0, 48), zto(-1))
    zp.wait_recv()
    zp = copy(zfull(-3, 48, 48), zfull(-3, 48, 48), zto(1))
    ym.wait_recv()
    yp.wait_recv()
    zm.wait_recv()
    zp.wait_recv()

    xh, xl = split(x32[...].reshape(32, HALF))
    rh, rl = split(rfull[...])
    m = nn(xh, rh) + nn(xl, rh) + nn(xh, rl)
    mbuf[0] = m[:, 0:128]
    mbuf[1] = m[:, 128:256]
    dm = copy(mbuf.at[1 - c], m_in, core)
    yh, yl = split(yfull[...])
    dm.wait_recv()
    mh, ml = split(mbuf[c] + m_in[...])
    s = nt(mh, yh) + nt(ml, yh) + nt(mh, yl)
    for tg in range(2):
        for tc in range(2):
            for tl in range(2):
                at = 16 * tc + 8 * tl
                sbuf[tg * 4 + tc * 2 + tl] = s[at : at + 8, tg * 512 : (tg + 1) * 512]
    ds = []
    for i, rel in enumerate(rels):
        to = xto(rel)
        t = to["grp"] * 4 + to["rows_2"] * 2 + to["cols"]
        ds.append(copy(sbuf.at[t], s_in.at[i], to))
    total = sbuf[g * 4 + c * 2 + cl]
    for i, d in enumerate(ds):
        d.wait_recv()
        total = total + s_in[i]
    out_ref[...] = total * (1.0 / math.sqrt(1024))
    for d in started:
        d.wait_send()


def per_device(band_vectors, coulomb, pair_weight, occ_index, vir_index, freq_index, freq_table):
    smem = pl.BlockSpec(memory_space=pltpu.SMEM)
    vmem = pl.BlockSpec(memory_space=pltpu.VMEM)
    pt_hi, pt_lo, w_hi, w_lo = pl.pallas_call(
        pair_kernel,
        out_shape=(
            jax.ShapeDtypeStruct((1536, KB), BF16),
            jax.ShapeDtypeStruct((1536, KB), BF16),
            jax.ShapeDtypeStruct((512, KB), BF16),
            jax.ShapeDtypeStruct((512, KB), BF16),
        ),
        in_specs=[smem, smem, smem, vmem, vmem],
        out_specs=(vmem, vmem, vmem, vmem),
        scratch_shapes=[
            pltpu.VMEM((8192, 128), F32),
            pltpu.VMEM((1536 * 8, 128), F32),
            pltpu.VMEM((256, 128), F32),
        ],
        name="pairs",
    )(occ_index, vir_index, pair_weight, band_vectors, coulomb.reshape(1, KB))
    return pl.pallas_call(
        main_kernel,
        out_shape=jax.ShapeDtypeStruct((8, 512), F32),
        in_specs=[vmem, vmem, vmem, vmem, smem, smem],
        out_specs=vmem,
        scratch_shapes=[
            pltpu.VMEM((HALF, 256), F32),
            pltpu.VMEM((256, HALF), F32),
            pltpu.VMEM((HALF, 256), F32),
            pltpu.VMEM((256, HALF), F32),
            pltpu.VMEM((HALF, 256), F32),
            pltpu.VMEM((256, HALF), F32),
            pltpu.VMEM((4, 96, 256), F32),
            pltpu.VMEM((4, 96, 256), F32),
            pltpu.VMEM((2, 64, HALF), F32),
            pltpu.VMEM((2, 64, HALF), F32),
            pltpu.VMEM((4, 24, 256), F32),
            pltpu.VMEM((8, 8, HALF), F32),
            pltpu.VMEM((4, 8, HALF), F32),
            pltpu.VMEM((HALF, 256), F32),
            pltpu.VMEM((1024, 128), F32),
            pltpu.VMEM((2, 32, 128), F32),
            pltpu.VMEM((32, 128), F32),
            pltpu.VMEM((8, 8, 512), F32),
            pltpu.VMEM((7, 8, 512), F32),
            pltpu.SemaphoreType.DMA((64,)),
            pltpu.SemaphoreType.DMA((64,)),
        ],
        compiler_params=pltpu.CompilerParams(collective_id=0, has_side_effects=True),
        name="window",
    )(pt_hi, pt_lo, w_hi, w_lo, freq_index, freq_table)


def solution(mesh):
    torus = Mesh(
        mesh.devices.reshape(mesh.shape["grp"], 4, 8, 2, mesh.shape["cols"]),
        ("grp", "rows_0", "rows_1", "rows_2", "cols"),
    )
    placed = (P(ROWS, None), P(ROWS), P(), P(), P(), P(), P())
    return jax.shard_map(
        per_device, mesh=torus, in_specs=placed, out_specs=P(ROWS_COLS, "grp"), check_vma=False
    )
```

```python
import math

import jax
import jax.numpy as jnp
from jax import lax
from jax.experimental import pallas as pl
from jax.experimental.pallas import tpu as pltpu
from jax.sharding import Mesh
from jax.sharding import PartitionSpec as P

NB = 49152
ROWS = ("rows_0", "rows_1", "rows_2")
ROWS_COLS = ("rows_0", "rows_1", "rows_2", "cols")
MESH = pl.DeviceIdType.MESH
F32 = jnp.float32
BF16 = jnp.bfloat16
KB = 768
NK = KB // 128
HALF = 768
RELS = [(a, b, d) for a in range(2) for b in range(2) for d in range(2)][1:]
LONG = [(d, h, l) for l in range(2) for d, h in ((0, 0), (1, 1))]
SHORT = [(d, h, l) for l in range(2) for d, h in ((0, 1), (1, 0))]


def split(x):
    hi = x.astype(BF16)
    return hi, (x - hi.astype(F32)).astype(BF16)


def nt(a, b):
    return lax.dot_general(a, b, (((1,), (1,)), ((), ())), preferred_element_type=F32)


def nn(a, b):
    return lax.dot_general(a, b, (((1,), (0,)), ((), ())), preferred_element_type=F32)


def nt3(ah, al, bh, bl):
    return nt(ah, bh) + nt(ah, bl) + nt(al, bh)


def nn3(ah, al, bh, bl):
    return nn(ah, bh) + nn(ah, bl) + nn(al, bh)


def mod(a, n):
    return lax.rem(a + n, n)


def window_kernel(
    occ, vir, fidx, ftab, weight, coulomb, v_hbm, out_ref,
    v_ref, vt, pt, ph, pw, qh, ql, nh, nl,
    r_all, x_all, r_in, x_in,
    zin, yin, rfin, xfin, ry_in, xz_in,
    x32, rfull, yfull, mbuf, m_in, sbuf, s_in,
    load, send, recv,
):
    y = lax.axis_index("rows_0")
    z = lax.axis_index("rows_1")
    c = lax.axis_index("rows_2")
    g = lax.axis_index("grp")
    cl = lax.axis_index("cols")
    plane = 2 * g + cl
    started = []

    def copy(src, dst, to):
        i = len(started)
        d = pltpu.make_async_remote_copy(
            src_ref=src, dst_ref=dst, send_sem=send.at[i], recv_sem=recv.at[i],
            device_id=to, device_id_type=MESH,
        )
        d.start()
        started.append(d)
        return d

    def zto(k):
        return {"rows_1": mod(z + k, 8)}

    def yto(k):
        return {"rows_0": mod(y + k, 4)}

    def xto(rel):
        rg, rc, rl = rel
        return {"grp": mod(g + rg, 2), "rows_2": mod(c + rc, 2), "cols": mod(cl + rl, 2)}

    loads = []
    for k in range(NK):
        rows = pl.ds(k * 128, 128)
        loads.append(pltpu.make_async_copy(v_hbm.at[rows], v_ref.at[rows], load.at[k]))
        loads[k].start()

    barrier = pltpu.get_barrier_semaphore()
    for k in range(1, 8):
        pl.semaphore_signal(barrier, inc=1, device_id=zto(k), device_id_type=MESH)
    for k in range(1, 4):
        pl.semaphore_signal(barrier, inc=1, device_id=yto(k), device_id_type=MESH)
    for rel in RELS:
        pl.semaphore_signal(barrier, inc=1, device_id=xto(rel), device_id_type=MESH)

    for k in range(NK):
        loads[k].wait()
        for nb in range(8):
            block = v_ref[k * 128 : (k + 1) * 128, nb * 128 : (nb + 1) * 128]
            vt[nb * 128 : (nb + 1) * 128, k, :] = block.T

    def gather(base, to):
        def some(i, carry):
            for u in range(16):
                at = i * 16 + u
                pt[to + at] = vt[occ[base + at]] * vt[vir[base + at]]
            return carry

        lax.fori_loop(0, 8, some, 0)

    def weights(base):
        row = weight[pl.ds(pl.multiple_of(base, 128), 128)].reshape(1, 128)
        return jnp.broadcast_to(row, (128, 128)).T

    def cvec(k):
        return coulomb[k * 128 : (k + 1) * 128].reshape(1, 128)

    for s in range(2):
        base = 256 * plane + 128 * s
        gather(base, 128 * s)
        w = weights(base)
        for k in range(NK):
            x = pt[s * 128 : (s + 1) * 128, k, :] * w * cvec(k)
            hi, lo = split(x)
            qh[s * 128 : (s + 1) * 128, k * 128 : (k + 1) * 128] = hi
            ql[s * 128 : (s + 1) * 128, k * 128 : (k + 1) * 128] = lo
    for k in range(NK):
        for m in range(16):
            two = [
                vt[pl.ds(32 * (2 * m + e) + 8 * plane, 8), k, :] for e in range(2)
            ]
            hi, lo = split(jnp.concatenate(two, axis=0) * cvec(k))
            nh[m * 16 : (m + 1) * 16, k * 128 : (k + 1) * 128] = hi
            nl[m * 16 : (m + 1) * 16, k * 128 : (k + 1) * 128] = lo

    def block(t, carry, slot, half):
        for s in range(2):
            base = 512 * t + 256 * s + 128 * half
            gather(base, 128 * s)
            w = weights(base)
            for k in range(NK):
                hi, lo = split(pt[s * 128 : (s + 1) * 128, k, :] * w)
                ph[s * 128 : (s + 1) * 128, k * 128 : (k + 1) * 128] = hi
                pw[s * 128 : (s + 1) * 128, k * 128 : (k + 1) * 128] = lo
        r = nt3(ph[...], pw[...], qh[...], ql[...])
        at = pl.multiple_of(t * 256, 256)
        r_all[slot, 0, pl.ds(at, 256), :] = r[:, 0:128]
        r_all[slot, 1, pl.ds(at, 256), :] = r[:, 128:256]
        x_all[slot, t] = nt3(nh[...], nl[...], ph[...], pw[...])
        return carry

    lax.fori_loop(0, 3, lambda t, a: block(t, a, 0, 1 - c), 0)
    pl.semaphore_wait(barrier, 17)
    core = {"rows_2": 1 - c}
    dr = copy(r_all.at[0], r_in, core)
    dx = copy(x_all.at[0], x_in, core)
    lax.fori_loop(0, 3, lambda t, a: block(t, a, 1, c), 0)

    def zrows(k, start, size):
        return pl.ds(pl.multiple_of(mod(z + k, 8) * 96 + start, 8), size)

    def yrows(k, start, size):
        return pl.ds(pl.multiple_of(mod(y + k, 4) * 64 + start, 8), size)

    sign = (-1, 1)

    def zterm(flow, s):
        d, h, l = flow
        return r_all.at[1, l, zrows(sign[d] * (5 - s), 48 * h, 48)]

    def zhop(flow, s, src):
        d, h, l = flow
        return copy(src, zin.at[d, h, l, s - 1], zto(sign[d]))

    dr.wait_recv()
    r_all[1] += r_in[...]
    zf = {}
    for f in LONG:
        zf[f] = zhop(f, 1, zterm(f, 1))
    for f in SHORT:
        zf[f] = zhop(f, 2, zterm(f, 2))

    def zpass(f, s):
        d, h, l = f
        zf[f].wait_recv()
        zin[d, h, l, s - 1] += zterm(f, s + 1)[...]
        zf[f] = zhop(f, s + 1, zin.at[d, h, l, s - 1])

    def yterm(k, h, q):
        return x_all.at[1, q, yrows(k, 32 * h, 32)]

    dx.wait_recv()
    x_all[1] += x_in[...]
    yl = {}
    ys = {}
    for q in range(3):
        for d in range(2):
            yl[d, q] = copy(yterm(2, d, q), yin.at[d, q, 0], yto(sign[d]))
    for q in range(3):
        for d in range(2):
            ys[d, q] = copy(yterm(sign[d], 1 - d, q), yin.at[d, q, 1], yto(sign[d]))

    for f in LONG:
        zpass(f, 1)
    for q in range(3):
        for d in range(2):
            yl[d, q].wait_recv()
            yin[d, q, 0] += yterm(sign[d], d, q)[...]
            yl[d, q] = copy(yin.at[d, q, 0], yin.at[d, q, 2], yto(sign[d]))
    for f in SHORT:
        zpass(f, 2)
    for f in LONG:
        zpass(f, 2)
    xz = []

    def yfinish(q):
        for d in range(2):
            ys[d, q].wait_recv()
            yl[d, q].wait_recv()
        for h in range(2):
            xfin[q, 32 * h : 32 * h + 32] = (
                yterm(0, h, q)[...] + yin[h, q, 2] + yin[1 - h, q, 1]
            )
        for k in (4, 3, 5, 2, 6, 1, 7):
            rows = pl.ds(pl.multiple_of(mod(z + k, 8) * 8, 8), 8)
            xz.append(copy(xfin.at[q, rows], xz_in.at[k, q], zto(k)))

    for f in SHORT:
        zpass(f, 3)
    yfinish(0)
    for f in LONG:
        zpass(f, 3)
    yfinish(1)
    yfinish(2)
    for f in SHORT:
        zf[f].wait_recv()
    for f in LONG:
        zf[f].wait_recv()
    for h in range(2):
        for l in range(2):
            rfin[l, 48 * h : 48 * h + 48] = (
                r_all[1, l, zrows(0, 48 * h, 48)] + zin[0, h, l, 3] + zin[1, h, l, 3]
            )
    ry = []
    for k in (2, 1, 3):
        rows = pl.ds(pl.multiple_of(mod(y + k, 4) * 24, 8), 24)
        ry.append(copy(rfin.at[:, rows], ry_in.at[k], yto(k)))

    for d in xz:
        d.wait_recv()
    tile = xfin[:, pl.ds(pl.multiple_of(z * 8, 8), 8)]
    for k in range(1, 8):
        tile = tile + xz_in[k]
    chip = y * 8 + z
    row = lax.broadcasted_iota(jnp.int32, (3, 8, 256), 1)
    factor = jnp.zeros((3, 8, 256), F32)
    for i in range(8):
        factor = jnp.where(row == i, ftab[fidx[32 * chip + 8 * plane + i]], factor)
    mine = pl.ds(pl.multiple_of(plane * 8, 8), 8)
    x32[:, mine] = tile * factor * (1.0 / math.sqrt(NB))
    xs = [copy(x32.at[:, mine], x32.at[:, mine], xto(rel)) for rel in ((1, 0, 1), (1, 0, 0), (0, 0, 1))]

    for d in ry:
        d.wait_recv()
    tile = rfin[:, pl.ds(pl.multiple_of(y * 24, 8), 24)]
    for k in range(1, 4):
        tile = tile + ry_in[k]

    def rtile(kz, ky):
        at = (mod(z + kz, 8) * 4 + mod(y + ky, 4)) * 24
        return rfull.at[:, pl.ds(pl.multiple_of(at, 8), 24)]

    rtile(0, 0)[...] = tile * (1.0 / NB)
    ya = {k: copy(rtile(0, 0), rtile(0, 0), yto(k)) for k in (2, 1, 3)}
    za = {}

    def far(d, k):
        return 4 if (k < 2) == (d == 0) else 3

    def zsend(d, k, s):
        src = rtile(-sign[d] * (s - 1), k)
        za[d, k] = copy(src, src, zto(sign[d]))

    for d in range(2):
        zsend(d, 0, 1)

    for d in xs:
        d.wait_recv()
    myrows = pl.multiple_of(chip * 32, 32)
    lanes = pl.ds(pl.multiple_of(lax.rem(plane, 2) * 128, 128), 128)
    yfull[pl.ds(myrows, 32)] = x32[plane // 2, :, lanes]
    ymine = yfull.at[pl.ds(myrows, 32)]
    yz = {k: copy(ymine, ymine, zto(k)) for k in (4, 3, 5, 2, 6, 1, 7)}

    for k in (1, 3, 2):
        ya[k].wait_recv()
        for d in range(2):
            zsend(d, 4 - k, 1)

    yrot = {}

    def ytile(ky, kz):
        at = (mod(y + ky, 4) * 8 + mod(z + kz, 8)) * 32
        return yfull.at[pl.ds(pl.multiple_of(at, 32), 32)]

    def ysend(kz):
        for d in range(2):
            yrot[d, kz] = copy(ytile(0, kz), ytile(0, kz), yto(sign[d]))

    def zforward(s):
        for k in (0, 3, 1, 2):
            for d in range(2):
                if far(d, k) > s:
                    za[d, k].wait_recv()
                    zsend(d, k, s + 1)
                elif far(d, k) == s:
                    za[d, k].wait_recv()

    zforward(1)
    ysend(0)
    for k in (1, 7, 2, 6):
        yz[k].wait_recv()
        ysend(8 - k)
    zforward(2)
    for k in (3, 5, 4):
        yz[k].wait_recv()
        ysend(8 - k)
    last = []
    for kz in (0, 7, 1, 6, 2):
        for d in range(2):
            yrot[d, kz].wait_recv()
            if kz % 2 == d:
                src = ytile(-sign[d], kz)
                last.append(copy(src, src, yto(sign[d])))
    zforward(3)
    for kz in (5, 3, 4):
        for d in range(2):
            yrot[d, kz].wait_recv()
            if kz % 2 == d:
                src = ytile(-sign[d], kz)
                last.append(copy(src, src, yto(sign[d])))
    zforward(4)

    m = jnp.zeros((32, 256), F32)
    for q in range(3):
        xh, xl = split(x32[q])
        rows = slice(256 * q, 256 * q + 256)
        rh, rl = split(jnp.concatenate([rfull[0, rows], rfull[1, rows]], axis=1))
        m = m + nn3(xh, xl, rh, rl)
    mbuf[0] = m[:, 0:128]
    mbuf[1] = m[:, 128:256]
    dm = copy(mbuf.at[1 - c], m_in, core)
    for d in last:
        d.wait_recv()
    yh, yw = split(yfull[...])
    dm.wait_recv()
    mh, ml = split(mbuf[c] + m_in[...])
    s = nt3(mh, ml, yh, yw)
    for tg in range(2):
        for tc in range(2):
            for tl in range(2):
                at = 16 * tc + 8 * tl
                sbuf[tg * 4 + tc * 2 + tl] = s[at : at + 8, tg * 512 : (tg + 1) * 512]
    ds = []
    for i, rel in enumerate(RELS):
        to = xto(rel)
        t = to["grp"] * 4 + to["rows_2"] * 2 + to["cols"]
        ds.append(copy(sbuf.at[t], s_in.at[i], to))
    total = sbuf[g * 4 + c * 2 + cl]
    for i, d in enumerate(ds):
        d.wait_recv()
        total = total + s_in[i]
    out_ref[...] = total * (1.0 / math.sqrt(1024))
    for d in started:
        d.wait_send()


def per_device(band_vectors, coulomb, pair_weight, occ_index, vir_index, freq_index, freq_table):
    smem = pl.BlockSpec(memory_space=pltpu.SMEM)
    vmem = pl.BlockSpec(memory_space=pltpu.VMEM)
    return pl.pallas_call(
        window_kernel,
        out_shape=jax.ShapeDtypeStruct((8, 512), F32),
        in_specs=[smem, smem, smem, smem, vmem, vmem, pl.BlockSpec(memory_space=pl.ANY)],
        out_specs=vmem,
        scratch_shapes=[
            pltpu.VMEM((KB, 1024), F32),
            pltpu.VMEM((1024, 8, 128), F32),
            pltpu.VMEM((256, 8, 128), F32),
            pltpu.VMEM((256, KB), BF16),
            pltpu.VMEM((256, KB), BF16),
            pltpu.VMEM((256, KB), BF16),
            pltpu.VMEM((256, KB), BF16),
            pltpu.VMEM((256, KB), BF16),
            pltpu.VMEM((256, KB), BF16),
            pltpu.VMEM((2, 2, HALF, 128), F32),
            pltpu.VMEM((2, 3, 256, 256), F32),
            pltpu.VMEM((2, HALF, 128), F32),
            pltpu.VMEM((3, 256, 256), F32),
            pltpu.VMEM((2, 2, 2, 4, 48, 128), F32),
            pltpu.VMEM((2, 3, 3, 32, 256), F32),
            pltpu.VMEM((2, 96, 128), F32),
            pltpu.VMEM((3, 64, 256), F32),
            pltpu.VMEM((4, 2, 24, 128), F32),
            pltpu.VMEM((8, 3, 8, 256), F32),
            pltpu.VMEM((3, 32, 256), F32),
            pltpu.VMEM((2, HALF, 128), F32),
            pltpu.VMEM((1024, 128), F32),
            pltpu.VMEM((2, 32, 128), F32),
            pltpu.VMEM((32, 128), F32),
            pltpu.VMEM((8, 8, 512), F32),
            pltpu.VMEM((7, 8, 512), F32),
            pltpu.SemaphoreType.DMA((NK,)),
            pltpu.SemaphoreType.DMA((160,)),
            pltpu.SemaphoreType.DMA((160,)),
        ],
        compiler_params=pltpu.CompilerParams(collective_id=0, has_side_effects=True),
        name="window",
    )(occ_index, vir_index, freq_index, freq_table, pair_weight, coulomb, band_vectors)


def solution(mesh):
    torus = Mesh(
        mesh.devices.reshape(mesh.shape["grp"], 4, 8, 2, mesh.shape["cols"]),
        ("grp", "rows_0", "rows_1", "rows_2", "cols"),
    )
    placed = (P(ROWS, None), P(ROWS), P(), P(), P(), P(), P())
    return jax.shard_map(
        per_device, mesh=torus, in_specs=placed, out_specs=P(ROWS_COLS, "grp"), check_vma=False
    )
```

```python
import math

import jax
import jax.numpy as jnp
from jax import lax
from jax.experimental import pallas as pl
from jax.experimental.pallas import tpu as pltpu
from jax.sharding import Mesh
from jax.sharding import PartitionSpec as P

NB = 49152
ROWS = ("rows_0", "rows_1", "rows_2")
ROWS_COLS = ("rows_0", "rows_1", "rows_2", "cols")
MESH = pl.DeviceIdType.MESH
F32 = jnp.float32
BF16 = jnp.bfloat16
KB = 768
NK = KB // 128
HALF = 768
RELS = [(a, b, d) for a in range(2) for b in range(2) for d in range(2)][1:]
NEAR = [(e, a, b, d) for e in range(4) for a in range(2) for b in range(2) for d in range(2)]


def split(x):
    hi = x.astype(BF16)
    return hi, (x - hi.astype(F32)).astype(BF16)


def nt(a, b):
    return lax.dot_general(a, b, (((1,), (1,)), ((), ())), preferred_element_type=F32)


def nn(a, b):
    return lax.dot_general(a, b, (((1,), (0,)), ((), ())), preferred_element_type=F32)


def nt3(ah, al, bh, bl):
    return nt(ah, bh) + nt(ah, bl) + nt(al, bh)


def nn3(ah, al, bh, bl):
    return nn(ah, bh) + nn(ah, bl) + nn(al, bh)


def mod(a, n):
    return lax.rem(a + n, n)


def window_kernel(
    occ, vir, fidx, ftab, weight, coulomb, v_hbm, out_ref,
    v_ref, vt, pt, ph, pw, qh, ql, nh, nl,
    r_own, r_oth, r_in, x_all, x_in,
    za_in, zb_in, zc_in, zr_in, yin, rfin, xfin, ry_in, xz_in,
    rq, xt, yt, xq, y32, yq, mbuf, m_in, sbuf, s_in,
    load, psend, precv, qsend, qrecv, ssend, srecv, send, recv,
):
    y = lax.axis_index("rows_0")
    z = lax.axis_index("rows_1")
    c = lax.axis_index("rows_2")
    g = lax.axis_index("grp")
    cl = lax.axis_index("cols")
    plane = 2 * g + cl
    started = []

    def copy(src, dst, to):
        i = len(started)
        d = pltpu.make_async_remote_copy(
            src_ref=src, dst_ref=dst, send_sem=send.at[i], recv_sem=recv.at[i],
            device_id=to, device_id_type=MESH,
        )
        d.start()
        started.append(d)
        return d

    def zto(k):
        return {"rows_1": mod(z + k, 8)}

    def yto(k):
        return {"rows_0": mod(y + k, 4)}

    def near(rel):
        ry, rg, rc, rl = rel
        return {
            "rows_0": mod(y + ry, 4), "grp": mod(g + rg, 2),
            "rows_2": mod(c + rc, 2), "cols": mod(cl + rl, 2),
        }

    vt2 = vt.reshape(8192, 128)
    pt2 = pt.reshape(2048, 128)
    loads = []
    for k in range(NK):
        rows = pl.ds(k * 128, 128)
        loads.append(pltpu.make_async_copy(v_hbm.at[rows], v_ref.at[rows], load.at[k]))
        loads[k].start()

    barrier = pltpu.get_barrier_semaphore()
    for k in range(1, 8):
        pl.semaphore_signal(barrier, inc=1, device_id=zto(k), device_id_type=MESH)
    for rel in NEAR[1:]:
        pl.semaphore_signal(barrier, inc=1, device_id=near(rel), device_id_type=MESH)

    for k in range(NK):
        loads[k].wait()
        for nb in range(8):
            block = v_ref[k * 128 : (k + 1) * 128, nb * 128 : (nb + 1) * 128]
            vt2[pl.ds(nb * 1024 + k, 128, stride=8), :] = block.T

    def gather(base, to):
        def some(i, carry):
            for u in range(16):
                at = i * 16 + u
                pt[to + at] = vt[occ[base + at]] * vt[vir[base + at]]
            return carry

        lax.fori_loop(0, 8, some, 0)

    def weights(base):
        row = weight[pl.ds(pl.multiple_of(base, 128), 128)].reshape(1, 128)
        return jnp.broadcast_to(row, (128, 128)).T

    def cvec(k):
        return coulomb[k * 128 : (k + 1) * 128].reshape(1, 128)

    for s in range(2):
        base = 256 * plane + 128 * mod(c + s, 2)
        gather(base, 128 * s)
        w = weights(base)
        for k in range(NK):
            x = pt2[pl.ds(s * 1024 + k, 128, stride=8), :] * w * cvec(k)
            hi, lo = split(x)
            qh[s * 128 : (s + 1) * 128, k * 128 : (k + 1) * 128] = hi
            ql[s * 128 : (s + 1) * 128, k * 128 : (k + 1) * 128] = lo
    for k in range(NK):
        for m in range(16):
            two = [
                vt2[pl.ds((32 * (2 * m + e) + 8 * plane) * 8 + k, 8, stride=8), :] for e in range(2)
            ]
            hi, lo = split(jnp.concatenate(two, axis=0) * cvec(k))
            nh[m * 16 : (m + 1) * 16, k * 128 : (k + 1) * 128] = hi
            nl[m * 16 : (m + 1) * 16, k * 128 : (k + 1) * 128] = lo

    core = {"rows_2": 1 - c}

    def to_partner(i):
        rows = pl.ds(pl.multiple_of(i * 256, 256), 256)
        return pltpu.make_async_remote_copy(
            src_ref=r_oth.at[rows], dst_ref=r_in.at[rows], send_sem=psend.at[i],
            recv_sem=precv.at[i], device_id=core, device_id_type=MESH,
        )

    def block(i, carry):
        half = mod(c + 1 + i // 3, 2)
        t = lax.rem(i, 3)
        for s in range(2):
            base = 512 * t + 256 * s + 128 * half
            gather(base, 128 * s)
            w = weights(base)
            for k in range(NK):
                hi, lo = split(pt2[pl.ds(s * 1024 + k, 128, stride=8), :] * w)
                ph[i, s * 128 : (s + 1) * 128, k * 128 : (k + 1) * 128] = hi
                pw[i, s * 128 : (s + 1) * 128, k * 128 : (k + 1) * 128] = lo
        r = nt3(ph[i], pw[i], qh[...], ql[...])
        n = half * 3 + t
        at = pl.multiple_of(n * 256, 256)
        r_own[pl.ds(at, 256), :] = r[:, 0:128]
        r_oth[pl.ds(at, 256), :] = r[:, 128:256]
        to_partner(n).start()
        return carry

    pl.semaphore_wait(barrier, 38)
    lax.fori_loop(0, 6, block, 0)

    def rpiece(k, ky):
        at = (ky * 8 + mod(z + k, 8)) * 48
        return r_own.at[pl.ds(pl.multiple_of(at, 8), 48)]

    sign = (-1, 1)
    for i in range(6):
        to_partner(i).wait()
    r_own[...] += r_in[...]
    fa = {}
    fb = {}
    fc = {}
    for j in range(2):
        for d in range(2):
            fa[d, j] = copy(rpiece(4 * sign[d], 2 * d + j), za_in.at[d, j], zto(2 * sign[d]))
    for ky in (0, 2, 1, 3):
        for d in range(2):
            fb[d, ky] = copy(rpiece(3 * sign[d], ky), zb_in.at[d, ky], zto(sign[d]))
    for ky in range(4):
        for d in range(2):
            fc[d, ky] = copy(rpiece(sign[d], ky), zc_in.at[d, ky], zto(sign[d]))

    px = []
    for t in range(3):
        x_all[0, t] = nt3(nh[...], nl[...], ph[t], pw[t])
        px.append(copy(x_all.at[0, t], x_in.at[t], core))
    for t in range(3):
        x_all[1, t] = nt3(nh[...], nl[...], ph[3 + t], pw[3 + t])

    def yrows(k, start, size):
        return pl.ds(pl.multiple_of(mod(y + k, 4) * 64 + start, 8), size)

    def yterm(k, h, q):
        return x_all.at[1, q, yrows(k, 32 * h, 32)]

    yl = {}
    ys = {}
    for q in range(3):
        px[q].wait_recv()
        x_all[1, q] += x_in[q]
        for d in range(2):
            yl[d, q] = copy(yterm(2, d, q), yin.at[d, q, 0], yto(sign[d]))
    for q in range(3):
        for d in range(2):
            ys[d, q] = copy(yterm(sign[d], 1 - d, q), yin.at[d, q, 1], yto(sign[d]))

    fr = {}
    for ky in (0, 2, 1, 3):
        for d in range(2):
            fb[d, ky].wait_recv()
            part = zb_in[d, ky] + rpiece(2 * sign[d], ky)[...]
            if ky // 2 == d:
                fa[d, ky % 2].wait_recv()
                part = part + za_in[d, ky % 2]
            zb_in[d, ky] = part
            fr[d, ky] = copy(zb_in.at[d, ky], zr_in.at[d, ky], zto(2 * sign[d]))
    for q in range(3):
        for d in range(2):
            yl[d, q].wait_recv()
            yin[d, q, 0] += yterm(sign[d], d, q)[...]
            yl[d, q] = copy(yin.at[d, q, 0], yin.at[d, q, 2], yto(sign[d]))

    for ky in (0, 2, 1, 3):
        part = rpiece(0, ky)[...]
        for d in range(2):
            fc[d, ky].wait_recv()
            fr[d, ky].wait_recv()
            part = part + (zc_in[d, ky] + zr_in[d, ky])
        rfin[ky] = part
    ry = [copy(rfin.at[mod(y + k, 4)], ry_in.at[k], yto(k)) for k in (2, 1, 3)]

    xz = []
    for q in range(3):
        for d in range(2):
            ys[d, q].wait_recv()
            yl[d, q].wait_recv()
        for h in range(2):
            xfin[q, 32 * h : 32 * h + 32] = (
                yterm(0, h, q)[...] + yin[h, q, 2] + yin[1 - h, q, 1]
            )
        for k in (4, 3, 5, 2, 6, 1, 7):
            rows = pl.ds(pl.multiple_of(mod(z + k, 8) * 8, 8), 8)
            xz.append(copy(xfin.at[q, rows], xz_in.at[k, q], zto(k)))

    for d in ry:
        d.wait_recv()
    rq[z] = (rfin[y] + (ry_in[1] + ry_in[2] + ry_in[3])) * (1.0 / NB)
    rz = [copy(rq.at[z], rq.at[z], zto(k)) for k in (4, 3, 5, 2, 6, 1, 7)]

    for d in xz:
        d.wait_recv()
    tile = xfin[:, pl.ds(pl.multiple_of(z * 8, 8), 8)]
    for k in range(1, 8):
        tile = tile + xz_in[k]
    chip = y * 8 + z
    row = lax.broadcasted_iota(jnp.int32, (3, 8, 256), 1)
    factor = jnp.zeros((3, 8, 256), F32)
    for i in range(8):
        factor = jnp.where(row == i, ftab[fidx[32 * chip + 8 * plane + i]], factor)
    tile = tile * factor * (1.0 / math.sqrt(NB))
    xt[0] = jnp.concatenate([tile[0], tile[1][:, 0:128]], axis=1)
    xt[1] = jnp.concatenate([tile[1][:, 128:256], tile[2]], axis=1)
    for j in range(4):
        yt[j] = tile[j // 2][:, 128 * (j % 2) : 128 * (j % 2) + 128]

    def quarter(i, rel, e):
        rg, rc, rl = rel
        to = {"grp": mod(g + rg, 2), "rows_2": mod(c + rc, 2), "cols": mod(cl + rl, 2)}
        to["rows_0"] = 2 * c + e
        return pltpu.make_async_remote_copy(
            src_ref=xt.at[e], dst_ref=xq.at[y, plane], send_sem=qsend.at[i],
            recv_sem=qrecv.at[y, plane], device_id=to, device_id_type=MESH,
        )

    quarters = [(rel, e) for e in range(2) for rel in [(0, 0, 0)] + RELS]
    for i, (rel, e) in enumerate(quarters):
        if rel == (0, 0, 0):

            @pl.when(y != 2 * c + e)
            def _(i=i, rel=rel, e=e):
                quarter(i, rel, e).start()

            @pl.when(y == 2 * c + e)
            def _(e=e):
                xq[y, plane] = xt[e]
        else:
            quarter(i, rel, e).start()
    yx = []
    for rg, rl in ((1, 1), (1, 0), (0, 1)):
        to = {"grp": mod(g + rg, 2), "cols": mod(cl + rl, 2)}
        yx.append(copy(yt.at[2 * to["grp"] + to["cols"]], y32.at[plane], to))
    y32[plane] = yt[plane]
    for d in yx:
        d.wait_recv()
    for j in range(4):
        yq[z, 8 * j : 8 * j + 8] = y32[j]
    yz = [copy(yq.at[z], yq.at[z], zto(k)) for k in (4, 3, 5, 2, 6, 1, 7)]

    for d in rz:
        d.wait_recv()
    for ys_ in range(4):
        for j in range(4):

            def arrived(ys_=ys_, j=j):
                pltpu.make_async_remote_copy(
                    src_ref=xt.at[0], dst_ref=xq.at[ys_, j], send_sem=qsend.at[0],
                    recv_sem=qrecv.at[ys_, j], device_id=core, device_id_type=MESH,
                ).wait_recv()

            own = (ys_ == y) & (j == plane) & (c == y // 2)
            pl.when(jnp.logical_not(own))(arrived)

    xh, xl = split(xq[...].reshape(128, 384))
    rh, rl_ = split(rq[...].reshape(384, 128))
    mbuf[...] = nn3(xh, xl, rh, rl_)
    my = [copy(mbuf, m_in.at[k], yto(k)) for k in (2, 1, 3)]
    for d in yz:
        d.wait_recv()
    yh, yw = split(yq[...].reshape(256, 128))
    for d in my:
        d.wait_recv()
    mh, ml = split(mbuf[...] + (m_in[1] + m_in[2] + m_in[3]))
    s = nt3(mh, ml, yh, yw)
    for i in range(16):
        sbuf[i] = s[8 * i : 8 * i + 8, :]

    e = lax.rem(y, 2)

    def result(i, ry_, rc, rl):
        to = {
            "grp": y // 2, "rows_0": mod(y + ry_, 4), "rows_2": mod(c + rc, 2), "cols": mod(cl + rl, 2),
        }
        src = to["rows_0"] * 4 + to["rows_2"] * 2 + to["cols"]
        return pltpu.make_async_remote_copy(
            src_ref=sbuf.at[src], dst_ref=s_in.at[e, plane, c], send_sem=ssend.at[i],
            recv_sem=srecv.at[e, plane, c], device_id=to, device_id_type=MESH,
        )

    results = [(a, b, d) for a in (0, 2, 1, 3) for b in range(2) for d in range(2)]
    for i, rel in enumerate(results):
        if rel == (0, 0, 0):

            @pl.when(y // 2 != g)
            def _(i=i, rel=rel):
                result(i, *rel).start()

            @pl.when(y // 2 == g)
            def _():
                s_in[e, plane, c] = sbuf[y * 4 + c * 2 + cl]
        else:
            result(i, *rel).start()
    for e_ in range(2):
        for j in range(4):
            for cs in range(2):

                def landed(e_=e_, j=j, cs=cs):
                    pltpu.make_async_remote_copy(
                        src_ref=sbuf.at[0], dst_ref=s_in.at[e_, j, cs], send_sem=ssend.at[0],
                        recv_sem=srecv.at[e_, j, cs], device_id=core, device_id_type=MESH,
                    ).wait_recv()

                own = (e_ == e) & (j == plane) & (cs == c) & (y // 2 == g)
                pl.when(jnp.logical_not(own))(landed)
    for e_ in range(2):
        total = s_in[e_, 0, 0]
        for n in range(1, 8):
            total = total + s_in[e_, n // 2, n % 2]
        out_ref[:, 256 * e_ : 256 * e_ + 256] = total * (1.0 / math.sqrt(1024))

    for i, (rel, e_) in enumerate(quarters):
        if rel == (0, 0, 0):

            @pl.when(y != 2 * c + e_)
            def _(i=i, rel=rel, e_=e_):
                quarter(i, rel, e_).wait_send()
        else:
            quarter(i, rel, e_).wait_send()
    for i, rel in enumerate(results):
        if rel == (0, 0, 0):

            @pl.when(y // 2 != g)
            def _(i=i, rel=rel):
                result(i, *rel).wait_send()
        else:
            result(i, *rel).wait_send()
    for d in started:
        d.wait_send()


def per_device(band_vectors, coulomb, pair_weight, occ_index, vir_index, freq_index, freq_table):
    smem = pl.BlockSpec(memory_space=pltpu.SMEM)
    vmem = pl.BlockSpec(memory_space=pltpu.VMEM)
    return pl.pallas_call(
        window_kernel,
        out_shape=jax.ShapeDtypeStruct((8, 512), F32),
        in_specs=[smem, smem, smem, smem, vmem, vmem, pl.BlockSpec(memory_space=pl.ANY)],
        out_specs=vmem,
        scratch_shapes=[
            pltpu.VMEM((KB, 1024), F32),
            pltpu.VMEM((1024, 8, 128), F32),
            pltpu.VMEM((256, 8, 128), F32),
            pltpu.VMEM((6, 256, KB), BF16),
            pltpu.VMEM((6, 256, KB), BF16),
            pltpu.VMEM((256, KB), BF16),
            pltpu.VMEM((256, KB), BF16),
            pltpu.VMEM((256, KB), BF16),
            pltpu.VMEM((256, KB), BF16),
            pltpu.VMEM((1536, 128), F32),
            pltpu.VMEM((1536, 128), F32),
            pltpu.VMEM((1536, 128), F32),
            pltpu.VMEM((2, 3, 256, 256), F32),
            pltpu.VMEM((3, 256, 256), F32),
            pltpu.VMEM((2, 2, 48, 128), F32),
            pltpu.VMEM((2, 4, 48, 128), F32),
            pltpu.VMEM((2, 4, 48, 128), F32),
            pltpu.VMEM((2, 4, 48, 128), F32),
            pltpu.VMEM((2, 3, 3, 32, 256), F32),
            pltpu.VMEM((4, 48, 128), F32),
            pltpu.VMEM((3, 64, 256), F32),
            pltpu.VMEM((4, 48, 128), F32),
            pltpu.VMEM((8, 3, 8, 256), F32),
            pltpu.VMEM((8, 48, 128), F32),
            pltpu.VMEM((2, 8, 384), F32),
            pltpu.VMEM((4, 8, 128), F32),
            pltpu.VMEM((4, 4, 8, 384), F32),
            pltpu.VMEM((4, 8, 128), F32),
            pltpu.VMEM((8, 32, 128), F32),
            pltpu.VMEM((128, 128), F32),
            pltpu.VMEM((4, 128, 128), F32),
            pltpu.VMEM((16, 8, 256), F32),
            pltpu.VMEM((2, 4, 2, 8, 256), F32),
            pltpu.SemaphoreType.DMA((NK,)),
            pltpu.SemaphoreType.DMA((6,)),
            pltpu.SemaphoreType.DMA((6,)),
            pltpu.SemaphoreType.DMA((16,)),
            pltpu.SemaphoreType.DMA((4, 4)),
            pltpu.SemaphoreType.DMA((16,)),
            pltpu.SemaphoreType.DMA((2, 4, 2)),
            pltpu.SemaphoreType.DMA((112,)),
            pltpu.SemaphoreType.DMA((112,)),
        ],
        compiler_params=pltpu.CompilerParams(collective_id=0, has_side_effects=True),
        name="window",
    )(occ_index, vir_index, freq_index, freq_table, pair_weight, coulomb, band_vectors)


def solution(mesh):
    torus = Mesh(
        mesh.devices.reshape(mesh.shape["grp"], 4, 8, 2, mesh.shape["cols"]),
        ("grp", "rows_0", "rows_1", "rows_2", "cols"),
    )
    placed = (P(ROWS, None), P(ROWS), P(), P(), P(), P(), P())
    return jax.shard_map(
        per_device, mesh=torus, in_specs=placed, out_specs=P(ROWS_COLS, "grp"), check_vma=False
    )
```

```python
import math

import jax
import jax.numpy as jnp
from jax import lax
from jax.experimental import pallas as pl
from jax.experimental.pallas import tpu as pltpu
from jax.sharding import Mesh
from jax.sharding import PartitionSpec as P

NB = 49152
ROWS = ("rows_0", "rows_1", "rows_2")
ROWS_COLS = ("rows_0", "rows_1", "rows_2", "cols")
MESH = pl.DeviceIdType.MESH
F32 = jnp.float32
BF16 = jnp.bfloat16
KB = 768
NK = KB // 128
HALF = 768
RELS = [(a, b, d) for a in range(2) for b in range(2) for d in range(2)][1:]
NEAR = [(e, a, b, d) for e in range(4) for a in range(2) for b in range(2) for d in range(2)]


def split(x):
    hi = x.astype(BF16)
    return hi, (x - hi.astype(F32)).astype(BF16)


def nt(a, b):
    return lax.dot_general(a, b, (((1,), (1,)), ((), ())), preferred_element_type=F32)


def nn(a, b):
    return lax.dot_general(a, b, (((1,), (0,)), ((), ())), preferred_element_type=F32)


def nt3(ah, al, bh, bl):
    return nt(ah, bh) + nt(ah, bl) + nt(al, bh)


def nn3(ah, al, bh, bl):
    return nn(ah, bh) + nn(ah, bl) + nn(al, bh)


def mod(a, n):
    return lax.rem(a + n, n)


def window_kernel(
    occ, vir, fidx, ftab, weight, coulomb, v_hbm, out_ref,
    v_ref, vt, pt, ph, pw, qh, ql, nh, nl,
    r_own, r_oth, r_in, x_all, x_in,
    za_in, zb_in, zc_in, zr_in, yin, rfin, xfin, ry_in, xz_in,
    rq, xt, yt, xq, y32, yq, mbuf, m_in, sbuf, s_in,
    load, psend, precv, qsend, qrecv, ssend, srecv, send, recv,
):
    y = lax.axis_index("rows_0")
    z = lax.axis_index("rows_1")
    c = lax.axis_index("rows_2")
    g = lax.axis_index("grp")
    cl = lax.axis_index("cols")
    plane = 2 * g + cl
    started = []

    def copy(src, dst, to):
        i = len(started)
        d = pltpu.make_async_remote_copy(
            src_ref=src, dst_ref=dst, send_sem=send.at[i], recv_sem=recv.at[i],
            device_id=to, device_id_type=MESH,
        )
        d.start()
        started.append(d)
        return d

    def zto(k):
        return {"rows_1": mod(z + k, 8)}

    def yto(k):
        return {"rows_0": mod(y + k, 4)}

    def near(rel):
        ry, rg, rc, rl = rel
        return {
            "rows_0": mod(y + ry, 4), "grp": mod(g + rg, 2),
            "rows_2": mod(c + rc, 2), "cols": mod(cl + rl, 2),
        }

    vt2 = vt.reshape(8192, 128)
    pt2 = pt.reshape(2048, 128)
    loads = []
    for k in range(NK):
        rows = pl.ds(k * 128, 128)
        loads.append(pltpu.make_async_copy(v_hbm.at[rows], v_ref.at[rows], load.at[k]))
        loads[k].start()

    barrier = pltpu.get_barrier_semaphore()
    for k in range(1, 8):
        pl.semaphore_signal(barrier, inc=1, device_id=zto(k), device_id_type=MESH)
    for rel in NEAR[1:]:
        pl.semaphore_signal(barrier, inc=1, device_id=near(rel), device_id_type=MESH)

    for k in range(NK):
        loads[k].wait()
        for nb in range(8):
            block = v_ref[k * 128 : (k + 1) * 128, nb * 128 : (nb + 1) * 128]
            vt2[pl.ds(nb * 1024 + k, 128, stride=8), :] = block.T

    def gather_some(base, to, count):
        for u in range(count):
            pt[to + u] = vt[occ[base + u]] * vt[vir[base + u]]

    def gather(base, to):
        def some(i, carry):
            gather_some(base + i * 32, to + i * 32, 32)
            return carry

        lax.fori_loop(0, 4, some, 0)

    def weights(base):
        row = weight[pl.ds(pl.multiple_of(base, 128), 128)].reshape(1, 128)
        return jnp.broadcast_to(row, (128, 128)).T

    def cvec(k):
        return coulomb[k * 128 : (k + 1) * 128].reshape(1, 128)

    for s in range(2):
        base = 256 * plane + 128 * mod(c + s, 2)
        gather(base, 128 * s)
        w = weights(base)
        for k in range(NK):
            x = pt2[pl.ds(s * 1024 + k, 128, stride=8), :] * w * cvec(k)
            hi, lo = split(x)
            qh[s * 128 : (s + 1) * 128, k * 128 : (k + 1) * 128] = hi
            ql[s * 128 : (s + 1) * 128, k * 128 : (k + 1) * 128] = lo
    core = {"rows_2": 1 - c}

    def to_partner(i):
        rows = pl.ds(pl.multiple_of(i * 256, 256), 256)
        return pltpu.make_async_remote_copy(
            src_ref=r_oth.at[rows], dst_ref=r_in.at[rows], send_sem=psend.at[i],
            recv_sem=precv.at[i], device_id=core, device_id_type=MESH,
        )

    def place(i):
        half = mod(c + 1 + i // 3, 2)
        t = lax.rem(i, 3)
        return half * 3 + t, [512 * t + 256 * s + 128 * half for s in range(2)]

    def rows_of(i, bases):
        for s in range(2):
            w = weights(bases[s])
            for k in range(NK):
                hi, lo = split(pt2[pl.ds(s * 1024 + k, 128, stride=8), :] * w)
                ph[i, s * 128 : (s + 1) * 128, k * 128 : (k + 1) * 128] = hi
                pw[i, s * 128 : (s + 1) * 128, k * 128 : (k + 1) * 128] = lo

    def response_of(i, n):
        r = nt3(ph[i], pw[i], qh[...], ql[...])
        at = pl.multiple_of(n * 256, 256)
        r_own[pl.ds(at, 256), :] = r[:, 0:128]
        r_oth[pl.ds(at, 256), :] = r[:, 128:256]

    def block(i, carry):
        n, _ = place(i - 1)
        _, bases = place(i)
        for s in range(2):
            gather_some(bases[s], 128 * s, 128)
        response_of(i - 1, n)
        to_partner(n).start()
        rows_of(i, bases)
        return carry

    first, bases = place(0)
    for s in range(2):
        gather(bases[s], 128 * s)
    rows_of(0, bases)
    pl.semaphore_wait(barrier, 38)
    lax.fori_loop(1, 6, block, 0)
    n, _ = place(5)
    response_of(5, n)
    to_partner(n).start()

    for k in range(NK):
        for m in range(16):
            two = [
                vt2[pl.ds((32 * (2 * m + e) + 8 * plane) * 8 + k, 8, stride=8), :] for e in range(2)
            ]
            hi, lo = split(jnp.concatenate(two, axis=0) * cvec(k))
            nh[m * 16 : (m + 1) * 16, k * 128 : (k + 1) * 128] = hi
            nl[m * 16 : (m + 1) * 16, k * 128 : (k + 1) * 128] = lo

    def rpiece(k, ky):
        at = (ky * 8 + mod(z + k, 8)) * 48
        return r_own.at[pl.ds(pl.multiple_of(at, 8), 48)]

    sign = (-1, 1)
    for i in range(6):
        to_partner(i).wait()
    r_own[...] += r_in[...]
    fa = {}
    fb = {}
    fc = {}
    for j in range(2):
        for d in range(2):
            fa[d, j] = copy(rpiece(4 * sign[d], 2 * d + j), za_in.at[d, j], zto(2 * sign[d]))
    for ky in (0, 2, 1, 3):
        for d in range(2):
            fb[d, ky] = copy(rpiece(3 * sign[d], ky), zb_in.at[d, ky], zto(sign[d]))
    for ky in range(4):
        for d in range(2):
            fc[d, ky] = copy(rpiece(sign[d], ky), zc_in.at[d, ky], zto(sign[d]))

    px = []
    for t in range(3):
        x_all[0, t] = nt3(nh[...], nl[...], ph[t], pw[t])
        px.append(copy(x_all.at[0, t], x_in.at[t], core))
    for t in range(3):
        x_all[1, t] = nt3(nh[...], nl[...], ph[3 + t], pw[3 + t])

    def yrows(k, start, size):
        return pl.ds(pl.multiple_of(mod(y + k, 4) * 64 + start, 8), size)

    def yterm(k, h, q):
        return x_all.at[1, q, yrows(k, 32 * h, 32)]

    yl = {}
    ys = {}
    for q in range(3):
        px[q].wait_recv()
        x_all[1, q] += x_in[q]
        for d in range(2):
            yl[d, q] = copy(yterm(2, d, q), yin.at[d, q, 0], yto(sign[d]))
    for q in range(3):
        for d in range(2):
            ys[d, q] = copy(yterm(sign[d], 1 - d, q), yin.at[d, q, 1], yto(sign[d]))

    fr = {}
    for ky in (0, 2, 1, 3):
        for d in range(2):
            fb[d, ky].wait_recv()
            part = zb_in[d, ky] + rpiece(2 * sign[d], ky)[...]
            if ky // 2 == d:
                fa[d, ky % 2].wait_recv()
                part = part + za_in[d, ky % 2]
            zb_in[d, ky] = part
            fr[d, ky] = copy(zb_in.at[d, ky], zr_in.at[d, ky], zto(2 * sign[d]))
    for q in range(3):
        for d in range(2):
            yl[d, q].wait_recv()
            yin[d, q, 0] += yterm(sign[d], d, q)[...]
            yl[d, q] = copy(yin.at[d, q, 0], yin.at[d, q, 2], yto(sign[d]))

    for ky in (0, 2, 1, 3):
        part = rpiece(0, ky)[...]
        for d in range(2):
            fc[d, ky].wait_recv()
            fr[d, ky].wait_recv()
            part = part + (zc_in[d, ky] + zr_in[d, ky])
        rfin[ky] = part
    ry = [copy(rfin.at[mod(y + k, 4)], ry_in.at[k], yto(k)) for k in (2, 1, 3)]

    xz = []
    for q in range(3):
        for d in range(2):
            ys[d, q].wait_recv()
            yl[d, q].wait_recv()
        for h in range(2):
            xfin[q, 32 * h : 32 * h + 32] = (
                yterm(0, h, q)[...] + yin[h, q, 2] + yin[1 - h, q, 1]
            )
        for k in (4, 3, 5, 2, 6, 1, 7):
            rows = pl.ds(pl.multiple_of(mod(z + k, 8) * 8, 8), 8)
            xz.append(copy(xfin.at[q, rows], xz_in.at[k, q], zto(k)))

    for d in ry:
        d.wait_recv()
    rq[z] = (rfin[y] + (ry_in[1] + ry_in[2] + ry_in[3])) * (1.0 / NB)
    rz = [copy(rq.at[z], rq.at[z], zto(k)) for k in (4, 3, 5, 2, 6, 1, 7)]

    for d in xz:
        d.wait_recv()
    tile = xfin[:, pl.ds(pl.multiple_of(z * 8, 8), 8)]
    for k in range(1, 8):
        tile = tile + xz_in[k]
    chip = y * 8 + z
    row = lax.broadcasted_iota(jnp.int32, (3, 8, 256), 1)
    factor = jnp.zeros((3, 8, 256), F32)
    for i in range(8):
        factor = jnp.where(row == i, ftab[fidx[32 * chip + 8 * plane + i]], factor)
    tile = tile * factor * (1.0 / math.sqrt(NB))
    xt[0] = jnp.concatenate([tile[0], tile[1][:, 0:128]], axis=1)
    xt[1] = jnp.concatenate([tile[1][:, 128:256], tile[2]], axis=1)
    for j in range(4):
        yt[j] = tile[j // 2][:, 128 * (j % 2) : 128 * (j % 2) + 128]

    def quarter(i, rel, e):
        rg, rc, rl = rel
        to = {"grp": mod(g + rg, 2), "rows_2": mod(c + rc, 2), "cols": mod(cl + rl, 2)}
        to["rows_0"] = 2 * c + e
        return pltpu.make_async_remote_copy(
            src_ref=xt.at[e], dst_ref=xq.at[y, plane], send_sem=qsend.at[i],
            recv_sem=qrecv.at[y, plane], device_id=to, device_id_type=MESH,
        )

    quarters = [(rel, e) for e in range(2) for rel in [(0, 0, 0)] + RELS]
    for i, (rel, e) in enumerate(quarters):
        if rel == (0, 0, 0):

            @pl.when(y != 2 * c + e)
            def _(i=i, rel=rel, e=e):
                quarter(i, rel, e).start()

            @pl.when(y == 2 * c + e)
            def _(e=e):
                xq[y, plane] = xt[e]
        else:
            quarter(i, rel, e).start()
    yx = []
    for rg, rl in ((1, 1), (1, 0), (0, 1)):
        to = {"grp": mod(g + rg, 2), "cols": mod(cl + rl, 2)}
        yx.append(copy(yt.at[2 * to["grp"] + to["cols"]], y32.at[plane], to))
    y32[plane] = yt[plane]
    for d in yx:
        d.wait_recv()
    for j in range(4):
        yq[z, 8 * j : 8 * j + 8] = y32[j]
    yz = [copy(yq.at[z], yq.at[z], zto(k)) for k in (4, 3, 5, 2, 6, 1, 7)]

    for d in rz:
        d.wait_recv()
    for ys_ in range(4):
        for j in range(4):

            def arrived(ys_=ys_, j=j):
                pltpu.make_async_remote_copy(
                    src_ref=xt.at[0], dst_ref=xq.at[ys_, j], send_sem=qsend.at[0],
                    recv_sem=qrecv.at[ys_, j], device_id=core, device_id_type=MESH,
                ).wait_recv()

            own = (ys_ == y) & (j == plane) & (c == y // 2)
            pl.when(jnp.logical_not(own))(arrived)

    xh, xl = split(xq[...].reshape(128, 384))
    rh, rl_ = split(rq[...].reshape(384, 128))
    mbuf[...] = nn3(xh, xl, rh, rl_)
    my = [copy(mbuf, m_in.at[k], yto(k)) for k in (2, 1, 3)]
    for d in yz:
        d.wait_recv()
    yh, yw = split(yq[...].reshape(256, 128))
    for d in my:
        d.wait_recv()
    mh, ml = split(mbuf[...] + (m_in[1] + m_in[2] + m_in[3]))
    s = nt3(mh, ml, yh, yw)
    for i in range(16):
        sbuf[i] = s[8 * i : 8 * i + 8, :]

    e = lax.rem(y, 2)

    def result(i, ry_, rc, rl):
        to = {
            "grp": y // 2, "rows_0": mod(y + ry_, 4), "rows_2": mod(c + rc, 2), "cols": mod(cl + rl, 2),
        }
        src = to["rows_0"] * 4 + to["rows_2"] * 2 + to["cols"]
        return pltpu.make_async_remote_copy(
            src_ref=sbuf.at[src], dst_ref=s_in.at[e, plane, c], send_sem=ssend.at[i],
            recv_sem=srecv.at[e, plane, c], device_id=to, device_id_type=MESH,
        )

    results = [(a, b, d) for a in (0, 2, 1, 3) for b in range(2) for d in range(2)]
    for i, rel in enumerate(results):
        if rel == (0, 0, 0):

            @pl.when(y // 2 != g)
            def _(i=i, rel=rel):
                result(i, *rel).start()

            @pl.when(y // 2 == g)
            def _():
                s_in[e, plane, c] = sbuf[y * 4 + c * 2 + cl]
        else:
            result(i, *rel).start()
    for e_ in range(2):
        for j in range(4):
            for cs in range(2):

                def landed(e_=e_, j=j, cs=cs):
                    pltpu.make_async_remote_copy(
                        src_ref=sbuf.at[0], dst_ref=s_in.at[e_, j, cs], send_sem=ssend.at[0],
                        recv_sem=srecv.at[e_, j, cs], device_id=core, device_id_type=MESH,
                    ).wait_recv()

                own = (e_ == e) & (j == plane) & (cs == c) & (y // 2 == g)
                pl.when(jnp.logical_not(own))(landed)
    for e_ in range(2):
        total = s_in[e_, 0, 0]
        for n in range(1, 8):
            total = total + s_in[e_, n // 2, n % 2]
        out_ref[:, 256 * e_ : 256 * e_ + 256] = total * (1.0 / math.sqrt(1024))

    for i, (rel, e_) in enumerate(quarters):
        if rel == (0, 0, 0):

            @pl.when(y != 2 * c + e_)
            def _(i=i, rel=rel, e_=e_):
                quarter(i, rel, e_).wait_send()
        else:
            quarter(i, rel, e_).wait_send()
    for i, rel in enumerate(results):
        if rel == (0, 0, 0):

            @pl.when(y // 2 != g)
            def _(i=i, rel=rel):
                result(i, *rel).wait_send()
        else:
            result(i, *rel).wait_send()
    for d in started:
        d.wait_send()


def per_device(band_vectors, coulomb, pair_weight, occ_index, vir_index, freq_index, freq_table):
    smem = pl.BlockSpec(memory_space=pltpu.SMEM)
    vmem = pl.BlockSpec(memory_space=pltpu.VMEM)
    return pl.pallas_call(
        window_kernel,
        out_shape=jax.ShapeDtypeStruct((8, 512), F32),
        in_specs=[smem, smem, smem, smem, vmem, vmem, pl.BlockSpec(memory_space=pl.ANY)],
        out_specs=vmem,
        scratch_shapes=[
            pltpu.VMEM((KB, 1024), F32),
            pltpu.VMEM((1024, 8, 128), F32),
            pltpu.VMEM((256, 8, 128), F32),
            pltpu.VMEM((6, 256, KB), BF16),
            pltpu.VMEM((6, 256, KB), BF16),
            pltpu.VMEM((256, KB), BF16),
            pltpu.VMEM((256, KB), BF16),
            pltpu.VMEM((256, KB), BF16),
            pltpu.VMEM((256, KB), BF16),
            pltpu.VMEM((1536, 128), F32),
            pltpu.VMEM((1536, 128), F32),
            pltpu.VMEM((1536, 128), F32),
            pltpu.VMEM((2, 3, 256, 256), F32),
            pltpu.VMEM((3, 256, 256), F32),
            pltpu.VMEM((2, 2, 48, 128), F32),
            pltpu.VMEM((2, 4, 48, 128), F32),
            pltpu.VMEM((2, 4, 48, 128), F32),
            pltpu.VMEM((2, 4, 48, 128), F32),
            pltpu.VMEM((2, 3, 3, 32, 256), F32),
            pltpu.VMEM((4, 48, 128), F32),
            pltpu.VMEM((3, 64, 256), F32),
            pltpu.VMEM((4, 48, 128), F32),
            pltpu.VMEM((8, 3, 8, 256), F32),
            pltpu.VMEM((8, 48, 128), F32),
            pltpu.VMEM((2, 8, 384), F32),
            pltpu.VMEM((4, 8, 128), F32),
            pltpu.VMEM((4, 4, 8, 384), F32),
            pltpu.VMEM((4, 8, 128), F32),
            pltpu.VMEM((8, 32, 128), F32),
            pltpu.VMEM((128, 128), F32),
            pltpu.VMEM((4, 128, 128), F32),
            pltpu.VMEM((16, 8, 256), F32),
            pltpu.VMEM((2, 4, 2, 8, 256), F32),
            pltpu.SemaphoreType.DMA((NK,)),
            pltpu.SemaphoreType.DMA((6,)),
            pltpu.SemaphoreType.DMA((6,)),
            pltpu.SemaphoreType.DMA((16,)),
            pltpu.SemaphoreType.DMA((4, 4)),
            pltpu.SemaphoreType.DMA((16,)),
            pltpu.SemaphoreType.DMA((2, 4, 2)),
            pltpu.SemaphoreType.DMA((112,)),
            pltpu.SemaphoreType.DMA((112,)),
        ],
        compiler_params=pltpu.CompilerParams(collective_id=0, has_side_effects=True),
        name="window",
    )(occ_index, vir_index, freq_index, freq_table, pair_weight, coulomb, band_vectors)


def solution(mesh):
    torus = Mesh(
        mesh.devices.reshape(mesh.shape["grp"], 4, 8, 2, mesh.shape["cols"]),
        ("grp", "rows_0", "rows_1", "rows_2", "cols"),
    )
    placed = (P(ROWS, None), P(ROWS), P(), P(), P(), P(), P())
    return jax.shard_map(
        per_device, mesh=torus, in_specs=placed, out_specs=P(ROWS_COLS, "grp"), check_vma=False
    )
```

```python
import math

import jax
import jax.numpy as jnp
from jax import lax
from jax.experimental import pallas as pl
from jax.experimental.pallas import tpu as pltpu
from jax.sharding import Mesh
from jax.sharding import PartitionSpec as P

NB = 49152
ROWS = ("rows_0", "rows_1", "rows_2")
ROWS_COLS = ("rows_0", "rows_1", "rows_2", "cols")
MESH = pl.DeviceIdType.MESH
F32 = jnp.float32
BF16 = jnp.bfloat16
KB = 768
NK = KB // 128
HALF = 768
RELS = [(a, b, d) for a in range(2) for b in range(2) for d in range(2)][1:]
NEAR = [(e, a, b, d) for e in range(4) for a in range(2) for b in range(2) for d in range(2)]


def split(x):
    hi = x.astype(BF16)
    return hi, (x - hi.astype(F32)).astype(BF16)


def nt(a, b):
    return lax.dot_general(a, b, (((1,), (1,)), ((), ())), preferred_element_type=F32)


def nn(a, b):
    return lax.dot_general(a, b, (((1,), (0,)), ((), ())), preferred_element_type=F32)


def nt3(ah, al, bh, bl):
    return nt(ah, bh) + nt(ah, bl) + nt(al, bh)


def nn3(ah, al, bh, bl):
    return nn(ah, bh) + nn(ah, bl) + nn(al, bh)


def mod(a, n):
    return lax.rem(a + n, n)


def window_kernel(
    occ, vir, fidx, ftab, weight, coulomb, v_hbm, out_ref,
    v_ref, vt, pt, qt, ph, pw, qh, ql, nh, nl,
    r_own, r_oth, r_in, x_all, x_in,
    za_in, zb_in, zc_in, zr_in, yin, rfin, xfin, ry_in, xz_in,
    rq, xt, yt, xq, y32, yq, mbuf, m_in, sbuf, s_in,
    load, psend, precv, qsend, qrecv, ssend, srecv, send, recv,
):
    y = lax.axis_index("rows_0")
    z = lax.axis_index("rows_1")
    c = lax.axis_index("rows_2")
    g = lax.axis_index("grp")
    cl = lax.axis_index("cols")
    plane = 2 * g + cl
    started = []

    def copy(src, dst, to):
        i = len(started)
        d = pltpu.make_async_remote_copy(
            src_ref=src, dst_ref=dst, send_sem=send.at[i], recv_sem=recv.at[i],
            device_id=to, device_id_type=MESH,
        )
        d.start()
        started.append(d)
        return d

    def zto(k):
        return {"rows_1": mod(z + k, 8)}

    def yto(k):
        return {"rows_0": mod(y + k, 4)}

    def near(rel):
        ry, rg, rc, rl = rel
        return {
            "rows_0": mod(y + ry, 4), "grp": mod(g + rg, 2),
            "rows_2": mod(c + rc, 2), "cols": mod(cl + rl, 2),
        }

    vt2 = vt.reshape(8192, 128)
    pts = (pt, qt)
    pt2s = (pt.reshape(2048, 128), qt.reshape(2048, 128))
    loads = []
    for k in range(NK):
        rows = pl.ds(k * 128, 128)
        loads.append(pltpu.make_async_copy(v_hbm.at[rows], v_ref.at[rows], load.at[k]))
        loads[k].start()

    barrier = pltpu.get_barrier_semaphore()
    for k in range(1, 8):
        pl.semaphore_signal(barrier, inc=1, device_id=zto(k), device_id_type=MESH)
    for rel in NEAR[1:]:
        pl.semaphore_signal(barrier, inc=1, device_id=near(rel), device_id_type=MESH)

    for k in range(NK):
        loads[k].wait()
        for nb in range(8):
            block = v_ref[k * 128 : (k + 1) * 128, nb * 128 : (nb + 1) * 128]
            vt2[pl.ds(nb * 1024 + k, 128, stride=8), :] = block.T

    def gather_some(base, to, count, rows=pt):
        for u in range(count):
            rows[to + u] = vt[occ[base + u]] * vt[vir[base + u]]

    def gather(base, to):
        def some(i, carry):
            gather_some(base + i * 32, to + i * 32, 32)
            return carry

        lax.fori_loop(0, 4, some, 0)

    def weights(base):
        row = weight[pl.ds(pl.multiple_of(base, 128), 128)].reshape(1, 128)
        return jnp.broadcast_to(row, (128, 128)).T

    def cvec(k):
        return coulomb[k * 128 : (k + 1) * 128].reshape(1, 128)

    for s in range(2):
        base = 256 * plane + 128 * mod(c + s, 2)
        gather(base, 128 * s)
        w = weights(base)
        for k in range(NK):
            x = pt2s[0][pl.ds(s * 1024 + k, 128, stride=8), :] * w * cvec(k)
            hi, lo = split(x)
            qh[s * 128 : (s + 1) * 128, k * 128 : (k + 1) * 128] = hi
            ql[s * 128 : (s + 1) * 128, k * 128 : (k + 1) * 128] = lo
    core = {"rows_2": 1 - c}

    def to_partner(i):
        rows = pl.ds(pl.multiple_of(i * 256, 256), 256)
        return pltpu.make_async_remote_copy(
            src_ref=r_oth.at[rows], dst_ref=r_in.at[rows], send_sem=psend.at[i],
            recv_sem=precv.at[i], device_id=core, device_id_type=MESH,
        )

    def place(i):
        half = mod(c + 1 + i // 3, 2)
        t = i % 3
        return half * 3 + t, [512 * t + 256 * s + 128 * half for s in range(2)]

    def rows_of(i, bases):
        for s in range(2):
            w = weights(bases[s])
            for k in range(NK):
                hi, lo = split(pt2s[i % 2][pl.ds(s * 1024 + k, 128, stride=8), :] * w)
                ph[i, s * 128 : (s + 1) * 128, k * 128 : (k + 1) * 128] = hi
                pw[i, s * 128 : (s + 1) * 128, k * 128 : (k + 1) * 128] = lo

    def response_of(i, n):
        r = nt3(ph[i], pw[i], qh[...], ql[...])
        at = pl.multiple_of(n * 256, 256)
        r_own[pl.ds(at, 256), :] = r[:, 0:128]
        r_oth[pl.ds(at, 256), :] = r[:, 128:256]

    for i in range(8):
        if i == 2:
            pl.semaphore_wait(barrier, 38)
        if i < 6:
            for e in range(2):
                gather_some(place(i)[1][e], 128 * e, 128, pts[i % 2])
        if 1 <= i < 7:
            rows_of(i - 1, place(i - 1)[1])
        if i >= 2:
            n, _ = place(i - 2)
            response_of(i - 2, n)
            to_partner(n).start()

    for k in range(NK):
        for m in range(16):
            two = [
                vt2[pl.ds((32 * (2 * m + e) + 8 * plane) * 8 + k, 8, stride=8), :] for e in range(2)
            ]
            hi, lo = split(jnp.concatenate(two, axis=0) * cvec(k))
            nh[m * 16 : (m + 1) * 16, k * 128 : (k + 1) * 128] = hi
            nl[m * 16 : (m + 1) * 16, k * 128 : (k + 1) * 128] = lo

    def rpiece(k, ky):
        at = (ky * 8 + mod(z + k, 8)) * 48
        return r_own.at[pl.ds(pl.multiple_of(at, 8), 48)]

    sign = (-1, 1)
    for i in range(6):
        to_partner(i).wait()
    r_own[...] += r_in[...]
    fa = {}
    fb = {}
    fc = {}
    for j in range(2):
        for d in range(2):
            fa[d, j] = copy(rpiece(4 * sign[d], 2 * d + j), za_in.at[d, j], zto(2 * sign[d]))
    for ky in (0, 2, 1, 3):
        for d in range(2):
            fb[d, ky] = copy(rpiece(3 * sign[d], ky), zb_in.at[d, ky], zto(sign[d]))
    for ky in range(4):
        for d in range(2):
            fc[d, ky] = copy(rpiece(sign[d], ky), zc_in.at[d, ky], zto(sign[d]))

    px = []
    for t in range(3):
        x_all[0, t] = nt3(nh[...], nl[...], ph[t], pw[t])
        px.append(copy(x_all.at[0, t], x_in.at[t], core))
    for t in range(3):
        x_all[1, t] = nt3(nh[...], nl[...], ph[3 + t], pw[3 + t])

    def yrows(k, start, size):
        return pl.ds(pl.multiple_of(mod(y + k, 4) * 64 + start, 8), size)

    def yterm(k, h, q):
        return x_all.at[1, q, yrows(k, 32 * h, 32)]

    yl = {}
    ys = {}
    for q in range(3):
        px[q].wait_recv()
        x_all[1, q] += x_in[q]
        for d in range(2):
            yl[d, q] = copy(yterm(2, d, q), yin.at[d, q, 0], yto(sign[d]))
    for q in range(3):
        for d in range(2):
            ys[d, q] = copy(yterm(sign[d], 1 - d, q), yin.at[d, q, 1], yto(sign[d]))

    fr = {}
    for ky in (0, 2, 1, 3):
        for d in range(2):
            fb[d, ky].wait_recv()
            part = zb_in[d, ky] + rpiece(2 * sign[d], ky)[...]
            if ky // 2 == d:
                fa[d, ky % 2].wait_recv()
                part = part + za_in[d, ky % 2]
            zb_in[d, ky] = part
            fr[d, ky] = copy(zb_in.at[d, ky], zr_in.at[d, ky], zto(2 * sign[d]))
    for q in range(3):
        for d in range(2):
            yl[d, q].wait_recv()
            yin[d, q, 0] += yterm(sign[d], d, q)[...]
            yl[d, q] = copy(yin.at[d, q, 0], yin.at[d, q, 2], yto(sign[d]))

    for ky in (0, 2, 1, 3):
        part = rpiece(0, ky)[...]
        for d in range(2):
            fc[d, ky].wait_recv()
            fr[d, ky].wait_recv()
            part = part + (zc_in[d, ky] + zr_in[d, ky])
        rfin[ky] = part
    ry = [copy(rfin.at[mod(y + k, 4)], ry_in.at[k], yto(k)) for k in (2, 1, 3)]

    xz = []
    for q in range(3):
        for d in range(2):
            ys[d, q].wait_recv()
            yl[d, q].wait_recv()
        for h in range(2):
            xfin[q, 32 * h : 32 * h + 32] = (
                yterm(0, h, q)[...] + yin[h, q, 2] + yin[1 - h, q, 1]
            )
        for k in (4, 3, 5, 2, 6, 1, 7):
            rows = pl.ds(pl.multiple_of(mod(z + k, 8) * 8, 8), 8)
            xz.append(copy(xfin.at[q, rows], xz_in.at[k, q], zto(k)))

    for d in ry:
        d.wait_recv()
    rq[z] = (rfin[y] + (ry_in[1] + ry_in[2] + ry_in[3])) * (1.0 / NB)
    rz = [copy(rq.at[z], rq.at[z], zto(k)) for k in (4, 3, 5, 2, 6, 1, 7)]

    for d in xz:
        d.wait_recv()
    tile = xfin[:, pl.ds(pl.multiple_of(z * 8, 8), 8)]
    for k in range(1, 8):
        tile = tile + xz_in[k]
    chip = y * 8 + z
    row = lax.broadcasted_iota(jnp.int32, (3, 8, 256), 1)
    factor = jnp.zeros((3, 8, 256), F32)
    for i in range(8):
        factor = jnp.where(row == i, ftab[fidx[32 * chip + 8 * plane + i]], factor)
    tile = tile * factor * (1.0 / math.sqrt(NB))
    xt[0] = jnp.concatenate([tile[0], tile[1][:, 0:128]], axis=1)
    xt[1] = jnp.concatenate([tile[1][:, 128:256], tile[2]], axis=1)
    for j in range(4):
        yt[j] = tile[j // 2][:, 128 * (j % 2) : 128 * (j % 2) + 128]

    def quarter(i, rel, e):
        rg, rc, rl = rel
        to = {"grp": mod(g + rg, 2), "rows_2": mod(c + rc, 2), "cols": mod(cl + rl, 2)}
        to["rows_0"] = 2 * c + e
        return pltpu.make_async_remote_copy(
            src_ref=xt.at[e], dst_ref=xq.at[y, plane], send_sem=qsend.at[i],
            recv_sem=qrecv.at[y, plane], device_id=to, device_id_type=MESH,
        )

    quarters = [(rel, e) for e in range(2) for rel in [(0, 0, 0)] + RELS]
    for i, (rel, e) in enumerate(quarters):
        if rel == (0, 0, 0):

            @pl.when(y != 2 * c + e)
            def _(i=i, rel=rel, e=e):
                quarter(i, rel, e).start()

            @pl.when(y == 2 * c + e)
            def _(e=e):
                xq[y, plane] = xt[e]
        else:
            quarter(i, rel, e).start()
    yx = []
    for rg, rl in ((1, 1), (1, 0), (0, 1)):
        to = {"grp": mod(g + rg, 2), "cols": mod(cl + rl, 2)}
        yx.append(copy(yt.at[2 * to["grp"] + to["cols"]], y32.at[plane], to))
    y32[plane] = yt[plane]
    for d in yx:
        d.wait_recv()
    for j in range(4):
        yq[z, 8 * j : 8 * j + 8] = y32[j]
    yz = [copy(yq.at[z], yq.at[z], zto(k)) for k in (4, 3, 5, 2, 6, 1, 7)]

    for d in rz:
        d.wait_recv()
    for ys_ in range(4):
        for j in range(4):

            def arrived(ys_=ys_, j=j):
                pltpu.make_async_remote_copy(
                    src_ref=xt.at[0], dst_ref=xq.at[ys_, j], send_sem=qsend.at[0],
                    recv_sem=qrecv.at[ys_, j], device_id=core, device_id_type=MESH,
                ).wait_recv()

            own = (ys_ == y) & (j == plane) & (c == y // 2)
            pl.when(jnp.logical_not(own))(arrived)

    xh, xl = split(xq[...].reshape(128, 384))
    rh, rl_ = split(rq[...].reshape(384, 128))
    mbuf[...] = nn3(xh, xl, rh, rl_)
    my = [copy(mbuf, m_in.at[k], yto(k)) for k in (2, 1, 3)]
    for d in yz:
        d.wait_recv()
    yh, yw = split(yq[...].reshape(256, 128))
    for d in my:
        d.wait_recv()
    mh, ml = split(mbuf[...] + (m_in[1] + m_in[2] + m_in[3]))
    s = nt3(mh, ml, yh, yw)
    for i in range(16):
        sbuf[i] = s[8 * i : 8 * i + 8, :]

    e = lax.rem(y, 2)

    def result(i, ry_, rc, rl):
        to = {
            "grp": y // 2, "rows_0": mod(y + ry_, 4), "rows_2": mod(c + rc, 2), "cols": mod(cl + rl, 2),
        }
        src = to["rows_0"] * 4 + to["rows_2"] * 2 + to["cols"]
        return pltpu.make_async_remote_copy(
            src_ref=sbuf.at[src], dst_ref=s_in.at[e, plane, c], send_sem=ssend.at[i],
            recv_sem=srecv.at[e, plane, c], device_id=to, device_id_type=MESH,
        )

    results = [(a, b, d) for a in (0, 2, 1, 3) for b in range(2) for d in range(2)]
    for i, rel in enumerate(results):
        if rel == (0, 0, 0):

            @pl.when(y // 2 != g)
            def _(i=i, rel=rel):
                result(i, *rel).start()

            @pl.when(y // 2 == g)
            def _():
                s_in[e, plane, c] = sbuf[y * 4 + c * 2 + cl]
        else:
            result(i, *rel).start()
    for e_ in range(2):
        for j in range(4):
            for cs in range(2):

                def landed(e_=e_, j=j, cs=cs):
                    pltpu.make_async_remote_copy(
                        src_ref=sbuf.at[0], dst_ref=s_in.at[e_, j, cs], send_sem=ssend.at[0],
                        recv_sem=srecv.at[e_, j, cs], device_id=core, device_id_type=MESH,
                    ).wait_recv()

                own = (e_ == e) & (j == plane) & (cs == c) & (y // 2 == g)
                pl.when(jnp.logical_not(own))(landed)
    for e_ in range(2):
        total = s_in[e_, 0, 0]
        for n in range(1, 8):
            total = total + s_in[e_, n // 2, n % 2]
        out_ref[:, 256 * e_ : 256 * e_ + 256] = total * (1.0 / math.sqrt(1024))

    for i, (rel, e_) in enumerate(quarters):
        if rel == (0, 0, 0):

            @pl.when(y != 2 * c + e_)
            def _(i=i, rel=rel, e_=e_):
                quarter(i, rel, e_).wait_send()
        else:
            quarter(i, rel, e_).wait_send()
    for i, rel in enumerate(results):
        if rel == (0, 0, 0):

            @pl.when(y // 2 != g)
            def _(i=i, rel=rel):
                result(i, *rel).wait_send()
        else:
            result(i, *rel).wait_send()
    for d in started:
        d.wait_send()


def per_device(band_vectors, coulomb, pair_weight, occ_index, vir_index, freq_index, freq_table):
    smem = pl.BlockSpec(memory_space=pltpu.SMEM)
    vmem = pl.BlockSpec(memory_space=pltpu.VMEM)
    return pl.pallas_call(
        window_kernel,
        out_shape=jax.ShapeDtypeStruct((8, 512), F32),
        in_specs=[smem, smem, smem, smem, vmem, vmem, pl.BlockSpec(memory_space=pl.ANY)],
        out_specs=vmem,
        scratch_shapes=[
            pltpu.VMEM((KB, 1024), F32),
            pltpu.VMEM((1024, 8, 128), F32),
            pltpu.VMEM((256, 8, 128), F32),
            pltpu.VMEM((256, 8, 128), F32),
            pltpu.VMEM((6, 256, KB), BF16),
            pltpu.VMEM((6, 256, KB), BF16),
            pltpu.VMEM((256, KB), BF16),
            pltpu.VMEM((256, KB), BF16),
            pltpu.VMEM((256, KB), BF16),
            pltpu.VMEM((256, KB), BF16),
            pltpu.VMEM((1536, 128), F32),
            pltpu.VMEM((1536, 128), F32),
            pltpu.VMEM((1536, 128), F32),
            pltpu.VMEM((2, 3, 256, 256), F32),
            pltpu.VMEM((3, 256, 256), F32),
            pltpu.VMEM((2, 2, 48, 128), F32),
            pltpu.VMEM((2, 4, 48, 128), F32),
            pltpu.VMEM((2, 4, 48, 128), F32),
            pltpu.VMEM((2, 4, 48, 128), F32),
            pltpu.VMEM((2, 3, 3, 32, 256), F32),
            pltpu.VMEM((4, 48, 128), F32),
            pltpu.VMEM((3, 64, 256), F32),
            pltpu.VMEM((4, 48, 128), F32),
            pltpu.VMEM((8, 3, 8, 256), F32),
            pltpu.VMEM((8, 48, 128), F32),
            pltpu.VMEM((2, 8, 384), F32),
            pltpu.VMEM((4, 8, 128), F32),
            pltpu.VMEM((4, 4, 8, 384), F32),
            pltpu.VMEM((4, 8, 128), F32),
            pltpu.VMEM((8, 32, 128), F32),
            pltpu.VMEM((128, 128), F32),
            pltpu.VMEM((4, 128, 128), F32),
            pltpu.VMEM((16, 8, 256), F32),
            pltpu.VMEM((2, 4, 2, 8, 256), F32),
            pltpu.SemaphoreType.DMA((NK,)),
            pltpu.SemaphoreType.DMA((6,)),
            pltpu.SemaphoreType.DMA((6,)),
            pltpu.SemaphoreType.DMA((16,)),
            pltpu.SemaphoreType.DMA((4, 4)),
            pltpu.SemaphoreType.DMA((16,)),
            pltpu.SemaphoreType.DMA((2, 4, 2)),
            pltpu.SemaphoreType.DMA((112,)),
            pltpu.SemaphoreType.DMA((112,)),
        ],
        compiler_params=pltpu.CompilerParams(collective_id=0, has_side_effects=True),
        name="window",
    )(occ_index, vir_index, freq_index, freq_table, pair_weight, coulomb, band_vectors)


def solution(mesh):
    torus = Mesh(
        mesh.devices.reshape(mesh.shape["grp"], 4, 8, 2, mesh.shape["cols"]),
        ("grp", "rows_0", "rows_1", "rows_2", "cols"),
    )
    placed = (P(ROWS, None), P(ROWS), P(), P(), P(), P(), P())
    return jax.shard_map(
        per_device, mesh=torus, in_specs=placed, out_specs=P(ROWS_COLS, "grp"), check_vma=False
    )
```

```python
import math

import jax
import jax.numpy as jnp
from jax import lax
from jax.experimental import pallas as pl
from jax.experimental.pallas import tpu as pltpu
from jax.sharding import Mesh
from jax.sharding import PartitionSpec as P

NB = 49152
ROWS = ("rows_0", "rows_1", "rows_2")
ROWS_COLS = ("rows_0", "rows_1", "rows_2", "cols")
MESH = pl.DeviceIdType.MESH
F32 = jnp.float32
BF16 = jnp.bfloat16
KB = 768
NK = KB // 128
HALF = 768
RELS = [(a, b, d) for a in range(2) for b in range(2) for d in range(2)][1:]
NEAR = [(e, a, b, d) for e in range(4) for a in range(2) for b in range(2) for d in range(2)]


def split(x):
    hi = x.astype(BF16)
    return hi, (x - hi.astype(F32)).astype(BF16)


def nt(a, b):
    return lax.dot_general(a, b, (((1,), (1,)), ((), ())), preferred_element_type=F32)


def nn(a, b):
    return lax.dot_general(a, b, (((1,), (0,)), ((), ())), preferred_element_type=F32)


def nt3(ah, al, bh, bl):
    return nt(ah, bh) + nt(ah, bl) + nt(al, bh)


def nn3(ah, al, bh, bl):
    return nn(ah, bh) + nn(ah, bl) + nn(al, bh)


def mod(a, n):
    return lax.rem(a + n, n)


def window_kernel(
    occ, vir, fidx, ftab, weight, coulomb, v_hbm, out_ref,
    v_ref, vt, pt, qt, ph, pw, qh, ql, nh, nl,
    r_own, r_oth, r_in, x_all, x_in,
    za_in, zb_in, zc_in, zr_in, yin, rfin, xfin, ry_in, xz_in,
    rq, xt, yt, xq, y32, yq, mbuf, m_in, sbuf, s_pair, s_in,
    load, psend, precv, xpsend, xprecv, qsend, qrecv, ssend, srecv, send, recv,
):
    y = lax.axis_index("rows_0")
    z = lax.axis_index("rows_1")
    c = lax.axis_index("rows_2")
    g = lax.axis_index("grp")
    cl = lax.axis_index("cols")
    plane = 2 * g + cl
    started = []

    def copy(src, dst, to):
        i = len(started)
        d = pltpu.make_async_remote_copy(
            src_ref=src, dst_ref=dst, send_sem=send.at[i], recv_sem=recv.at[i],
            device_id=to, device_id_type=MESH,
        )
        d.start()
        started.append(d)
        return d

    def zto(k):
        return {"rows_1": mod(z + k, 8)}

    def yto(k):
        return {"rows_0": mod(y + k, 4)}

    def near(rel):
        ry, rg, rc, rl = rel
        return {
            "rows_0": mod(y + ry, 4), "grp": mod(g + rg, 2),
            "rows_2": mod(c + rc, 2), "cols": mod(cl + rl, 2),
        }

    vt2 = vt.reshape(8192, 128)
    pts = (pt, qt)
    pt2s = (pt.reshape(2048, 128), qt.reshape(2048, 128))
    loads = []
    for k in range(NK):
        rows = pl.ds(k * 128, 128)
        loads.append(pltpu.make_async_copy(v_hbm.at[rows], v_ref.at[rows], load.at[k]))
        loads[k].start()

    barrier = pltpu.get_barrier_semaphore()
    for k in range(1, 8):
        pl.semaphore_signal(barrier, inc=1, device_id=zto(k), device_id_type=MESH)
    for rel in NEAR[1:]:
        pl.semaphore_signal(barrier, inc=1, device_id=near(rel), device_id_type=MESH)

    for k in range(NK):
        loads[k].wait()
        for nb in range(8):
            block = v_ref[k * 128 : (k + 1) * 128, nb * 128 : (nb + 1) * 128]
            vt2[pl.ds(nb * 1024 + k, 128, stride=8), :] = block.T

    def gather_some(base, to, count, rows=pt):
        for u in range(count):
            rows[to + u] = vt[occ[base + u]] * vt[vir[base + u]]

    def gather(base, to):
        def some(i, carry):
            gather_some(base + i * 32, to + i * 32, 32)
            return carry

        lax.fori_loop(0, 4, some, 0)

    def weights(base):
        row = weight[pl.ds(pl.multiple_of(base, 128), 128)].reshape(1, 128)
        return jnp.broadcast_to(row, (128, 128)).T

    def cvec(k):
        return coulomb[k * 128 : (k + 1) * 128].reshape(1, 128)

    window = [256 * plane + 128 * mod(c + s, 2) for s in range(2)]
    for s in range(2):
        gather(window[s], 128 * s)

    def window_rows():
        for s in range(2):
            w = weights(window[s])
            for k in range(NK):
                x = pt2s[0][pl.ds(s * 1024 + k, 128, stride=8), :] * w * cvec(k)
                hi, lo = split(x)
                qh[s * 128 : (s + 1) * 128, k * 128 : (k + 1) * 128] = hi
                ql[s * 128 : (s + 1) * 128, k * 128 : (k + 1) * 128] = lo

    def band_rows():
        for k in range(NK):
            for m in range(16):
                two = [
                    vt2[pl.ds((32 * (2 * m + e) + 8 * plane) * 8 + k, 8, stride=8), :] for e in range(2)
                ]
                hi, lo = split(jnp.concatenate(two, axis=0) * cvec(k))
                nh[m * 16 : (m + 1) * 16, k * 128 : (k + 1) * 128] = hi
                nl[m * 16 : (m + 1) * 16, k * 128 : (k + 1) * 128] = lo

    core = {"rows_2": 1 - c}

    def to_partner(i):
        rows = pl.ds(pl.multiple_of(i * 256, 256), 256)
        return pltpu.make_async_remote_copy(
            src_ref=r_oth.at[rows], dst_ref=r_in.at[rows], send_sem=psend.at[i],
            recv_sem=precv.at[i], device_id=core, device_id_type=MESH,
        )

    def place(i):
        return [512 * (i % 3) + 256 * s + 128 * (i // 3) for s in range(2)]

    def rows_of(i, bases):
        for s in range(2):
            w = weights(bases[s])
            for k in range(NK):
                hi, lo = split(pt2s[(i + 1) % 2][pl.ds(s * 1024 + k, 128, stride=8), :] * w)
                ph[i, s * 128 : (s + 1) * 128, k * 128 : (k + 1) * 128] = hi
                pw[i, s * 128 : (s + 1) * 128, k * 128 : (k + 1) * 128] = lo

    def response_of(i):
        r = nt3(ph[i], pw[i], qh[...], ql[...])
        r_own[i * 256 : (i + 1) * 256, :] = r[:, 0:128]
        r_oth[i * 256 : (i + 1) * 256, :] = r[:, 128:256]

    def rpiece(k, ky):
        at = (ky * 8 + mod(z + k, 8)) * 48
        return r_own.at[pl.ds(pl.multiple_of(at, 8), 48)]

    sign = (-1, 1)
    fa = {}
    fb = {}
    fc = {}

    def start_sums(half):
        for i in range(3):
            to_partner(3 * half + i).wait()
        rows = slice(768 * half, 768 * half + 768)
        r_own[rows] += r_in[rows]
        for j in range(2):
            ky = 2 * half + j
            fa[half, j] = copy(rpiece(4 * sign[half], ky), za_in.at[half, j], zto(2 * sign[half]))
        for ky in (2 * half, 2 * half + 1):
            for d in range(2):
                fb[d, ky] = copy(rpiece(3 * sign[d], ky), zb_in.at[d, ky], zto(sign[d]))
        for ky in (2 * half, 2 * half + 1):
            for d in range(2):
                fc[d, ky] = copy(rpiece(sign[d], ky), zc_in.at[d, ky], zto(sign[d]))

    def coupling_pair(i):
        return pltpu.make_async_remote_copy(
            src_ref=x_all.at[i], dst_ref=x_in.at[i % 3], send_sem=xpsend.at[i % 3],
            recv_sem=xprecv.at[i % 3], device_id=core, device_id_type=MESH,
        )

    for i in range(8):
        if i == 2:
            pl.semaphore_wait(barrier, 38)
        if i < 6:
            for e in range(2):
                gather_some(place(i)[e], 128 * e, 128, pts[(i + 1) % 2])
        if i == 0:
            window_rows()
        if i == 1:
            band_rows()
        if 1 <= i < 7:
            rows_of(i - 1, place(i - 1))
        if i >= 2:
            n = i - 2
            response_of(n)
            x_all[n] = nt3(nh[...], nl[...], ph[n], pw[n])
            to_partner(n).start()

            @pl.when(c != n // 3)
            def _(n=n):
                coupling_pair(n).start()
        if i == 5:
            start_sums(0)
    start_sums(1)

    def yrows(k, start, size):
        return pl.ds(pl.multiple_of(mod(y + k, 4) * 64 + start, 8), size)

    def yterm(k, h, q):
        return x_all.at[3 * c + q, yrows(k, 32 * h, 32)]

    yl = {}
    ys = {}
    for q in range(3):
        coupling_pair(q).wait_recv()
        x_all[3 * c + q] += x_in[q]
        for d in range(2):
            yl[d, q] = copy(yterm(2, d, q), yin.at[d, q, 0], yto(sign[d]))
    for q in range(3):
        for d in range(2):
            ys[d, q] = copy(yterm(sign[d], 1 - d, q), yin.at[d, q, 1], yto(sign[d]))

    fr = {}
    for ky in range(4):
        for d in range(2):
            fb[d, ky].wait_recv()
            part = zb_in[d, ky] + rpiece(2 * sign[d], ky)[...]
            if ky // 2 == d:
                fa[d, ky % 2].wait_recv()
                part = part + za_in[d, ky % 2]
            zb_in[d, ky] = part
            fr[d, ky] = copy(zb_in.at[d, ky], zr_in.at[d, ky], zto(2 * sign[d]))
    for q in range(3):
        for d in range(2):
            yl[d, q].wait_recv()
            yin[d, q, 0] += yterm(sign[d], d, q)[...]
            yl[d, q] = copy(yin.at[d, q, 0], yin.at[d, q, 2], yto(sign[d]))

    for ky in range(4):
        part = rpiece(0, ky)[...]
        for d in range(2):
            fc[d, ky].wait_recv()
            fr[d, ky].wait_recv()
            part = part + (zc_in[d, ky] + zr_in[d, ky])
        rfin[ky] = part
    ry = [copy(rfin.at[mod(y + k, 4)], ry_in.at[k], yto(k)) for k in (2, 1, 3)]

    xz = []
    for q in range(3):
        for d in range(2):
            ys[d, q].wait_recv()
            yl[d, q].wait_recv()
        for h in range(2):
            xfin[q, 32 * h : 32 * h + 32] = (
                yterm(0, h, q)[...] + yin[h, q, 2] + yin[1 - h, q, 1]
            )
        for k in (4, 3, 5, 2, 6, 1, 7):
            rows = pl.ds(pl.multiple_of(mod(z + k, 8) * 8, 8), 8)
            xz.append(copy(xfin.at[q, rows], xz_in.at[k, q], zto(k)))

    for d in ry:
        d.wait_recv()
    rq[z] = (rfin[y] + (ry_in[1] + ry_in[2] + ry_in[3])) * (1.0 / NB)
    rz = [copy(rq.at[z], rq.at[z], zto(k)) for k in (4, 3, 5, 2, 6, 1, 7)]

    for d in xz:
        d.wait_recv()
    tile = xfin[:, pl.ds(pl.multiple_of(z * 8, 8), 8)]
    for k in range(1, 8):
        tile = tile + xz_in[k]
    chip = y * 8 + z
    row = lax.broadcasted_iota(jnp.int32, (3, 8, 256), 1)
    factor = jnp.zeros((3, 8, 256), F32)
    for i in range(8):
        factor = jnp.where(row == i, ftab[fidx[32 * chip + 8 * plane + i]], factor)
    tile = tile * factor * (1.0 / math.sqrt(NB))
    xt[0] = jnp.concatenate([tile[0], tile[1][:, 0:128]], axis=1)
    xt[1] = jnp.concatenate([tile[1][:, 128:256], tile[2]], axis=1)
    for j in range(4):
        yt[j] = tile[j // 2][:, 128 * (j % 2) : 128 * (j % 2) + 128]

    def quarter(i, rel, e):
        rg, rc, rl = rel
        to = {"grp": mod(g + rg, 2), "rows_2": mod(c + rc, 2), "cols": mod(cl + rl, 2)}
        to["rows_0"] = 2 * c + e
        return pltpu.make_async_remote_copy(
            src_ref=xt.at[e], dst_ref=xq.at[y, plane], send_sem=qsend.at[i],
            recv_sem=qrecv.at[y, plane], device_id=to, device_id_type=MESH,
        )

    quarters = [(rel, e) for e in range(2) for rel in [(0, 0, 0)] + RELS]
    for i, (rel, e) in enumerate(quarters):
        if rel == (0, 0, 0):

            @pl.when(y != 2 * c + e)
            def _(i=i, rel=rel, e=e):
                quarter(i, rel, e).start()

            @pl.when(y == 2 * c + e)
            def _(e=e):
                xq[y, plane] = xt[e]
        else:
            quarter(i, rel, e).start()
    yx = []
    for rg, rl in ((1, 1), (1, 0), (0, 1)):
        to = {"grp": mod(g + rg, 2), "cols": mod(cl + rl, 2)}
        yx.append(copy(yt.at[2 * to["grp"] + to["cols"]], y32.at[plane], to))
    y32[plane] = yt[plane]
    for d in yx:
        d.wait_recv()
    for j in range(4):
        yq[z, 8 * j : 8 * j + 8] = y32[j]
    yz = [copy(yq.at[z], yq.at[z], zto(k)) for k in (4, 3, 5, 2, 6, 1, 7)]

    for d in rz:
        d.wait_recv()
    for ys_ in range(4):
        for j in range(4):

            def arrived(ys_=ys_, j=j):
                pltpu.make_async_remote_copy(
                    src_ref=xt.at[0], dst_ref=xq.at[ys_, j], send_sem=qsend.at[0],
                    recv_sem=qrecv.at[ys_, j], device_id=core, device_id_type=MESH,
                ).wait_recv()

            own = (ys_ == y) & (j == plane) & (c == y // 2)
            pl.when(jnp.logical_not(own))(arrived)

    xh, xl = split(xq[...].reshape(128, 384))
    rh, rl_ = split(rq[...].reshape(384, 128))
    mbuf[...] = nn3(xh, xl, rh, rl_)
    my = [copy(mbuf, m_in.at[k], yto(k)) for k in (2, 1, 3)]
    for d in yz:
        d.wait_recv()
    yh, yw = split(yq[...].reshape(256, 128))
    for d in my:
        d.wait_recv()
    mh, ml = split(mbuf[...] + (m_in[1] + m_in[2] + m_in[3]))
    s = nt3(mh, ml, yh, yw)
    for i in range(16):
        sbuf[(i // 2) % 2, (i // 4) * 2 + i % 2] = s[8 * i : 8 * i + 8, :]
    dp = copy(sbuf.at[1 - c], s_pair, core)

    e = lax.rem(y, 2)

    def result(i, ry_, rl):
        to = {"grp": y // 2, "rows_0": mod(y + ry_, 4), "cols": mod(cl + rl, 2)}
        return pltpu.make_async_remote_copy(
            src_ref=sbuf.at[c, to["rows_0"] * 2 + to["cols"]], dst_ref=s_in.at[e, plane],
            send_sem=ssend.at[i], recv_sem=srecv.at[e, plane], device_id=to, device_id_type=MESH,
        )

    dp.wait_recv()
    sbuf[c] += s_pair[...]
    results = [(a, d) for a in (2, 1, 3, 0) for d in (1, 0)]
    for i, rel in enumerate(results):
        if rel == (0, 0):

            @pl.when(y // 2 != g)
            def _(i=i, rel=rel):
                result(i, *rel).start()

            @pl.when(y // 2 == g)
            def _():
                s_in[e, plane] = sbuf[c, y * 2 + cl]
        else:
            result(i, *rel).start()
    for e_ in range(2):
        for j in range(4):

            def landed(e_=e_, j=j):
                pltpu.make_async_remote_copy(
                    src_ref=sbuf.at[0, 0], dst_ref=s_in.at[e_, j], send_sem=ssend.at[0],
                    recv_sem=srecv.at[e_, j], device_id=core, device_id_type=MESH,
                ).wait_recv()

            own = (e_ == e) & (j == plane) & (y // 2 == g)
            pl.when(jnp.logical_not(own))(landed)
    for e_ in range(2):
        total = s_in[e_, 0] + s_in[e_, 1] + (s_in[e_, 2] + s_in[e_, 3])
        out_ref[:, 256 * e_ : 256 * e_ + 256] = total * (1.0 / math.sqrt(1024))

    for i, (rel, e_) in enumerate(quarters):
        if rel == (0, 0, 0):

            @pl.when(y != 2 * c + e_)
            def _(i=i, rel=rel, e_=e_):
                quarter(i, rel, e_).wait_send()
        else:
            quarter(i, rel, e_).wait_send()
    for i, rel in enumerate(results):
        if rel == (0, 0):

            @pl.when(y // 2 != g)
            def _(i=i, rel=rel):
                result(i, *rel).wait_send()
        else:
            result(i, *rel).wait_send()
    for t in range(3):
        coupling_pair(t).wait_send()
    for d in started:
        d.wait_send()


def per_device(band_vectors, coulomb, pair_weight, occ_index, vir_index, freq_index, freq_table):
    smem = pl.BlockSpec(memory_space=pltpu.SMEM)
    vmem = pl.BlockSpec(memory_space=pltpu.VMEM)
    return pl.pallas_call(
        window_kernel,
        out_shape=jax.ShapeDtypeStruct((8, 512), F32),
        in_specs=[smem, smem, smem, smem, vmem, vmem, pl.BlockSpec(memory_space=pl.ANY)],
        out_specs=vmem,
        scratch_shapes=[
            pltpu.VMEM((KB, 1024), F32),
            pltpu.VMEM((1024, 8, 128), F32),
            pltpu.VMEM((256, 8, 128), F32),
            pltpu.VMEM((256, 8, 128), F32),
            pltpu.VMEM((6, 256, KB), BF16),
            pltpu.VMEM((6, 256, KB), BF16),
            pltpu.VMEM((256, KB), BF16),
            pltpu.VMEM((256, KB), BF16),
            pltpu.VMEM((256, KB), BF16),
            pltpu.VMEM((256, KB), BF16),
            pltpu.VMEM((1536, 128), F32),
            pltpu.VMEM((1536, 128), F32),
            pltpu.VMEM((1536, 128), F32),
            pltpu.VMEM((6, 256, 256), F32),
            pltpu.VMEM((3, 256, 256), F32),
            pltpu.VMEM((2, 2, 48, 128), F32),
            pltpu.VMEM((2, 4, 48, 128), F32),
            pltpu.VMEM((2, 4, 48, 128), F32),
            pltpu.VMEM((2, 4, 48, 128), F32),
            pltpu.VMEM((2, 3, 3, 32, 256), F32),
            pltpu.VMEM((4, 48, 128), F32),
            pltpu.VMEM((3, 64, 256), F32),
            pltpu.VMEM((4, 48, 128), F32),
            pltpu.VMEM((8, 3, 8, 256), F32),
            pltpu.VMEM((8, 48, 128), F32),
            pltpu.VMEM((2, 8, 384), F32),
            pltpu.VMEM((4, 8, 128), F32),
            pltpu.VMEM((4, 4, 8, 384), F32),
            pltpu.VMEM((4, 8, 128), F32),
            pltpu.VMEM((8, 32, 128), F32),
            pltpu.VMEM((128, 128), F32),
            pltpu.VMEM((4, 128, 128), F32),
            pltpu.VMEM((2, 8, 8, 256), F32),
            pltpu.VMEM((8, 8, 256), F32),
            pltpu.VMEM((2, 4, 8, 256), F32),
            pltpu.SemaphoreType.DMA((NK,)),
            pltpu.SemaphoreType.DMA((6,)),
            pltpu.SemaphoreType.DMA((6,)),
            pltpu.SemaphoreType.DMA((3,)),
            pltpu.SemaphoreType.DMA((3,)),
            pltpu.SemaphoreType.DMA((16,)),
            pltpu.SemaphoreType.DMA((4, 4)),
            pltpu.SemaphoreType.DMA((8,)),
            pltpu.SemaphoreType.DMA((2, 4)),
            pltpu.SemaphoreType.DMA((112,)),
            pltpu.SemaphoreType.DMA((112,)),
        ],
        compiler_params=pltpu.CompilerParams(collective_id=0, has_side_effects=True),
        name="window",
    )(occ_index, vir_index, freq_index, freq_table, pair_weight, coulomb, band_vectors)


def solution(mesh):
    torus = Mesh(
        mesh.devices.reshape(mesh.shape["grp"], 4, 8, 2, mesh.shape["cols"]),
        ("grp", "rows_0", "rows_1", "rows_2", "cols"),
    )
    placed = (P(ROWS, None), P(ROWS), P(), P(), P(), P(), P())
    return jax.shard_map(
        per_device, mesh=torus, in_specs=placed, out_specs=P(ROWS_COLS, "grp"), check_vma=False
    )
```

```python
import math

import jax
import jax.numpy as jnp
from jax import lax
from jax.experimental import pallas as pl
from jax.experimental.pallas import tpu as pltpu
from jax.sharding import Mesh
from jax.sharding import PartitionSpec as P

NB = 49152
ROWS = ("rows_0", "rows_1", "rows_2")
ROWS_COLS = ("rows_0", "rows_1", "rows_2", "cols")
MESH = pl.DeviceIdType.MESH
F32 = jnp.float32
BF16 = jnp.bfloat16
KB = 768
NK = KB // 128
HALF = 768
RELS = [(a, b, d) for a in range(2) for b in range(2) for d in range(2)][1:]
NEAR = [(e, a, b, d) for e in range(4) for a in range(2) for b in range(2) for d in range(2)]


def split(x):
    hi = x.astype(BF16)
    return hi, (x - hi.astype(F32)).astype(BF16)


def nt(a, b):
    return lax.dot_general(a, b, (((1,), (1,)), ((), ())), preferred_element_type=F32)


def nn(a, b):
    return lax.dot_general(a, b, (((1,), (0,)), ((), ())), preferred_element_type=F32)


def nt3(ah, al, bh, bl):
    return nt(ah, bh) + nt(ah, bl) + nt(al, bh)


def nn3(ah, al, bh, bl):
    return nn(ah, bh) + nn(ah, bl) + nn(al, bh)


def mod(a, n):
    return lax.rem(a + n, n)


def window_kernel(
    occ_hbm, vir_hbm, fidx_hbm, ftab_hbm, weight_hbm, coulomb_hbm, v_hbm, out_ref,
    occ, vir, fidx, ftab, weight, coulomb, v_ref, vt, pt, qt, ph, pw, qh, ql, nh, nl,
    r_own, r_oth, r_in, x_all, x_in,
    za_in, zb_in, zc_in, zr_in, yin, rfin, xfin, ry_in, xz_in,
    rq, xt, yt, xq, y32, yq, mbuf, m_in, sbuf, s_pair, s_in,
    load, psend, precv, xpsend, xprecv, qsend, qrecv, ssend, srecv, send, recv,
):
    y = lax.axis_index("rows_0")
    z = lax.axis_index("rows_1")
    c = lax.axis_index("rows_2")
    g = lax.axis_index("grp")
    cl = lax.axis_index("cols")
    plane = 2 * g + cl
    started = []

    def copy(src, dst, to):
        i = len(started)
        d = pltpu.make_async_remote_copy(
            src_ref=src, dst_ref=dst, send_sem=send.at[i], recv_sem=recv.at[i],
            device_id=to, device_id_type=MESH,
        )
        d.start()
        started.append(d)
        return d

    def zto(k):
        return {"rows_1": mod(z + k, 8)}

    def yto(k):
        return {"rows_0": mod(y + k, 4)}

    def near(rel):
        ry, rg, rc, rl = rel
        return {
            "rows_0": mod(y + ry, 4), "grp": mod(g + rg, 2),
            "rows_2": mod(c + rc, 2), "cols": mod(cl + rl, 2),
        }

    vt2 = vt.reshape(8192, 128)
    pts = (pt, qt)
    pt2s = (pt.reshape(2048, 128), qt.reshape(2048, 128))
    loads = []
    for k in range(NK):
        rows = pl.ds(k * 128, 128)
        loads.append(pltpu.make_async_copy(v_hbm.at[rows], v_ref.at[rows], load.at[k]))
    smalls = (
        (occ_hbm, occ), (vir_hbm, vir), (weight_hbm, weight),
        (coulomb_hbm, coulomb), (fidx_hbm, fidx), (ftab_hbm, ftab),
    )
    for k, (src, dst) in enumerate(smalls):
        loads.append(pltpu.make_async_copy(src, dst, load.at[NK + k]))
    for d in loads:
        d.start()

    barrier = pltpu.get_barrier_semaphore()
    for k in range(1, 8):
        pl.semaphore_signal(barrier, inc=1, device_id=zto(k), device_id_type=MESH)
    for rel in NEAR[1:]:
        pl.semaphore_signal(barrier, inc=1, device_id=near(rel), device_id_type=MESH)

    for k in range(NK):
        loads[k].wait()
        for nb in range(8):
            block = v_ref[k * 128 : (k + 1) * 128, nb * 128 : (nb + 1) * 128]
            vt2[pl.ds(nb * 1024 + k, 128, stride=8), :] = block.T

    for d in loads[NK:]:
        d.wait()

    def gather_some(base, to, count, rows=pt):
        for u in range(count):
            rows[to + u] = vt[occ[base + u]] * vt[vir[base + u]]

    def gather(base, to):
        def some(i, carry):
            gather_some(base + i * 32, to + i * 32, 32)
            return carry

        lax.fori_loop(0, 4, some, 0)

    def weights(base):
        row = weight[pl.ds(pl.multiple_of(base, 128), 128)].reshape(1, 128)
        return jnp.broadcast_to(row, (128, 128)).T

    def cvec(k):
        return coulomb[k * 128 : (k + 1) * 128].reshape(1, 128)

    window = [256 * plane + 128 * mod(c + s, 2) for s in range(2)]
    for s in range(2):
        gather(window[s], 128 * s)

    def window_rows():
        for s in range(2):
            w = weights(window[s])
            for k in range(NK):
                x = pt2s[0][pl.ds(s * 1024 + k, 128, stride=8), :] * w * cvec(k)
                hi, lo = split(x)
                qh[s * 128 : (s + 1) * 128, k * 128 : (k + 1) * 128] = hi
                ql[s * 128 : (s + 1) * 128, k * 128 : (k + 1) * 128] = lo

    def band_rows():
        for k in range(NK):
            for m in range(16):
                two = [
                    vt2[pl.ds((32 * (2 * m + e) + 8 * plane) * 8 + k, 8, stride=8), :] for e in range(2)
                ]
                hi, lo = split(jnp.concatenate(two, axis=0) * cvec(k))
                nh[m * 16 : (m + 1) * 16, k * 128 : (k + 1) * 128] = hi
                nl[m * 16 : (m + 1) * 16, k * 128 : (k + 1) * 128] = lo

    core = {"rows_2": 1 - c}

    def to_partner(i):
        rows = pl.ds(pl.multiple_of(i * 256, 256), 256)
        return pltpu.make_async_remote_copy(
            src_ref=r_oth.at[rows], dst_ref=r_in.at[rows], send_sem=psend.at[i],
            recv_sem=precv.at[i], device_id=core, device_id_type=MESH,
        )

    def place(i):
        return [512 * (i % 3) + 256 * s + 128 * (i // 3) for s in range(2)]

    def rows_of(i, bases):
        for s in range(2):
            w = weights(bases[s])
            for k in range(NK):
                hi, lo = split(pt2s[(i + 1) % 2][pl.ds(s * 1024 + k, 128, stride=8), :] * w)
                ph[i, s * 128 : (s + 1) * 128, k * 128 : (k + 1) * 128] = hi
                pw[i, s * 128 : (s + 1) * 128, k * 128 : (k + 1) * 128] = lo

    def response_of(i):
        r = nt3(ph[i], pw[i], qh[...], ql[...])
        r_own[i * 256 : (i + 1) * 256, :] = r[:, 0:128]
        r_oth[i * 256 : (i + 1) * 256, :] = r[:, 128:256]

    def rpiece(k, ky):
        at = (ky * 8 + mod(z + k, 8)) * 48
        return r_own.at[pl.ds(pl.multiple_of(at, 8), 48)]

    sign = (-1, 1)
    fa = {}
    fb = {}
    fc = {}

    def start_sums(half):
        for i in range(3):
            to_partner(3 * half + i).wait()
        rows = slice(768 * half, 768 * half + 768)
        r_own[rows] += r_in[rows]
        for j in range(2):
            ky = 2 * half + j
            fa[half, j] = copy(rpiece(4 * sign[half], ky), za_in.at[half, j], zto(2 * sign[half]))
        for ky in (2 * half, 2 * half + 1):
            for d in range(2):
                fb[d, ky] = copy(rpiece(3 * sign[d], ky), zb_in.at[d, ky], zto(sign[d]))
        for ky in (2 * half, 2 * half + 1):
            for d in range(2):
                fc[d, ky] = copy(rpiece(sign[d], ky), zc_in.at[d, ky], zto(sign[d]))

    def coupling_pair(i):
        return pltpu.make_async_remote_copy(
            src_ref=x_all.at[i], dst_ref=x_in.at[i % 3], send_sem=xpsend.at[i % 3],
            recv_sem=xprecv.at[i % 3], device_id=core, device_id_type=MESH,
        )

    for i in range(8):
        if i == 2:
            pl.semaphore_wait(barrier, 38)
        if i < 6:
            for e in range(2):
                gather_some(place(i)[e], 128 * e, 128, pts[(i + 1) % 2])
        if i == 0:
            window_rows()
        if i == 1:
            band_rows()
        if 1 <= i < 7:
            rows_of(i - 1, place(i - 1))
        if i >= 2:
            n = i - 2
            response_of(n)
            x_all[n] = nt3(nh[...], nl[...], ph[n], pw[n])
            to_partner(n).start()

            @pl.when(c != n // 3)
            def _(n=n):
                coupling_pair(n).start()
        if i == 5:
            start_sums(0)
    start_sums(1)

    def yrows(k, start, size):
        return pl.ds(pl.multiple_of(mod(y + k, 4) * 64 + start, 8), size)

    def yterm(k, h, q):
        return x_all.at[3 * c + q, yrows(k, 32 * h, 32)]

    yl = {}
    ys = {}
    for q in range(3):
        coupling_pair(q).wait_recv()
        x_all[3 * c + q] += x_in[q]
        for d in range(2):
            yl[d, q] = copy(yterm(2, d, q), yin.at[d, q, 0], yto(sign[d]))
    for q in range(3):
        for d in range(2):
            ys[d, q] = copy(yterm(sign[d], 1 - d, q), yin.at[d, q, 1], yto(sign[d]))

    fr = {}
    xz = []

    def relay(ky):
        for d in range(2):
            fb[d, ky].wait_recv()
            part = zb_in[d, ky] + rpiece(2 * sign[d], ky)[...]
            if ky // 2 == d:
                fa[d, ky % 2].wait_recv()
                part = part + za_in[d, ky % 2]
            zb_in[d, ky] = part
            fr[d, ky] = copy(zb_in.at[d, ky], zr_in.at[d, ky], zto(2 * sign[d]))

    def pass_on(q):
        for d in range(2):
            yl[d, q].wait_recv()
            yin[d, q, 0] += yterm(sign[d], d, q)[...]
            yl[d, q] = copy(yin.at[d, q, 0], yin.at[d, q, 2], yto(sign[d]))

    def finish_piece(ky):
        part = rpiece(0, ky)[...]
        for d in range(2):
            fc[d, ky].wait_recv()
            fr[d, ky].wait_recv()
            part = part + (zc_in[d, ky] + zr_in[d, ky])
        rfin[ky] = part

    def finish_rows(q):
        for d in range(2):
            ys[d, q].wait_recv()
            yl[d, q].wait_recv()
        for h in range(2):
            xfin[q, 32 * h : 32 * h + 32] = (
                yterm(0, h, q)[...] + yin[h, q, 2] + yin[1 - h, q, 1]
            )
        for k in (4, 3, 5, 2, 6, 1, 7):
            rows = pl.ds(pl.multiple_of(mod(z + k, 8) * 8, 8), 8)
            xz.append(copy(xfin.at[q, rows], xz_in.at[k, q], zto(k)))

    relay(0)
    relay(1)
    pass_on(0)
    relay(2)
    pass_on(1)
    relay(3)
    pass_on(2)
    finish_piece(0)
    finish_piece(1)
    finish_rows(0)
    finish_rows(1)
    finish_piece(2)
    finish_rows(2)
    finish_piece(3)
    ry = [copy(rfin.at[mod(y + k, 4)], ry_in.at[k], yto(k)) for k in (2, 1, 3)]

    for d in ry:
        d.wait_recv()
    rq[z] = (rfin[y] + (ry_in[1] + ry_in[2] + ry_in[3])) * (1.0 / NB)
    rz = [copy(rq.at[z], rq.at[z], zto(k)) for k in (4, 3, 5, 2, 6, 1, 7)]

    for d in xz:
        d.wait_recv()
    tile = xfin[:, pl.ds(pl.multiple_of(z * 8, 8), 8)]
    for k in range(1, 8):
        tile = tile + xz_in[k]
    chip = y * 8 + z
    row = lax.broadcasted_iota(jnp.int32, (3, 8, 256), 1)
    factor = jnp.zeros((3, 8, 256), F32)
    for i in range(8):
        factor = jnp.where(row == i, ftab[fidx[32 * chip + 8 * plane + i]], factor)
    tile = tile * factor * (1.0 / math.sqrt(NB))
    xt[0] = jnp.concatenate([tile[0], tile[1][:, 0:128]], axis=1)
    xt[1] = jnp.concatenate([tile[1][:, 128:256], tile[2]], axis=1)
    for j in range(4):
        yt[j] = tile[j // 2][:, 128 * (j % 2) : 128 * (j % 2) + 128]

    def quarter(i, rel, e):
        rg, rc, rl = rel
        to = {"grp": mod(g + rg, 2), "rows_2": mod(c + rc, 2), "cols": mod(cl + rl, 2)}
        to["rows_0"] = 2 * c + e
        return pltpu.make_async_remote_copy(
            src_ref=xt.at[e], dst_ref=xq.at[y, plane], send_sem=qsend.at[i],
            recv_sem=qrecv.at[y, plane], device_id=to, device_id_type=MESH,
        )

    quarters = [(rel, e) for e in range(2) for rel in [(0, 0, 0)] + RELS]
    for i, (rel, e) in enumerate(quarters):
        if rel == (0, 0, 0):

            @pl.when(y != 2 * c + e)
            def _(i=i, rel=rel, e=e):
                quarter(i, rel, e).start()

            @pl.when(y == 2 * c + e)
            def _(e=e):
                xq[y, plane] = xt[e]
        else:
            quarter(i, rel, e).start()
    yx = []
    for rg, rl in ((1, 1), (1, 0), (0, 1)):
        to = {"grp": mod(g + rg, 2), "cols": mod(cl + rl, 2)}
        yx.append(copy(yt.at[2 * to["grp"] + to["cols"]], y32.at[plane], to))
    y32[plane] = yt[plane]
    for d in yx:
        d.wait_recv()
    for j in range(4):
        yq[z, 8 * j : 8 * j + 8] = y32[j]
    yz = [copy(yq.at[z], yq.at[z], zto(k)) for k in (4, 3, 5, 2, 6, 1, 7)]

    for d in rz:
        d.wait_recv()
    for ys_ in range(4):
        for j in range(4):

            def arrived(ys_=ys_, j=j):
                pltpu.make_async_remote_copy(
                    src_ref=xt.at[0], dst_ref=xq.at[ys_, j], send_sem=qsend.at[0],
                    recv_sem=qrecv.at[ys_, j], device_id=core, device_id_type=MESH,
                ).wait_recv()

            own = (ys_ == y) & (j == plane) & (c == y // 2)
            pl.when(jnp.logical_not(own))(arrived)

    xh, xl = split(xq[...].reshape(128, 384))
    rh, rl_ = split(rq[...].reshape(384, 128))
    mbuf[...] = nn3(xh, xl, rh, rl_)
    my = [copy(mbuf, m_in.at[k], yto(k)) for k in (2, 1, 3)]
    for d in yz:
        d.wait_recv()
    yh, yw = split(yq[...].reshape(256, 128))
    for d in my:
        d.wait_recv()
    mh, ml = split(mbuf[...] + (m_in[1] + m_in[2] + m_in[3]))
    s = nt3(mh, ml, yh, yw)
    for i in range(16):
        sbuf[(i // 2) % 2, (i // 4) * 2 + i % 2] = s[8 * i : 8 * i + 8, :]
    dp = copy(sbuf.at[1 - c], s_pair, core)

    e = lax.rem(y, 2)

    def result(i, ry_, rl):
        to = {"grp": y // 2, "rows_0": mod(y + ry_, 4), "cols": mod(cl + rl, 2)}
        return pltpu.make_async_remote_copy(
            src_ref=sbuf.at[c, to["rows_0"] * 2 + to["cols"]], dst_ref=s_in.at[e, plane],
            send_sem=ssend.at[i], recv_sem=srecv.at[e, plane], device_id=to, device_id_type=MESH,
        )

    dp.wait_recv()
    sbuf[c] += s_pair[...]
    results = [(a, d) for a in (2, 1, 3, 0) for d in (1, 0)]
    for i, rel in enumerate(results):
        if rel == (0, 0):

            @pl.when(y // 2 != g)
            def _(i=i, rel=rel):
                result(i, *rel).start()

            @pl.when(y // 2 == g)
            def _():
                s_in[e, plane] = sbuf[c, y * 2 + cl]
        else:
            result(i, *rel).start()
    for e_ in range(2):
        for j in range(4):

            def landed(e_=e_, j=j):
                pltpu.make_async_remote_copy(
                    src_ref=sbuf.at[0, 0], dst_ref=s_in.at[e_, j], send_sem=ssend.at[0],
                    recv_sem=srecv.at[e_, j], device_id=core, device_id_type=MESH,
                ).wait_recv()

            own = (e_ == e) & (j == plane) & (y // 2 == g)
            pl.when(jnp.logical_not(own))(landed)
    for e_ in range(2):
        total = s_in[e_, 0] + s_in[e_, 1] + (s_in[e_, 2] + s_in[e_, 3])
        out_ref[:, 256 * e_ : 256 * e_ + 256] = total * (1.0 / math.sqrt(1024))

    for i, (rel, e_) in enumerate(quarters):
        if rel == (0, 0, 0):

            @pl.when(y != 2 * c + e_)
            def _(i=i, rel=rel, e_=e_):
                quarter(i, rel, e_).wait_send()
        else:
            quarter(i, rel, e_).wait_send()
    for i, rel in enumerate(results):
        if rel == (0, 0):

            @pl.when(y // 2 != g)
            def _(i=i, rel=rel):
                result(i, *rel).wait_send()
        else:
            result(i, *rel).wait_send()
    for t in range(3):
        coupling_pair(t).wait_send()
    for d in started:
        d.wait_send()


def per_device(band_vectors, coulomb, pair_weight, occ_index, vir_index, freq_index, freq_table):
    vmem = pl.BlockSpec(memory_space=pltpu.VMEM)
    return pl.pallas_call(
        window_kernel,
        out_shape=jax.ShapeDtypeStruct((8, 512), F32),
        in_specs=[pl.BlockSpec(memory_space=pl.ANY)] * 7,
        out_specs=vmem,
        scratch_shapes=[
            pltpu.SMEM((1536,), jnp.int32),
            pltpu.SMEM((1536,), jnp.int32),
            pltpu.SMEM((1024,), jnp.int32),
            pltpu.SMEM((16,), F32),
            pltpu.VMEM((1536,), F32),
            pltpu.VMEM((KB,), F32),
            pltpu.VMEM((KB, 1024), F32),
            pltpu.VMEM((1024, 8, 128), F32),
            pltpu.VMEM((256, 8, 128), F32),
            pltpu.VMEM((256, 8, 128), F32),
            pltpu.VMEM((6, 256, KB), BF16),
            pltpu.VMEM((6, 256, KB), BF16),
            pltpu.VMEM((256, KB), BF16),
            pltpu.VMEM((256, KB), BF16),
            pltpu.VMEM((256, KB), BF16),
            pltpu.VMEM((256, KB), BF16),
            pltpu.VMEM((1536, 128), F32),
            pltpu.VMEM((1536, 128), F32),
            pltpu.VMEM((1536, 128), F32),
            pltpu.VMEM((6, 256, 256), F32),
            pltpu.VMEM((3, 256, 256), F32),
            pltpu.VMEM((2, 2, 48, 128), F32),
            pltpu.VMEM((2, 4, 48, 128), F32),
            pltpu.VMEM((2, 4, 48, 128), F32),
            pltpu.VMEM((2, 4, 48, 128), F32),
            pltpu.VMEM((2, 3, 3, 32, 256), F32),
            pltpu.VMEM((4, 48, 128), F32),
            pltpu.VMEM((3, 64, 256), F32),
            pltpu.VMEM((4, 48, 128), F32),
            pltpu.VMEM((8, 3, 8, 256), F32),
            pltpu.VMEM((8, 48, 128), F32),
            pltpu.VMEM((2, 8, 384), F32),
            pltpu.VMEM((4, 8, 128), F32),
            pltpu.VMEM((4, 4, 8, 384), F32),
            pltpu.VMEM((4, 8, 128), F32),
            pltpu.VMEM((8, 32, 128), F32),
            pltpu.VMEM((128, 128), F32),
            pltpu.VMEM((4, 128, 128), F32),
            pltpu.VMEM((2, 8, 8, 256), F32),
            pltpu.VMEM((8, 8, 256), F32),
            pltpu.VMEM((2, 4, 8, 256), F32),
            pltpu.SemaphoreType.DMA((NK + 6,)),
            pltpu.SemaphoreType.DMA((6,)),
            pltpu.SemaphoreType.DMA((6,)),
            pltpu.SemaphoreType.DMA((3,)),
            pltpu.SemaphoreType.DMA((3,)),
            pltpu.SemaphoreType.DMA((16,)),
            pltpu.SemaphoreType.DMA((4, 4)),
            pltpu.SemaphoreType.DMA((8,)),
            pltpu.SemaphoreType.DMA((2, 4)),
            pltpu.SemaphoreType.DMA((112,)),
            pltpu.SemaphoreType.DMA((112,)),
        ],
        compiler_params=pltpu.CompilerParams(collective_id=0, has_side_effects=True),
        name="window",
    )(occ_index, vir_index, freq_index, freq_table, pair_weight, coulomb, band_vectors)


def solution(mesh):
    torus = Mesh(
        mesh.devices.reshape(mesh.shape["grp"], 4, 8, 2, mesh.shape["cols"]),
        ("grp", "rows_0", "rows_1", "rows_2", "cols"),
    )
    placed = (P(ROWS, None), P(ROWS), P(), P(), P(), P(), P())
    return jax.shard_map(
        per_device, mesh=torus, in_specs=placed, out_specs=P(ROWS_COLS, "grp"), check_vma=False
    )
```

```python
import math

import jax
import jax.numpy as jnp
from jax import lax
from jax.experimental import pallas as pl
from jax.experimental.pallas import tpu as pltpu
from jax.sharding import Mesh
from jax.sharding import PartitionSpec as P

NB = 49152
ROWS = ("rows_0", "rows_1", "rows_2")
ROWS_COLS = ("rows_0", "rows_1", "rows_2", "cols")
MESH = pl.DeviceIdType.MESH
F32 = jnp.float32
BF16 = jnp.bfloat16
KB = 768
NK = KB // 128
HALF = 768
RELS = [(a, b, d) for a in range(2) for b in range(2) for d in range(2)][1:]
NEAR = [(e, a, b, d) for e in range(4) for a in range(2) for b in range(2) for d in range(2)]


def split(x):
    hi = x.astype(BF16)
    return hi, (x - hi.astype(F32)).astype(BF16)


def nt(a, b):
    return lax.dot_general(a, b, (((1,), (1,)), ((), ())), preferred_element_type=F32)


def nn(a, b):
    return lax.dot_general(a, b, (((1,), (0,)), ((), ())), preferred_element_type=F32)


def nt3(ah, al, bh, bl):
    return nt(ah, bh) + nt(ah, bl) + nt(al, bh)


def nn3(ah, al, bh, bl):
    return nn(ah, bh) + nn(ah, bl) + nn(al, bh)


def mod(a, n):
    return lax.rem(a + n, n)


def window_kernel(
    occ_hbm, vir_hbm, fidx_hbm, ftab_hbm, weight_hbm, coulomb_hbm, v_hbm, out_ref,
    occ, vir, fidx, ftab, weight, coulomb, v_ref, vt, pt, qt, ph, pw, qh, ql, nh, nl,
    r_own, r_oth, r_in, x_all, x_in,
    za_in, zb_in, zc_in, zr_in, yin, rfin, xfin, ry_in, xz_in,
    rq, xt, yt, xq, y32, yq, mbuf, m_in, sbuf, s_pair, s_in,
    load, psend, precv, xpsend, xprecv, qsend, qrecv, ssend, srecv, send, recv,
):
    y = lax.axis_index("rows_0")
    z = lax.axis_index("rows_1")
    c = lax.axis_index("rows_2")
    g = lax.axis_index("grp")
    cl = lax.axis_index("cols")
    plane = 2 * g + cl
    started = []

    def copy(src, dst, to):
        i = len(started)
        d = pltpu.make_async_remote_copy(
            src_ref=src, dst_ref=dst, send_sem=send.at[i], recv_sem=recv.at[i],
            device_id=to, device_id_type=MESH,
        )
        d.start()
        started.append(d)
        return d

    def zto(k):
        return {"rows_1": mod(z + k, 8)}

    def yto(k):
        return {"rows_0": mod(y + k, 4)}

    def near(rel):
        ry, rg, rc, rl = rel
        return {
            "rows_0": mod(y + ry, 4), "grp": mod(g + rg, 2),
            "rows_2": mod(c + rc, 2), "cols": mod(cl + rl, 2),
        }

    vt2 = vt.reshape(8192, 128)
    pts = (pt, qt)
    pt2s = (pt.reshape(2048, 128), qt.reshape(2048, 128))
    loads = []
    for k in range(NK):
        rows = pl.ds(k * 128, 128)
        loads.append(pltpu.make_async_copy(v_hbm.at[rows], v_ref.at[rows], load.at[k]))
    smalls = (
        (occ_hbm, occ), (vir_hbm, vir), (weight_hbm, weight),
        (coulomb_hbm, coulomb), (fidx_hbm, fidx), (ftab_hbm, ftab),
    )
    for k, (src, dst) in enumerate(smalls):
        loads.append(pltpu.make_async_copy(src, dst, load.at[NK + k]))
    for d in loads:
        d.start()

    barrier = pltpu.get_barrier_semaphore()
    for k in range(1, 8):
        pl.semaphore_signal(barrier, inc=1, device_id=zto(k), device_id_type=MESH)
    for rel in NEAR[1:]:
        pl.semaphore_signal(barrier, inc=1, device_id=near(rel), device_id_type=MESH)

    for k in range(NK):
        loads[k].wait()
        for nb in range(8):
            block = v_ref[k * 128 : (k + 1) * 128, nb * 128 : (nb + 1) * 128]
            vt2[pl.ds(nb * 1024 + k, 128, stride=8), :] = block.T

    for d in loads[NK:]:
        d.wait()

    def gather_some(base, to, count, rows=pt):
        for u in range(count):
            rows[to + u] = vt[occ[base + u]] * vt[vir[base + u]]

    def weights(base):
        row = weight[pl.ds(pl.multiple_of(base, 128), 128)].reshape(1, 128)
        return jnp.broadcast_to(row, (128, 128)).T

    def cvec(k):
        return coulomb[k * 128 : (k + 1) * 128].reshape(1, 128)

    window = [256 * plane + 128 * mod(c + s, 2) for s in range(2)]

    def window_rows():
        for s in range(2):
            w = weights(window[s])
            for k in range(NK):
                x = pt2s[1][pl.ds(s * 1024 + k, 128, stride=8), :] * w * cvec(k)
                hi, lo = split(x)
                qh[s * 128 : (s + 1) * 128, k * 128 : (k + 1) * 128] = hi
                ql[s * 128 : (s + 1) * 128, k * 128 : (k + 1) * 128] = lo

    def band_rows():
        for k in range(NK):
            for m in range(16):
                two = [
                    vt2[pl.ds((32 * (2 * m + e) + 8 * plane) * 8 + k, 8, stride=8), :] for e in range(2)
                ]
                hi, lo = split(jnp.concatenate(two, axis=0) * cvec(k))
                nh[m * 16 : (m + 1) * 16, k * 128 : (k + 1) * 128] = hi
                nl[m * 16 : (m + 1) * 16, k * 128 : (k + 1) * 128] = lo

    core = {"rows_2": 1 - c}

    def to_partner(i):
        rows = pl.ds(pl.multiple_of(i * 256, 256), 256)
        return pltpu.make_async_remote_copy(
            src_ref=r_oth.at[rows], dst_ref=r_in.at[rows], send_sem=psend.at[i],
            recv_sem=precv.at[i], device_id=core, device_id_type=MESH,
        )

    def place(i):
        return [512 * (i % 3) + 256 * s + 128 * (i // 3) for s in range(2)]

    def buffer_of(i):
        return 0 if i == 0 else (i + 1) % 2

    def rows_of(i, bases):
        for s in range(2):
            w = weights(bases[s])
            for k in range(NK):
                hi, lo = split(pt2s[buffer_of(i)][pl.ds(s * 1024 + k, 128, stride=8), :] * w)
                ph[i, s * 128 : (s + 1) * 128, k * 128 : (k + 1) * 128] = hi
                pw[i, s * 128 : (s + 1) * 128, k * 128 : (k + 1) * 128] = lo

    def response_of(i):
        r = nt3(ph[i], pw[i], qh[...], ql[...])
        r_own[i * 256 : (i + 1) * 256, :] = r[:, 0:128]
        r_oth[i * 256 : (i + 1) * 256, :] = r[:, 128:256]

    def rpiece(k, ky):
        at = (ky * 8 + mod(z + k, 8)) * 48
        return r_own.at[pl.ds(pl.multiple_of(at, 8), 48)]

    sign = (-1, 1)
    fa = {}
    fb = {}
    fc = {}

    def start_sum(ky):
        for i in ((0, 1), (2,), (3, 4), (5,))[ky]:
            to_partner(i).wait()
        rows = slice(384 * ky, 384 * ky + 384)
        r_own[rows] += r_in[rows]
        n, j = ky // 2, ky % 2
        fa[n, j] = copy(rpiece(4 * sign[n], ky), za_in.at[n, j], zto(2 * sign[n]))
        for d in range(2):
            fb[d, ky] = copy(rpiece(3 * sign[d], ky), zb_in.at[d, ky], zto(sign[d]))
        for d in range(2):
            fc[d, ky] = copy(rpiece(sign[d], ky), zc_in.at[d, ky], zto(sign[d]))

    def coupling_pair(i):
        return pltpu.make_async_remote_copy(
            src_ref=x_all.at[i], dst_ref=x_in.at[i % 3], send_sem=xpsend.at[i % 3],
            recv_sem=xprecv.at[i % 3], device_id=core, device_id_type=MESH,
        )

    def gather_block(i):
        for e in range(2):
            gather_some(place(i)[e], 128 * e, 128, pts[buffer_of(i)])

    def coupling_of(n):
        x_all[n] = nt3(nh[...], nl[...], ph[n], pw[n])

    def send_coupling(n):
        @pl.when(c != n // 3)
        def _():
            coupling_pair(n).start()

    gather_block(0)
    band_rows()
    for e in range(2):
        gather_some(window[e], 128 * e, 128, pts[1])
    rows_of(0, place(0))
    gather_block(1)
    window_rows()
    coupling_of(0)
    pl.semaphore_wait(barrier, 38)
    send_coupling(0)
    gather_block(2)
    rows_of(1, place(1))
    response_of(0)
    to_partner(0).start()
    for n in range(1, 5):
        if n + 2 < 6:
            gather_block(n + 2)
        rows_of(n + 1, place(n + 1))
        response_of(n)
        coupling_of(n)
        to_partner(n).start()
        send_coupling(n)
        if n in (2, 3):
            start_sum(n - 2)
    response_of(5)
    to_partner(5).start()
    start_sum(2)
    coupling_of(5)
    send_coupling(5)
    start_sum(3)

    def yrows(k, start, size):
        return pl.ds(pl.multiple_of(mod(y + k, 4) * 64 + start, 8), size)

    def yterm(k, h, q):
        return x_all.at[3 * c + q, yrows(k, 32 * h, 32)]

    yl = {}
    ys = {}
    for q in range(3):
        coupling_pair(q).wait_recv()
        x_all[3 * c + q] += x_in[q]
        for d in range(2):
            yl[d, q] = copy(yterm(2, d, q), yin.at[d, q, 0], yto(sign[d]))
    for q in range(3):
        for d in range(2):
            ys[d, q] = copy(yterm(sign[d], 1 - d, q), yin.at[d, q, 1], yto(sign[d]))

    fr = {}
    xz = []

    def relay(ky):
        for d in range(2):
            fb[d, ky].wait_recv()
            part = zb_in[d, ky] + rpiece(2 * sign[d], ky)[...]
            if ky // 2 == d:
                fa[d, ky % 2].wait_recv()
                part = part + za_in[d, ky % 2]
            zb_in[d, ky] = part
            fr[d, ky] = copy(zb_in.at[d, ky], zr_in.at[d, ky], zto(2 * sign[d]))

    def pass_on(q):
        for d in range(2):
            yl[d, q].wait_recv()
            yin[d, q, 0] += yterm(sign[d], d, q)[...]
            yl[d, q] = copy(yin.at[d, q, 0], yin.at[d, q, 2], yto(sign[d]))

    def finish_piece(ky):
        part = rpiece(0, ky)[...]
        for d in range(2):
            fc[d, ky].wait_recv()
            fr[d, ky].wait_recv()
            part = part + (zc_in[d, ky] + zr_in[d, ky])
        rfin[ky] = part

    def finish_rows(q):
        for d in range(2):
            ys[d, q].wait_recv()
            yl[d, q].wait_recv()
        for h in range(2):
            xfin[q, 32 * h : 32 * h + 32] = (
                yterm(0, h, q)[...] + yin[h, q, 2] + yin[1 - h, q, 1]
            )
        for k in (4, 3, 5, 2, 6, 1, 7):
            rows = pl.ds(pl.multiple_of(mod(z + k, 8) * 8, 8), 8)
            xz.append(copy(xfin.at[q, rows], xz_in.at[k, q], zto(k)))

    relay(0)
    relay(1)
    pass_on(0)
    relay(2)
    pass_on(1)
    relay(3)
    pass_on(2)
    finish_piece(0)
    finish_piece(1)
    finish_rows(0)
    finish_rows(1)
    finish_piece(2)
    finish_rows(2)
    finish_piece(3)
    ry = [copy(rfin.at[mod(y + k, 4)], ry_in.at[k], yto(k)) for k in (2, 1, 3)]

    for d in ry:
        d.wait_recv()
    rq[z] = (rfin[y] + (ry_in[1] + ry_in[2] + ry_in[3])) * (1.0 / NB)
    rz = [copy(rq.at[z], rq.at[z], zto(k)) for k in (4, 3, 5, 2, 6, 1, 7)]

    for d in xz:
        d.wait_recv()
    tile = xfin[:, pl.ds(pl.multiple_of(z * 8, 8), 8)]
    for k in range(1, 8):
        tile = tile + xz_in[k]
    chip = y * 8 + z
    row = lax.broadcasted_iota(jnp.int32, (3, 8, 256), 1)
    factor = jnp.zeros((3, 8, 256), F32)
    for i in range(8):
        factor = jnp.where(row == i, ftab[fidx[32 * chip + 8 * plane + i]], factor)
    tile = tile * factor * (1.0 / math.sqrt(NB))
    xt[0] = jnp.concatenate([tile[0], tile[1][:, 0:128]], axis=1)
    xt[1] = jnp.concatenate([tile[1][:, 128:256], tile[2]], axis=1)
    for j in range(4):
        yt[j] = tile[j // 2][:, 128 * (j % 2) : 128 * (j % 2) + 128]

    def quarter(i, rel, e):
        rg, rc, rl = rel
        to = {"grp": mod(g + rg, 2), "rows_2": mod(c + rc, 2), "cols": mod(cl + rl, 2)}
        to["rows_0"] = 2 * c + e
        return pltpu.make_async_remote_copy(
            src_ref=xt.at[e], dst_ref=xq.at[y, plane], send_sem=qsend.at[i],
            recv_sem=qrecv.at[y, plane], device_id=to, device_id_type=MESH,
        )

    quarters = [(rel, e) for e in range(2) for rel in [(0, 0, 0)] + RELS]
    for i, (rel, e) in enumerate(quarters):
        if rel == (0, 0, 0):

            @pl.when(y != 2 * c + e)
            def _(i=i, rel=rel, e=e):
                quarter(i, rel, e).start()

            @pl.when(y == 2 * c + e)
            def _(e=e):
                xq[y, plane] = xt[e]
        else:
            quarter(i, rel, e).start()
    yx = []
    for rg, rl in ((1, 1), (1, 0), (0, 1)):
        to = {"grp": mod(g + rg, 2), "cols": mod(cl + rl, 2)}
        yx.append(copy(yt.at[2 * to["grp"] + to["cols"]], y32.at[plane], to))
    y32[plane] = yt[plane]
    for d in yx:
        d.wait_recv()
    for j in range(4):
        yq[z, 8 * j : 8 * j + 8] = y32[j]
    yz = [copy(yq.at[z], yq.at[z], zto(k)) for k in (4, 3, 5, 2, 6, 1, 7)]

    for d in rz:
        d.wait_recv()
    for ys_ in range(4):
        for j in range(4):

            def arrived(ys_=ys_, j=j):
                pltpu.make_async_remote_copy(
                    src_ref=xt.at[0], dst_ref=xq.at[ys_, j], send_sem=qsend.at[0],
                    recv_sem=qrecv.at[ys_, j], device_id=core, device_id_type=MESH,
                ).wait_recv()

            own = (ys_ == y) & (j == plane) & (c == y // 2)
            pl.when(jnp.logical_not(own))(arrived)

    xh, xl = split(xq[...].reshape(128, 384))
    rh, rl_ = split(rq[...].reshape(384, 128))
    mbuf[...] = nn3(xh, xl, rh, rl_)
    my = [copy(mbuf, m_in.at[k], yto(k)) for k in (2, 1, 3)]
    for d in yz:
        d.wait_recv()
    yh, yw = split(yq[...].reshape(256, 128))
    for d in my:
        d.wait_recv()
    mh, ml = split(mbuf[...] + (m_in[1] + m_in[2] + m_in[3]))
    s = nt3(mh, ml, yh, yw)
    for i in range(16):
        sbuf[(i // 2) % 2, (i // 4) * 2 + i % 2] = s[8 * i : 8 * i + 8, :]
    dp = copy(sbuf.at[1 - c], s_pair, core)

    e = lax.rem(y, 2)

    def result(i, ry_, rl):
        to = {"grp": y // 2, "rows_0": mod(y + ry_, 4), "cols": mod(cl + rl, 2)}
        return pltpu.make_async_remote_copy(
            src_ref=sbuf.at[c, to["rows_0"] * 2 + to["cols"]], dst_ref=s_in.at[e, plane],
            send_sem=ssend.at[i], recv_sem=srecv.at[e, plane], device_id=to, device_id_type=MESH,
        )

    dp.wait_recv()
    sbuf[c] += s_pair[...]
    results = [(a, d) for a in (2, 1, 3, 0) for d in (1, 0)]
    for i, rel in enumerate(results):
        if rel == (0, 0):

            @pl.when(y // 2 != g)
            def _(i=i, rel=rel):
                result(i, *rel).start()

            @pl.when(y // 2 == g)
            def _():
                s_in[e, plane] = sbuf[c, y * 2 + cl]
        else:
            result(i, *rel).start()
    for e_ in range(2):
        for j in range(4):

            def landed(e_=e_, j=j):
                pltpu.make_async_remote_copy(
                    src_ref=sbuf.at[0, 0], dst_ref=s_in.at[e_, j], send_sem=ssend.at[0],
                    recv_sem=srecv.at[e_, j], device_id=core, device_id_type=MESH,
                ).wait_recv()

            own = (e_ == e) & (j == plane) & (y // 2 == g)
            pl.when(jnp.logical_not(own))(landed)
    for e_ in range(2):
        total = s_in[e_, 0] + s_in[e_, 1] + (s_in[e_, 2] + s_in[e_, 3])
        out_ref[:, 256 * e_ : 256 * e_ + 256] = total * (1.0 / math.sqrt(1024))

    for i, (rel, e_) in enumerate(quarters):
        if rel == (0, 0, 0):

            @pl.when(y != 2 * c + e_)
            def _(i=i, rel=rel, e_=e_):
                quarter(i, rel, e_).wait_send()
        else:
            quarter(i, rel, e_).wait_send()
    for i, rel in enumerate(results):
        if rel == (0, 0):

            @pl.when(y // 2 != g)
            def _(i=i, rel=rel):
                result(i, *rel).wait_send()
        else:
            result(i, *rel).wait_send()
    for t in range(3):
        coupling_pair(t).wait_send()
    for d in started:
        d.wait_send()


def per_device(band_vectors, coulomb, pair_weight, occ_index, vir_index, freq_index, freq_table):
    vmem = pl.BlockSpec(memory_space=pltpu.VMEM)
    return pl.pallas_call(
        window_kernel,
        out_shape=jax.ShapeDtypeStruct((8, 512), F32),
        in_specs=[pl.BlockSpec(memory_space=pl.ANY)] * 7,
        out_specs=vmem,
        scratch_shapes=[
            pltpu.SMEM((1536,), jnp.int32),
            pltpu.SMEM((1536,), jnp.int32),
            pltpu.SMEM((1024,), jnp.int32),
            pltpu.SMEM((16,), F32),
            pltpu.VMEM((1536,), F32),
            pltpu.VMEM((KB,), F32),
            pltpu.VMEM((KB, 1024), F32),
            pltpu.VMEM((1024, 8, 128), F32),
            pltpu.VMEM((256, 8, 128), F32),
            pltpu.VMEM((256, 8, 128), F32),
            pltpu.VMEM((6, 256, KB), BF16),
            pltpu.VMEM((6, 256, KB), BF16),
            pltpu.VMEM((256, KB), BF16),
            pltpu.VMEM((256, KB), BF16),
            pltpu.VMEM((256, KB), BF16),
            pltpu.VMEM((256, KB), BF16),
            pltpu.VMEM((1536, 128), F32),
            pltpu.VMEM((1536, 128), F32),
            pltpu.VMEM((1536, 128), F32),
            pltpu.VMEM((6, 256, 256), F32),
            pltpu.VMEM((3, 256, 256), F32),
            pltpu.VMEM((2, 2, 48, 128), F32),
            pltpu.VMEM((2, 4, 48, 128), F32),
            pltpu.VMEM((2, 4, 48, 128), F32),
            pltpu.VMEM((2, 4, 48, 128), F32),
            pltpu.VMEM((2, 3, 3, 32, 256), F32),
            pltpu.VMEM((4, 48, 128), F32),
            pltpu.VMEM((3, 64, 256), F32),
            pltpu.VMEM((4, 48, 128), F32),
            pltpu.VMEM((8, 3, 8, 256), F32),
            pltpu.VMEM((8, 48, 128), F32),
            pltpu.VMEM((2, 8, 384), F32),
            pltpu.VMEM((4, 8, 128), F32),
            pltpu.VMEM((4, 4, 8, 384), F32),
            pltpu.VMEM((4, 8, 128), F32),
            pltpu.VMEM((8, 32, 128), F32),
            pltpu.VMEM((128, 128), F32),
            pltpu.VMEM((4, 128, 128), F32),
            pltpu.VMEM((2, 8, 8, 256), F32),
            pltpu.VMEM((8, 8, 256), F32),
            pltpu.VMEM((2, 4, 8, 256), F32),
            pltpu.SemaphoreType.DMA((NK + 6,)),
            pltpu.SemaphoreType.DMA((6,)),
            pltpu.SemaphoreType.DMA((6,)),
            pltpu.SemaphoreType.DMA((3,)),
            pltpu.SemaphoreType.DMA((3,)),
            pltpu.SemaphoreType.DMA((16,)),
            pltpu.SemaphoreType.DMA((4, 4)),
            pltpu.SemaphoreType.DMA((8,)),
            pltpu.SemaphoreType.DMA((2, 4)),
            pltpu.SemaphoreType.DMA((112,)),
            pltpu.SemaphoreType.DMA((112,)),
        ],
        compiler_params=pltpu.CompilerParams(collective_id=0, has_side_effects=True),
        name="window",
    )(occ_index, vir_index, freq_index, freq_table, pair_weight, coulomb, band_vectors)


def solution(mesh):
    torus = Mesh(
        mesh.devices.reshape(mesh.shape["grp"], 4, 8, 2, mesh.shape["cols"]),
        ("grp", "rows_0", "rows_1", "rows_2", "cols"),
    )
    placed = (P(ROWS, None), P(ROWS), P(), P(), P(), P(), P())
    return jax.shard_map(
        per_device, mesh=torus, in_specs=placed, out_specs=P(ROWS_COLS, "grp"), check_vma=False
    )
```

```python
import math

import jax
import jax.numpy as jnp
from jax import lax
from jax.experimental import pallas as pl
from jax.experimental.pallas import tpu as pltpu
from jax.sharding import Mesh
from jax.sharding import PartitionSpec as P

NB = 49152
ROWS = ("rows_0", "rows_1", "rows_2")
ROWS_COLS = ("rows_0", "rows_1", "rows_2", "cols")
MESH = pl.DeviceIdType.MESH
F32 = jnp.float32
BF16 = jnp.bfloat16
KB = 768
NK = KB // 128
HALF = 768
RELS = [(a, b, d) for a in range(2) for b in range(2) for d in range(2)][1:]
NEAR = [(e, a, b, d) for e in range(4) for a in range(2) for b in range(2) for d in range(2)]


def split(x):
    hi = x.astype(BF16)
    return hi, (x - hi.astype(F32)).astype(BF16)


def nt(a, b):
    return lax.dot_general(a, b, (((1,), (1,)), ((), ())), preferred_element_type=F32)


def nn(a, b):
    return lax.dot_general(a, b, (((1,), (0,)), ((), ())), preferred_element_type=F32)


def nt3(ah, al, bh, bl):
    return nt(ah, bh) + nt(ah, bl) + nt(al, bh)


def nn3(ah, al, bh, bl):
    return nn(ah, bh) + nn(ah, bl) + nn(al, bh)


def mod(a, n):
    return lax.rem(a + n, n)


def window_kernel(
    occ_hbm, vir_hbm, fidx_hbm, ftab_hbm, weight_hbm, coulomb_hbm, v_hbm, out_ref,
    occ, vir, fidx, ftab, weight, coulomb, v_ref, vt, pt, qt, ph, pw, qh, ql, nh, nl,
    r_own, r_oth, r_in, x_all, x_in,
    za_in, zb_in, zc_in, zr_in, yin, rfin, xfin, ry_in, xz_in,
    rq, xt, yt, xq, y32, yq, mbuf, m_in, sbuf, s_pair, s_in,
    load, psend, precv, xpsend, xprecv, qsend, qrecv, ssend, srecv, send, recv,
):
    y = lax.axis_index("rows_0")
    z = lax.axis_index("rows_1")
    c = lax.axis_index("rows_2")
    g = lax.axis_index("grp")
    cl = lax.axis_index("cols")
    plane = 2 * g + cl
    started = []

    def copy(src, dst, to):
        i = len(started)
        d = pltpu.make_async_remote_copy(
            src_ref=src, dst_ref=dst, send_sem=send.at[i], recv_sem=recv.at[i],
            device_id=to, device_id_type=MESH,
        )
        d.start()
        started.append(d)
        return d

    def zto(k):
        return {"rows_1": mod(z + k, 8)}

    def yto(k):
        return {"rows_0": mod(y + k, 4)}

    def near(rel):
        ry, rg, rc, rl = rel
        return {
            "rows_0": mod(y + ry, 4), "grp": mod(g + rg, 2),
            "rows_2": mod(c + rc, 2), "cols": mod(cl + rl, 2),
        }

    vt2 = vt.reshape(8192, 128)
    pts = (pt, qt)
    pt2s = (pt.reshape(2048, 128), qt.reshape(2048, 128))
    loads = []
    for k in range(NK):
        rows = pl.ds(k * 128, 128)
        loads.append(pltpu.make_async_copy(v_hbm.at[rows], v_ref.at[rows], load.at[k]))
    smalls = (
        (occ_hbm, occ), (vir_hbm, vir), (weight_hbm, weight),
        (coulomb_hbm, coulomb), (fidx_hbm, fidx), (ftab_hbm, ftab),
    )
    for k, (src, dst) in enumerate(smalls):
        loads.append(pltpu.make_async_copy(src, dst, load.at[NK + k]))
    for d in loads:
        d.start()

    barrier = pltpu.get_barrier_semaphore()
    for k in range(1, 8):
        pl.semaphore_signal(barrier, inc=1, device_id=zto(k), device_id_type=MESH)
    for rel in NEAR[1:]:
        pl.semaphore_signal(barrier, inc=1, device_id=near(rel), device_id_type=MESH)

    for k in range(NK):
        loads[k].wait()
        for nb in range(8):
            block = v_ref[k * 128 : (k + 1) * 128, nb * 128 : (nb + 1) * 128]
            vt2[pl.ds(nb * 1024 + k, 128, stride=8), :] = block.T

    for d in loads[NK:]:
        d.wait()

    def gather_some(base, to, count, rows=pt):
        for u in range(count):
            rows[to + u] = vt[occ[base + u]] * vt[vir[base + u]]

    def weights(base):
        row = weight[pl.ds(pl.multiple_of(base, 128), 128)].reshape(1, 128)
        return jnp.broadcast_to(row, (128, 128)).T

    def cvec(k):
        return coulomb[k * 128 : (k + 1) * 128].reshape(1, 128)

    window = [256 * plane + 128 * mod(c + s, 2) for s in range(2)]

    def window_rows():
        for s in range(2):
            w = weights(window[s])
            for k in range(NK):
                x = pt2s[1][pl.ds(s * 1024 + k, 128, stride=8), :] * w * cvec(k)
                hi, lo = split(x)
                qh[s * 128 : (s + 1) * 128, k * 128 : (k + 1) * 128] = hi
                ql[s * 128 : (s + 1) * 128, k * 128 : (k + 1) * 128] = lo

    def band_rows():
        for k in range(NK):
            for m in range(16):
                two = [
                    vt2[pl.ds((32 * (2 * m + e) + 8 * plane) * 8 + k, 8, stride=8), :] for e in range(2)
                ]
                hi, lo = split(jnp.concatenate(two, axis=0) * cvec(k))
                nh[m * 16 : (m + 1) * 16, k * 128 : (k + 1) * 128] = hi
                nl[m * 16 : (m + 1) * 16, k * 128 : (k + 1) * 128] = lo

    core = {"rows_2": 1 - c}

    def to_partner(i):
        rows = pl.ds(pl.multiple_of(i * 256, 256), 256)
        return pltpu.make_async_remote_copy(
            src_ref=r_oth.at[rows], dst_ref=r_in.at[rows], send_sem=psend.at[i],
            recv_sem=precv.at[i], device_id=core, device_id_type=MESH,
        )

    def place(i):
        return [512 * (i % 3) + 256 * s + 128 * (i // 3) for s in range(2)]

    def buffer_of(i):
        return 0 if i == 0 else (i + 1) % 2

    def rows_of(i, bases):
        for s in range(2):
            w = weights(bases[s])
            for k in range(NK):
                hi, lo = split(pt2s[buffer_of(i)][pl.ds(s * 1024 + k, 128, stride=8), :] * w)
                ph[i, s * 128 : (s + 1) * 128, k * 128 : (k + 1) * 128] = hi
                pw[i, s * 128 : (s + 1) * 128, k * 128 : (k + 1) * 128] = lo

    def response_of(i):
        r = nt3(ph[i], pw[i], qh[...], ql[...])
        r_own[i * 256 : (i + 1) * 256, :] = r[:, 0:128]
        r_oth[i * 256 : (i + 1) * 256, :] = r[:, 128:256]

    def rpiece(k, ky):
        at = (ky * 8 + mod(z + k, 8)) * 48
        return r_own.at[pl.ds(pl.multiple_of(at, 8), 48)]

    sign = (-1, 1)
    fa = {}
    fb = {}
    fc = {}

    def start_sum(ky):
        for i in ((0, 1), (2,), (3, 4), (5,))[ky]:
            to_partner(i).wait()
        rows = slice(384 * ky, 384 * ky + 384)
        r_own[rows] += r_in[rows]
        n, j = ky // 2, ky % 2
        fa[n, j] = copy(rpiece(4 * sign[n], ky), za_in.at[n, j], zto(2 * sign[n]))
        for d in range(2):
            fb[d, ky] = copy(rpiece(3 * sign[d], ky), zb_in.at[d, ky], zto(sign[d]))
        for d in range(2):
            fc[d, ky] = copy(rpiece(sign[d], ky), zc_in.at[d, ky], zto(sign[d]))

    def coupling_pair(i):
        return pltpu.make_async_remote_copy(
            src_ref=x_all.at[i], dst_ref=x_in.at[i % 3], send_sem=xpsend.at[i % 3],
            recv_sem=xprecv.at[i % 3], device_id=core, device_id_type=MESH,
        )

    def yterm(k, h, q):
        rows = pl.multiple_of(mod(y + k, 4) * 64 + 32 * h, 8)
        return x_all.at[3 * c + q, pl.ds(rows, 32)]

    yl = {}
    ys = {}

    def start_long(q):
        coupling_pair(q).wait_recv()
        x_all[3 * c + q] += x_in[q]
        for d in range(2):
            yl[d, q] = copy(yterm(2, d, q), yin.at[d, q, 0], yto(sign[d]))

    def start_short(q):
        for d in range(2):
            ys[d, q] = copy(yterm(sign[d], 1 - d, q), yin.at[d, q, 1], yto(sign[d]))

    def gather_block(i):
        for e in range(2):
            gather_some(place(i)[e], 128 * e, 128, pts[buffer_of(i)])

    def coupling_of(n):
        x_all[n] = nt3(nh[...], nl[...], ph[n], pw[n])

    def send_coupling(n):
        @pl.when(c != n // 3)
        def _():
            coupling_pair(n).start()

    gather_block(0)
    band_rows()
    for e in range(2):
        gather_some(window[e], 128 * e, 128, pts[1])
    rows_of(0, place(0))
    gather_block(1)
    window_rows()
    coupling_of(0)
    pl.semaphore_wait(barrier, 38)
    send_coupling(0)
    gather_block(2)
    rows_of(1, place(1))
    response_of(0)
    to_partner(0).start()
    for n in range(1, 5):
        if n + 2 < 6:
            gather_block(n + 2)
        rows_of(n + 1, place(n + 1))
        response_of(n)
        coupling_of(n)
        to_partner(n).start()
        send_coupling(n)
        if n in (2, 3):
            start_sum(n - 2)
    response_of(5)
    to_partner(5).start()
    start_long(0)
    start_short(0)
    start_sum(2)
    coupling_of(5)
    send_coupling(5)
    start_long(1)
    start_sum(3)
    start_long(2)
    start_short(1)
    start_short(2)

    fr = {}
    xz = []

    def relay(ky):
        for d in range(2):
            fb[d, ky].wait_recv()
            part = zb_in[d, ky] + rpiece(2 * sign[d], ky)[...]
            if ky // 2 == d:
                fa[d, ky % 2].wait_recv()
                part = part + za_in[d, ky % 2]
            zb_in[d, ky] = part
            fr[d, ky] = copy(zb_in.at[d, ky], zr_in.at[d, ky], zto(2 * sign[d]))

    def pass_on(q):
        for d in range(2):
            yl[d, q].wait_recv()
            yin[d, q, 0] += yterm(sign[d], d, q)[...]
            yl[d, q] = copy(yin.at[d, q, 0], yin.at[d, q, 2], yto(sign[d]))

    def finish_piece(ky):
        part = rpiece(0, ky)[...]
        for d in range(2):
            fc[d, ky].wait_recv()
            fr[d, ky].wait_recv()
            part = part + (zc_in[d, ky] + zr_in[d, ky])
        rfin[ky] = part

    def finish_rows(q):
        for d in range(2):
            ys[d, q].wait_recv()
            yl[d, q].wait_recv()
        for h in range(2):
            xfin[q, 32 * h : 32 * h + 32] = (
                yterm(0, h, q)[...] + yin[h, q, 2] + yin[1 - h, q, 1]
            )
        for k in (4, 3, 5, 2, 6, 1, 7):
            rows = pl.ds(pl.multiple_of(mod(z + k, 8) * 8, 8), 8)
            xz.append(copy(xfin.at[q, rows], xz_in.at[k, q], zto(k)))

    relay(0)
    pass_on(0)
    relay(1)
    relay(2)
    pass_on(1)
    relay(3)
    pass_on(2)
    finish_piece(0)
    finish_piece(1)
    finish_rows(0)
    finish_rows(1)
    finish_piece(2)
    finish_rows(2)
    finish_piece(3)
    ry = [copy(rfin.at[mod(y + k, 4)], ry_in.at[k], yto(k)) for k in (2, 1, 3)]

    for d in ry:
        d.wait_recv()
    rq[z] = (rfin[y] + (ry_in[1] + ry_in[2] + ry_in[3])) * (1.0 / NB)
    rz = [copy(rq.at[z], rq.at[z], zto(k)) for k in (4, 3, 5, 2, 6, 1, 7)]

    for d in xz:
        d.wait_recv()
    tile = xfin[:, pl.ds(pl.multiple_of(z * 8, 8), 8)]
    for k in range(1, 8):
        tile = tile + xz_in[k]
    chip = y * 8 + z
    row = lax.broadcasted_iota(jnp.int32, (3, 8, 256), 1)
    factor = jnp.zeros((3, 8, 256), F32)
    for i in range(8):
        factor = jnp.where(row == i, ftab[fidx[32 * chip + 8 * plane + i]], factor)
    tile = tile * factor * (1.0 / math.sqrt(NB))
    xt[0] = jnp.concatenate([tile[0], tile[1][:, 0:128]], axis=1)
    xt[1] = jnp.concatenate([tile[1][:, 128:256], tile[2]], axis=1)
    for j in range(4):
        yt[j] = tile[j // 2][:, 128 * (j % 2) : 128 * (j % 2) + 128]

    def quarter(i, rel, e):
        rg, rc, rl = rel
        to = {"grp": mod(g + rg, 2), "rows_2": mod(c + rc, 2), "cols": mod(cl + rl, 2)}
        to["rows_0"] = 2 * c + e
        return pltpu.make_async_remote_copy(
            src_ref=xt.at[e], dst_ref=xq.at[y, plane], send_sem=qsend.at[i],
            recv_sem=qrecv.at[y, plane], device_id=to, device_id_type=MESH,
        )

    quarters = [(rel, e) for e in range(2) for rel in [(0, 0, 0)] + RELS]
    for i, (rel, e) in enumerate(quarters):
        if rel == (0, 0, 0):

            @pl.when(y != 2 * c + e)
            def _(i=i, rel=rel, e=e):
                quarter(i, rel, e).start()

            @pl.when(y == 2 * c + e)
            def _(e=e):
                xq[y, plane] = xt[e]
        else:
            quarter(i, rel, e).start()
    yx = []
    for rg, rl in ((1, 1), (1, 0), (0, 1)):
        to = {"grp": mod(g + rg, 2), "cols": mod(cl + rl, 2)}
        yx.append(copy(yt.at[2 * to["grp"] + to["cols"]], y32.at[plane], to))
    y32[plane] = yt[plane]
    for d in yx:
        d.wait_recv()
    for j in range(4):
        yq[z, 8 * j : 8 * j + 8] = y32[j]
    yz = [copy(yq.at[z], yq.at[z], zto(k)) for k in (4, 3, 5, 2, 6, 1, 7)]

    for d in rz:
        d.wait_recv()
    for ys_ in range(4):
        for j in range(4):

            def arrived(ys_=ys_, j=j):
                pltpu.make_async_remote_copy(
                    src_ref=xt.at[0], dst_ref=xq.at[ys_, j], send_sem=qsend.at[0],
                    recv_sem=qrecv.at[ys_, j], device_id=core, device_id_type=MESH,
                ).wait_recv()

            own = (ys_ == y) & (j == plane) & (c == y // 2)
            pl.when(jnp.logical_not(own))(arrived)

    xh, xl = split(xq[...].reshape(128, 384))
    rh, rl_ = split(rq[...].reshape(384, 128))
    mbuf[...] = nn3(xh, xl, rh, rl_)
    my = [copy(mbuf, m_in.at[k], yto(k)) for k in (2, 1, 3)]
    for d in yz:
        d.wait_recv()
    yh, yw = split(yq[...].reshape(256, 128))
    for d in my:
        d.wait_recv()
    mh, ml = split(mbuf[...] + (m_in[1] + m_in[2] + m_in[3]))
    s = nt3(mh, ml, yh, yw)
    for i in range(16):
        sbuf[(i // 2) % 2, (i // 4) * 2 + i % 2] = s[8 * i : 8 * i + 8, :]
    dp = copy(sbuf.at[1 - c], s_pair, core)

    e = lax.rem(y, 2)

    def result(i, ry_, rl):
        to = {"grp": y // 2, "rows_0": mod(y + ry_, 4), "cols": mod(cl + rl, 2)}
        return pltpu.make_async_remote_copy(
            src_ref=sbuf.at[c, to["rows_0"] * 2 + to["cols"]], dst_ref=s_in.at[e, plane],
            send_sem=ssend.at[i], recv_sem=srecv.at[e, plane], device_id=to, device_id_type=MESH,
        )

    dp.wait_recv()
    sbuf[c] += s_pair[...]
    results = [(a, d) for a in (2, 1, 3, 0) for d in (1, 0)]
    for i, rel in enumerate(results):
        if rel == (0, 0):

            @pl.when(y // 2 != g)
            def _(i=i, rel=rel):
                result(i, *rel).start()

            @pl.when(y // 2 == g)
            def _():
                s_in[e, plane] = sbuf[c, y * 2 + cl]
        else:
            result(i, *rel).start()
    for e_ in range(2):
        for j in range(4):

            def landed(e_=e_, j=j):
                pltpu.make_async_remote_copy(
                    src_ref=sbuf.at[0, 0], dst_ref=s_in.at[e_, j], send_sem=ssend.at[0],
                    recv_sem=srecv.at[e_, j], device_id=core, device_id_type=MESH,
                ).wait_recv()

            own = (e_ == e) & (j == plane) & (y // 2 == g)
            pl.when(jnp.logical_not(own))(landed)
    for e_ in range(2):
        total = s_in[e_, 0] + s_in[e_, 1] + (s_in[e_, 2] + s_in[e_, 3])
        out_ref[:, 256 * e_ : 256 * e_ + 256] = total * (1.0 / math.sqrt(1024))

    for i, (rel, e_) in enumerate(quarters):
        if rel == (0, 0, 0):

            @pl.when(y != 2 * c + e_)
            def _(i=i, rel=rel, e_=e_):
                quarter(i, rel, e_).wait_send()
        else:
            quarter(i, rel, e_).wait_send()
    for i, rel in enumerate(results):
        if rel == (0, 0):

            @pl.when(y // 2 != g)
            def _(i=i, rel=rel):
                result(i, *rel).wait_send()
        else:
            result(i, *rel).wait_send()
    for t in range(3):
        coupling_pair(t).wait_send()
    for d in started:
        d.wait_send()


def per_device(band_vectors, coulomb, pair_weight, occ_index, vir_index, freq_index, freq_table):
    vmem = pl.BlockSpec(memory_space=pltpu.VMEM)
    return pl.pallas_call(
        window_kernel,
        out_shape=jax.ShapeDtypeStruct((8, 512), F32),
        in_specs=[pl.BlockSpec(memory_space=pl.ANY)] * 7,
        out_specs=vmem,
        scratch_shapes=[
            pltpu.SMEM((1536,), jnp.int32),
            pltpu.SMEM((1536,), jnp.int32),
            pltpu.SMEM((1024,), jnp.int32),
            pltpu.SMEM((16,), F32),
            pltpu.VMEM((1536,), F32),
            pltpu.VMEM((KB,), F32),
            pltpu.VMEM((KB, 1024), F32),
            pltpu.VMEM((1024, 8, 128), F32),
            pltpu.VMEM((256, 8, 128), F32),
            pltpu.VMEM((256, 8, 128), F32),
            pltpu.VMEM((6, 256, KB), BF16),
            pltpu.VMEM((6, 256, KB), BF16),
            pltpu.VMEM((256, KB), BF16),
            pltpu.VMEM((256, KB), BF16),
            pltpu.VMEM((256, KB), BF16),
            pltpu.VMEM((256, KB), BF16),
            pltpu.VMEM((1536, 128), F32),
            pltpu.VMEM((1536, 128), F32),
            pltpu.VMEM((1536, 128), F32),
            pltpu.VMEM((6, 256, 256), F32),
            pltpu.VMEM((3, 256, 256), F32),
            pltpu.VMEM((2, 2, 48, 128), F32),
            pltpu.VMEM((2, 4, 48, 128), F32),
            pltpu.VMEM((2, 4, 48, 128), F32),
            pltpu.VMEM((2, 4, 48, 128), F32),
            pltpu.VMEM((2, 3, 3, 32, 256), F32),
            pltpu.VMEM((4, 48, 128), F32),
            pltpu.VMEM((3, 64, 256), F32),
            pltpu.VMEM((4, 48, 128), F32),
            pltpu.VMEM((8, 3, 8, 256), F32),
            pltpu.VMEM((8, 48, 128), F32),
            pltpu.VMEM((2, 8, 384), F32),
            pltpu.VMEM((4, 8, 128), F32),
            pltpu.VMEM((4, 4, 8, 384), F32),
            pltpu.VMEM((4, 8, 128), F32),
            pltpu.VMEM((8, 32, 128), F32),
            pltpu.VMEM((128, 128), F32),
            pltpu.VMEM((4, 128, 128), F32),
            pltpu.VMEM((2, 8, 8, 256), F32),
            pltpu.VMEM((8, 8, 256), F32),
            pltpu.VMEM((2, 4, 8, 256), F32),
            pltpu.SemaphoreType.DMA((NK + 6,)),
            pltpu.SemaphoreType.DMA((6,)),
            pltpu.SemaphoreType.DMA((6,)),
            pltpu.SemaphoreType.DMA((3,)),
            pltpu.SemaphoreType.DMA((3,)),
            pltpu.SemaphoreType.DMA((16,)),
            pltpu.SemaphoreType.DMA((4, 4)),
            pltpu.SemaphoreType.DMA((8,)),
            pltpu.SemaphoreType.DMA((2, 4)),
            pltpu.SemaphoreType.DMA((112,)),
            pltpu.SemaphoreType.DMA((112,)),
        ],
        compiler_params=pltpu.CompilerParams(collective_id=0, has_side_effects=True),
        name="window",
    )(occ_index, vir_index, freq_index, freq_table, pair_weight, coulomb, band_vectors)


def solution(mesh):
    torus = Mesh(
        mesh.devices.reshape(mesh.shape["grp"], 4, 8, 2, mesh.shape["cols"]),
        ("grp", "rows_0", "rows_1", "rows_2", "cols"),
    )
    placed = (P(ROWS, None), P(ROWS), P(), P(), P(), P(), P())
    return jax.shard_map(
        per_device, mesh=torus, in_specs=placed, out_specs=P(ROWS_COLS, "grp"), check_vma=False
    )
```

```python
import math

import jax
import jax.numpy as jnp
from jax import lax
from jax.experimental import pallas as pl
from jax.experimental.pallas import tpu as pltpu
from jax.sharding import Mesh
from jax.sharding import PartitionSpec as P

NB = 49152
ROWS = ("rows_0", "rows_1", "rows_2")
ROWS_COLS = ("rows_0", "rows_1", "rows_2", "cols")
MESH = pl.DeviceIdType.MESH
F32 = jnp.float32
BF16 = jnp.bfloat16
KB = 768
NK = KB // 128
HALF = 768
RELS = [(a, b, d) for a in range(2) for b in range(2) for d in range(2)][1:]
NEAR = [(e, a, b, d) for e in range(4) for a in range(2) for b in range(2) for d in range(2)]


def split(x):
    hi = x.astype(BF16)
    return hi, (x - hi.astype(F32)).astype(BF16)


def nt(a, b):
    return lax.dot_general(a, b, (((1,), (1,)), ((), ())), preferred_element_type=F32)


def nn(a, b):
    return lax.dot_general(a, b, (((1,), (0,)), ((), ())), preferred_element_type=F32)


def nt3(ah, al, bh, bl):
    return nt(ah, bh) + nt(ah, bl) + nt(al, bh)


def nn3(ah, al, bh, bl):
    return nn(ah, bh) + nn(ah, bl) + nn(al, bh)


def mod(a, n):
    return lax.rem(a + n, n)


def window_kernel(
    occ_hbm, vir_hbm, fidx_hbm, ftab_hbm, weight_hbm, coulomb_hbm, v_hbm, out_ref,
    occ, vir, fidx, ftab, weight, coulomb, v_ref, vt, pt, qt, ph, pw, qh, ql, nh, nl,
    r_own, r_oth, r_in, x_all, x_in,
    za_in, zb_in, zc_in, zr_in, yin, rfin, xfin, ry_in, xz_in,
    rq, xt, yt, xq, y32, yq, mbuf, m_in, sbuf, s_pair, s_in,
    load, psend, precv, xpsend, xprecv, qsend, qrecv, ssend, srecv, send, recv,
):
    y = lax.axis_index("rows_0")
    z = lax.axis_index("rows_1")
    c = lax.axis_index("rows_2")
    g = lax.axis_index("grp")
    cl = lax.axis_index("cols")
    plane = 2 * g + cl
    started = []

    def copy(src, dst, to):
        i = len(started)
        d = pltpu.make_async_remote_copy(
            src_ref=src, dst_ref=dst, send_sem=send.at[i], recv_sem=recv.at[i],
            device_id=to, device_id_type=MESH,
        )
        d.start()
        started.append(d)
        return d

    def zto(k):
        return {"rows_1": mod(z + k, 8)}

    def yto(k):
        return {"rows_0": mod(y + k, 4)}

    def near(rel):
        ry, rg, rc, rl = rel
        return {
            "rows_0": mod(y + ry, 4), "grp": mod(g + rg, 2),
            "rows_2": mod(c + rc, 2), "cols": mod(cl + rl, 2),
        }

    vt2 = vt.reshape(8192, 128)
    pts = (pt, qt)
    pt2s = (pt.reshape(2048, 128), qt.reshape(2048, 128))
    loads = []
    for k in range(NK):
        rows = pl.ds(k * 128, 128)
        loads.append(pltpu.make_async_copy(v_hbm.at[rows], v_ref.at[rows], load.at[k]))
    smalls = (
        (occ_hbm, occ), (vir_hbm, vir), (weight_hbm, weight),
        (coulomb_hbm, coulomb), (fidx_hbm, fidx), (ftab_hbm, ftab),
    )
    for k, (src, dst) in enumerate(smalls):
        loads.append(pltpu.make_async_copy(src, dst, load.at[NK + k]))
    for d in loads:
        d.start()

    barrier = pltpu.get_barrier_semaphore()
    for k in range(1, 8):
        pl.semaphore_signal(barrier, inc=1, device_id=zto(k), device_id_type=MESH)
    for rel in NEAR[1:]:
        pl.semaphore_signal(barrier, inc=1, device_id=near(rel), device_id_type=MESH)

    for k in range(NK):
        loads[k].wait()
        for nb in range(8):
            block = v_ref[k * 128 : (k + 1) * 128, nb * 128 : (nb + 1) * 128]
            vt2[pl.ds(nb * 1024 + k, 128, stride=8), :] = block.T

    for d in loads[NK:]:
        d.wait()

    def gather_some(base, to, count, rows=pt):
        for u in range(count):
            rows[to + u] = vt[occ[base + u]] * vt[vir[base + u]]

    def weights(base):
        row = weight[pl.ds(pl.multiple_of(base, 128), 128)].reshape(1, 128)
        return jnp.broadcast_to(row, (128, 128)).T

    def cvec(k):
        return coulomb[k * 128 : (k + 1) * 128].reshape(1, 128)

    window = [256 * plane + 128 * mod(c + s, 2) for s in range(2)]

    def window_rows():
        for s in range(2):
            w = weights(window[s])
            for k in range(NK):
                x = pt2s[1][pl.ds(s * 1024 + k, 128, stride=8), :] * w * cvec(k)
                hi, lo = split(x)
                qh[s * 128 : (s + 1) * 128, k * 128 : (k + 1) * 128] = hi
                ql[s * 128 : (s + 1) * 128, k * 128 : (k + 1) * 128] = lo

    def band_rows():
        for k in range(NK):
            for m in range(16):
                two = [
                    vt2[pl.ds((32 * (2 * m + e) + 8 * plane) * 8 + k, 8, stride=8), :] for e in range(2)
                ]
                hi, lo = split(jnp.concatenate(two, axis=0) * cvec(k))
                nh[m * 16 : (m + 1) * 16, k * 128 : (k + 1) * 128] = hi
                nl[m * 16 : (m + 1) * 16, k * 128 : (k + 1) * 128] = lo

    core = {"rows_2": 1 - c}

    def to_partner(i):
        rows = pl.ds(pl.multiple_of(i * 256, 256), 256)
        return pltpu.make_async_remote_copy(
            src_ref=r_oth.at[rows], dst_ref=r_in.at[rows], send_sem=psend.at[i],
            recv_sem=precv.at[i], device_id=core, device_id_type=MESH,
        )

    def place(i):
        return [512 * (i % 3) + 256 * s + 128 * (i // 3) for s in range(2)]

    def buffer_of(i):
        return 0 if i == 0 else (i + 1) % 2

    def rows_of(i, bases):
        for s in range(2):
            w = weights(bases[s])
            for k in range(NK):
                hi, lo = split(pt2s[buffer_of(i)][pl.ds(s * 1024 + k, 128, stride=8), :] * w)
                ph[i, s * 128 : (s + 1) * 128, k * 128 : (k + 1) * 128] = hi
                pw[i, s * 128 : (s + 1) * 128, k * 128 : (k + 1) * 128] = lo

    def response_of(i):
        r = nt3(ph[i], pw[i], qh[...], ql[...])
        r_own[i * 256 : (i + 1) * 256, :] = r[:, 0:128]
        r_oth[i * 256 : (i + 1) * 256, :] = r[:, 128:256]

    def rpiece(k, ky):
        at = (ky * 8 + mod(z + k, 8)) * 48
        return r_own.at[pl.ds(pl.multiple_of(at, 8), 48)]

    sign = (-1, 1)
    fa = {}
    fb = {}
    fc = {}

    def start_sum(ky):
        for i in ((0, 1), (2,), (3, 4), (5,))[ky]:
            to_partner(i).wait()
        rows = slice(384 * ky, 384 * ky + 384)
        r_own[rows] += r_in[rows]
        n, j = ky // 2, ky % 2
        fa[n, j] = copy(rpiece(4 * sign[n], ky), za_in.at[n, j], zto(2 * sign[n]))
        for d in range(2):
            fb[d, ky] = copy(rpiece(3 * sign[d], ky), zb_in.at[d, ky], zto(sign[d]))
        for d in range(2):
            fc[d, ky] = copy(rpiece(sign[d], ky), zc_in.at[d, ky], zto(sign[d]))

    def coupling_pair(i):
        return pltpu.make_async_remote_copy(
            src_ref=x_all.at[i], dst_ref=x_in.at[i % 3], send_sem=xpsend.at[i % 3],
            recv_sem=xprecv.at[i % 3], device_id=core, device_id_type=MESH,
        )

    def gather_block(i):
        for e in range(2):
            gather_some(place(i)[e], 128 * e, 128, pts[buffer_of(i)])

    def coupling_of(n):
        x_all[n] = nt3(nh[...], nl[...], ph[n], pw[n])

    def send_coupling(n):
        @pl.when(c != n // 3)
        def _():
            coupling_pair(n).start()

    gather_block(0)
    band_rows()
    for e in range(2):
        gather_some(window[e], 128 * e, 128, pts[1])
    rows_of(0, place(0))
    gather_block(1)
    window_rows()
    coupling_of(0)
    pl.semaphore_wait(barrier, 38)
    send_coupling(0)
    gather_block(2)
    rows_of(1, place(1))
    response_of(0)
    to_partner(0).start()
    for n in range(1, 5):
        if n + 2 < 6:
            gather_block(n + 2)
        rows_of(n + 1, place(n + 1))
        response_of(n)
        coupling_of(n)
        to_partner(n).start()
        send_coupling(n)
        if n in (2, 3):
            start_sum(n - 2)
    response_of(5)
    to_partner(5).start()
    start_sum(2)
    coupling_of(5)
    send_coupling(5)
    start_sum(3)

    def yrows(k, start, size):
        return pl.ds(pl.multiple_of(mod(y + k, 4) * 64 + start, 8), size)

    def yterm(k, h, q):
        return x_all.at[3 * c + q, yrows(k, 32 * h, 32)]

    yl = {}
    ys = {}
    for q in range(3):
        coupling_pair(q).wait_recv()
        x_all[3 * c + q] += x_in[q]
        for d in range(2):
            yl[d, q] = copy(yterm(2, d, q), yin.at[d, q, 0], yto(sign[d]))
    for q in range(3):
        for d in range(2):
            ys[d, q] = copy(yterm(sign[d], 1 - d, q), yin.at[d, q, 1], yto(sign[d]))

    fr = {}
    xz = []

    def relay(ky):
        for d in range(2):
            fb[d, ky].wait_recv()
            part = zb_in[d, ky] + rpiece(2 * sign[d], ky)[...]
            if ky // 2 == d:
                fa[d, ky % 2].wait_recv()
                part = part + za_in[d, ky % 2]
            zb_in[d, ky] = part
            fr[d, ky] = copy(zb_in.at[d, ky], zr_in.at[d, ky], zto(2 * sign[d]))

    def pass_on(q):
        for d in range(2):
            yl[d, q].wait_recv()
            yin[d, q, 0] += yterm(sign[d], d, q)[...]
            yl[d, q] = copy(yin.at[d, q, 0], yin.at[d, q, 2], yto(sign[d]))

    def finish_piece(ky):
        part = rpiece(0, ky)[...]
        for d in range(2):
            fc[d, ky].wait_recv()
            fr[d, ky].wait_recv()
            part = part + (zc_in[d, ky] + zr_in[d, ky])
        rfin[ky] = part

    def finish_rows(q):
        for d in range(2):
            ys[d, q].wait_recv()
            yl[d, q].wait_recv()
        for h in range(2):
            xfin[q, 32 * h : 32 * h + 32] = (
                yterm(0, h, q)[...] + yin[h, q, 2] + yin[1 - h, q, 1]
            )
        for k in (4, 3, 5, 2, 6, 1, 7):
            rows = pl.ds(pl.multiple_of(mod(z + k, 8) * 8, 8), 8)
            xz.append(copy(xfin.at[q, rows], xz_in.at[k, q], zto(k)))

    relay(0)
    relay(1)
    pass_on(0)
    relay(2)
    pass_on(1)
    relay(3)
    pass_on(2)
    finish_piece(0)
    finish_piece(1)
    finish_rows(0)
    finish_rows(1)
    finish_piece(2)
    finish_piece(3)
    ry = [copy(rfin.at[mod(y + k, 4)], ry_in.at[k], yto(k)) for k in (2, 1, 3)]
    finish_rows(2)

    for d in ry:
        d.wait_recv()
    rq[z] = (rfin[y] + (ry_in[1] + ry_in[2] + ry_in[3])) * (1.0 / NB)
    rz = [copy(rq.at[z], rq.at[z], zto(k)) for k in (4, 3, 5, 2, 6, 1, 7)]

    for d in xz:
        d.wait_recv()
    tile = xfin[:, pl.ds(pl.multiple_of(z * 8, 8), 8)]
    for k in range(1, 8):
        tile = tile + xz_in[k]
    chip = y * 8 + z
    row = lax.broadcasted_iota(jnp.int32, (3, 8, 256), 1)
    factor = jnp.zeros((3, 8, 256), F32)
    for i in range(8):
        factor = jnp.where(row == i, ftab[fidx[32 * chip + 8 * plane + i]], factor)
    tile = tile * factor * (1.0 / math.sqrt(NB))
    xt[0] = jnp.concatenate([tile[0], tile[1][:, 0:128]], axis=1)
    xt[1] = jnp.concatenate([tile[1][:, 128:256], tile[2]], axis=1)
    for j in range(4):
        yt[j] = tile[j // 2][:, 128 * (j % 2) : 128 * (j % 2) + 128]

    def quarter(i, rel, e):
        rg, rc, rl = rel
        to = {"grp": mod(g + rg, 2), "rows_2": mod(c + rc, 2), "cols": mod(cl + rl, 2)}
        to["rows_0"] = 2 * c + e
        return pltpu.make_async_remote_copy(
            src_ref=xt.at[e], dst_ref=xq.at[y, plane], send_sem=qsend.at[i],
            recv_sem=qrecv.at[y, plane], device_id=to, device_id_type=MESH,
        )

    quarters = [(rel, e) for e in range(2) for rel in [(0, 0, 0)] + RELS]
    for i, (rel, e) in enumerate(quarters):
        if rel == (0, 0, 0):

            @pl.when(y != 2 * c + e)
            def _(i=i, rel=rel, e=e):
                quarter(i, rel, e).start()

            @pl.when(y == 2 * c + e)
            def _(e=e):
                xq[y, plane] = xt[e]
        else:
            quarter(i, rel, e).start()
    yx = []
    for rg, rl in ((1, 1), (1, 0), (0, 1)):
        to = {"grp": mod(g + rg, 2), "cols": mod(cl + rl, 2)}
        yx.append(copy(yt.at[2 * to["grp"] + to["cols"]], y32.at[plane], to))
    y32[plane] = yt[plane]
    for d in yx:
        d.wait_recv()
    for j in range(4):
        yq[z, 8 * j : 8 * j + 8] = y32[j]
    yz = [copy(yq.at[z], yq.at[z], zto(k)) for k in (4, 3, 5, 2, 6, 1, 7)]

    for d in rz:
        d.wait_recv()
    for ys_ in range(4):
        for j in range(4):

            def arrived(ys_=ys_, j=j):
                pltpu.make_async_remote_copy(
                    src_ref=xt.at[0], dst_ref=xq.at[ys_, j], send_sem=qsend.at[0],
                    recv_sem=qrecv.at[ys_, j], device_id=core, device_id_type=MESH,
                ).wait_recv()

            own = (ys_ == y) & (j == plane) & (c == y // 2)
            pl.when(jnp.logical_not(own))(arrived)

    xh, xl = split(xq[...].reshape(128, 384))
    rh, rl_ = split(rq[...].reshape(384, 128))
    mbuf[...] = nn3(xh, xl, rh, rl_)
    my = [copy(mbuf, m_in.at[k], yto(k)) for k in (2, 1, 3)]
    for d in yz:
        d.wait_recv()
    yh, yw = split(yq[...].reshape(256, 128))
    for d in my:
        d.wait_recv()
    mh, ml = split(mbuf[...] + (m_in[1] + m_in[2] + m_in[3]))
    s = nt3(mh, ml, yh, yw)
    for i in range(16):
        sbuf[(i // 2) % 2, (i // 4) * 2 + i % 2] = s[8 * i : 8 * i + 8, :]
    dp = copy(sbuf.at[1 - c], s_pair, core)

    e = lax.rem(y, 2)

    def result(i, ry_, rl):
        to = {"grp": y // 2, "rows_0": mod(y + ry_, 4), "cols": mod(cl + rl, 2)}
        return pltpu.make_async_remote_copy(
            src_ref=sbuf.at[c, to["rows_0"] * 2 + to["cols"]], dst_ref=s_in.at[e, plane],
            send_sem=ssend.at[i], recv_sem=srecv.at[e, plane], device_id=to, device_id_type=MESH,
        )

    dp.wait_recv()
    sbuf[c] += s_pair[...]
    results = [(a, d) for a in (2, 1, 3, 0) for d in (1, 0)]
    for i, rel in enumerate(results):
        if rel == (0, 0):

            @pl.when(y // 2 != g)
            def _(i=i, rel=rel):
                result(i, *rel).start()

            @pl.when(y // 2 == g)
            def _():
                s_in[e, plane] = sbuf[c, y * 2 + cl]
        else:
            result(i, *rel).start()
    for e_ in range(2):
        for j in range(4):

            def landed(e_=e_, j=j):
                pltpu.make_async_remote_copy(
                    src_ref=sbuf.at[0, 0], dst_ref=s_in.at[e_, j], send_sem=ssend.at[0],
                    recv_sem=srecv.at[e_, j], device_id=core, device_id_type=MESH,
                ).wait_recv()

            own = (e_ == e) & (j == plane) & (y // 2 == g)
            pl.when(jnp.logical_not(own))(landed)
    for e_ in range(2):
        total = s_in[e_, 0] + s_in[e_, 1] + (s_in[e_, 2] + s_in[e_, 3])
        out_ref[:, 256 * e_ : 256 * e_ + 256] = total * (1.0 / math.sqrt(1024))

    for i, (rel, e_) in enumerate(quarters):
        if rel == (0, 0, 0):

            @pl.when(y != 2 * c + e_)
            def _(i=i, rel=rel, e_=e_):
                quarter(i, rel, e_).wait_send()
        else:
            quarter(i, rel, e_).wait_send()
    for i, rel in enumerate(results):
        if rel == (0, 0):

            @pl.when(y // 2 != g)
            def _(i=i, rel=rel):
                result(i, *rel).wait_send()
        else:
            result(i, *rel).wait_send()
    for t in range(3):
        coupling_pair(t).wait_send()
    for d in started:
        d.wait_send()


def per_device(band_vectors, coulomb, pair_weight, occ_index, vir_index, freq_index, freq_table):
    vmem = pl.BlockSpec(memory_space=pltpu.VMEM)
    return pl.pallas_call(
        window_kernel,
        out_shape=jax.ShapeDtypeStruct((8, 512), F32),
        in_specs=[pl.BlockSpec(memory_space=pl.ANY)] * 7,
        out_specs=vmem,
        scratch_shapes=[
            pltpu.SMEM((1536,), jnp.int32),
            pltpu.SMEM((1536,), jnp.int32),
            pltpu.SMEM((1024,), jnp.int32),
            pltpu.SMEM((16,), F32),
            pltpu.VMEM((1536,), F32),
            pltpu.VMEM((KB,), F32),
            pltpu.VMEM((KB, 1024), F32),
            pltpu.VMEM((1024, 8, 128), F32),
            pltpu.VMEM((256, 8, 128), F32),
            pltpu.VMEM((256, 8, 128), F32),
            pltpu.VMEM((6, 256, KB), BF16),
            pltpu.VMEM((6, 256, KB), BF16),
            pltpu.VMEM((256, KB), BF16),
            pltpu.VMEM((256, KB), BF16),
            pltpu.VMEM((256, KB), BF16),
            pltpu.VMEM((256, KB), BF16),
            pltpu.VMEM((1536, 128), F32),
            pltpu.VMEM((1536, 128), F32),
            pltpu.VMEM((1536, 128), F32),
            pltpu.VMEM((6, 256, 256), F32),
            pltpu.VMEM((3, 256, 256), F32),
            pltpu.VMEM((2, 2, 48, 128), F32),
            pltpu.VMEM((2, 4, 48, 128), F32),
            pltpu.VMEM((2, 4, 48, 128), F32),
            pltpu.VMEM((2, 4, 48, 128), F32),
            pltpu.VMEM((2, 3, 3, 32, 256), F32),
            pltpu.VMEM((4, 48, 128), F32),
            pltpu.VMEM((3, 64, 256), F32),
            pltpu.VMEM((4, 48, 128), F32),
            pltpu.VMEM((8, 3, 8, 256), F32),
            pltpu.VMEM((8, 48, 128), F32),
            pltpu.VMEM((2, 8, 384), F32),
            pltpu.VMEM((4, 8, 128), F32),
            pltpu.VMEM((4, 4, 8, 384), F32),
            pltpu.VMEM((4, 8, 128), F32),
            pltpu.VMEM((8, 32, 128), F32),
            pltpu.VMEM((128, 128), F32),
            pltpu.VMEM((4, 128, 128), F32),
            pltpu.VMEM((2, 8, 8, 256), F32),
            pltpu.VMEM((8, 8, 256), F32),
            pltpu.VMEM((2, 4, 8, 256), F32),
            pltpu.SemaphoreType.DMA((NK + 6,)),
            pltpu.SemaphoreType.DMA((6,)),
            pltpu.SemaphoreType.DMA((6,)),
            pltpu.SemaphoreType.DMA((3,)),
            pltpu.SemaphoreType.DMA((3,)),
            pltpu.SemaphoreType.DMA((16,)),
            pltpu.SemaphoreType.DMA((4, 4)),
            pltpu.SemaphoreType.DMA((8,)),
            pltpu.SemaphoreType.DMA((2, 4)),
            pltpu.SemaphoreType.DMA((112,)),
            pltpu.SemaphoreType.DMA((112,)),
        ],
        compiler_params=pltpu.CompilerParams(collective_id=0, has_side_effects=True),
        name="window",
    )(occ_index, vir_index, freq_index, freq_table, pair_weight, coulomb, band_vectors)


def solution(mesh):
    torus = Mesh(
        mesh.devices.reshape(mesh.shape["grp"], 4, 8, 2, mesh.shape["cols"]),
        ("grp", "rows_0", "rows_1", "rows_2", "cols"),
    )
    placed = (P(ROWS, None), P(ROWS), P(), P(), P(), P(), P())
    return jax.shard_map(
        per_device, mesh=torus, in_specs=placed, out_specs=P(ROWS_COLS, "grp"), check_vma=False
    )
```
